128 devices in a mesh: face: 4 (over z), tile: 32 (over x, y, core).
Axes of the slice: x: 4, y: 4, z: 4, core: 2. Of those that a mesh axis runs over, the one named last changes fastest.
Arguments:
- fields: bfloat16 [3072, 384, 128], P('tile', 'face'), may hold values from -6 to 6
- first_kernel_taps: bfloat16 [9, 128, 128], replicated, may hold values from -0.1875 to 0.1875
- first_conv_bias: float32 [128], replicated, may hold values from -0.5 to 0.5
- second_kernel_taps: bfloat16 [9, 128, 128], replicated, may hold values from -0.1875 to 0.1875
- second_conv_bias: float32 [128], replicated, may hold values from -0.5 to 0.5
- obs_weight: bfloat16 [128, 128], replicated, may hold values from -0.5 to 0.5
- obs_values: bfloat16 [131072, 128], P(('face', 'tile')), may hold values from -6 to 6
- obs_owner: int32 [131072, 1], P(('face', 'tile')), may hold values from 0 to 127; in each aligned block of 1024 rows (0 to 1023, 1024 to 2047, ...) at most 16 rows name the same one
- obs_cells: int32 [131072], P(('face', 'tile')), may hold values from 0 to 9215
- polar_neighbor_sector: int32 [4, 2], replicated, may hold values from 0 to 3, as said below
- polar_link_reversal: int32 [4, 2], replicated, may hold values from 0 to 1
Outputs:
- level_out: bfloat16 [3072, 384, 128], P('tile', 'face')
The draws below stay inside these ranges and needn't reach their ends.
Inputs may be any that keep to these rules, and one draw needn't show every extreme that they name: `obs_owner`: among the rows of one device at most 16 name the same tile, and in every draw some device sends exactly 16 rows to one tile. `polar_neighbor_sector`: each column links the sectors in one cycle through all 4 of them; no sector names itself.
All inputs are finite; a program needn't handle non-finite values.
Results may differ from the reference program's by a relative error of at most 0.0034.
Values may be sent and summed in bfloat16 or wider, within the bound.
No kernel may reach another device: no remote copies, remote signals or barrier semaphores. Data moves between devices by JAX's collectives and lax.ppermute only.
A program may use at most 64 MiB of HBM per device.

```python
import math
import jax
import jax.numpy as jnp
import numpy as np
from jax import lax

C = 128
F = 128
SIDE = 96
OBS_DEV = 1024
FIRST_DILATION = 2
SECOND_DILATION = 4
NFACES = 4
NTILES = 32
TILES = 128
LAT = 3072
LON = 384
OBS = 131072
CAP = 16


def draw_polar_neighbor_sector(key, part):
    column_keys = jax.random.split(jax.random.fold_in(key, 7), 2)
    columns = []
    for column in range(2):
        order = jax.random.permutation(column_keys[column], NFACES).astype(jnp.int32)
        following = jnp.roll(order, -1)
        links = jnp.zeros((NFACES,), jnp.int32).at[order].set(following)
        columns.append(links)
    return jnp.stack(columns, axis=1).astype(jnp.int32)


def with_ends(values, own_key, low, largest):
    extent = values.shape
    spot = [jax.random.randint(jax.random.fold_in(own_key, axis), (), 0, extent[axis]) for axis in range(len(extent))]
    values = values.at[tuple(spot)].set(low)
    longest = extent.index(max(extent))
    spot[longest] = (spot[longest] + 1) % extent[longest]
    return values.at[tuple(spot)].set(largest)


def block_scale(stream_key, shape, shards, least, largest):
    factor_of = 1.0
    for axis_at, shards_of in shards:
        heights = jax.random.uniform(jax.random.fold_in(jax.random.fold_in(stream_key, 6), axis_at), (shards_of,), jnp.float32, least / len(shards), largest / len(shards))
        factor_of = factor_of * jnp.repeat(jnp.exp(heights), shape[axis_at] // shards_of).reshape((-1,) + (1,) * (len(shape) - 1 - axis_at))
    return factor_of


def assign_block(own_key, own, number, rows, count, top, limit, skew):
    ranking = jax.random.permutation(own_key, count)
    packed, usual = shares(count, rows * top, limit, skew, True), shares(count, rows * top, limit, skew, False)
    places = jnp.arange(count)

    def named(tallies, offset_by):
        used = int((tallies > 0).sum())
        fixed = max(1, used // 4)
        moved = fixed + (places - fixed + offset_by * (used - fixed)) % max(1, count - fixed)
        return jnp.zeros((count,), jnp.int32).at[ranking[jnp.where(places < fixed, places, moved)]].set(jnp.asarray(tallies, jnp.int32))

    tallies = jnp.where(number % 4 == 0, named(packed, number // 4), named(usual, number - number // 4 - 1))
    mixed = jax.random.permutation(jax.random.fold_in(own, 3), count)
    giver, taker = mixed[0:count // 2 * 2:2], mixed[1:count // 2 * 2:2]
    margin = jnp.minimum(tallies[giver] - 1, limit - tallies[taker]) // 2
    margin = jnp.where((giver == ranking[0]) | (taker == ranking[0]) | (tallies[taker] == 0), 0, jnp.maximum(margin, 0))
    moved = jax.random.randint(jax.random.fold_in(own, 4), (count // 2,), 0, 1 << 20) % (margin + 1)
    tallies = tallies.at[giver].add(-moved).at[taker].add(moved)
    items = jnp.searchsorted(jnp.cumsum(tallies), jnp.arange(rows * top), side="right").astype(jnp.int32)
    table = items.reshape(top, rows).T
    table = table[jax.random.permutation(jax.random.fold_in(own, 1), rows)]
    offset_by = jax.random.randint(jax.random.fold_in(own, 2), (rows, 1), 0, top)
    return jnp.take_along_axis(table, (jnp.arange(top)[None, :] + offset_by) % top, axis=1)


def shares(amount, total, bound, slope, full):
    loads = [(1 << 20) // math.isqrt(standing ** slope) + 1 for standing in range(1, amount + 1)]
    largest = bound if full else min(bound, max(-(-total // amount), total * loads[0] // sum(loads)))
    least = 1 if total - largest >= amount - 1 else 0
    counts, rest = [largest] + [least] * (amount - 1), total - largest - least * (amount - 1)
    while rest > 0:
        movable = [i for i in range(1, amount) if counts[i] < largest] or [i for i in range(1, amount) if counts[i] < bound]
        pool, budget = sum([loads[i] for i in movable]), rest
        for i in movable:
            addition = min(bound - counts[i], max(1, budget * loads[i] // pool), rest)
            counts[i] = counts[i] + addition
            rest = rest - addition
    return np.array(counts)


def normal_values(key, shape, spread, bound, shards=(), dtype=jnp.bfloat16):
    values = spread * jax.random.normal(key, shape, jnp.float32)
    if shards:
        values = values * block_scale(key, shape, shards, -0.22, 0.18)
    return jnp.clip(values, -bound, bound).astype(dtype)


def setup_inputs(seed: int = 0) -> dict:
    streams_of = jax.random.split(jax.random.key(seed), 12)
    fields = normal_values(streams_of[0], (LAT, LON, C), 1.0, 6.0, ((0, 32), (1, 4)))
    first_kernel_taps = normal_values(streams_of[1], (9, C, C), (9 * C) ** -0.5, 0.1875)
    first_conv_bias = jnp.clip(jax.random.uniform(streams_of[2], (C,), jnp.float32, -0.5, 0.5), -0.5, 0.5)
    second_kernel_taps = normal_values(streams_of[3], (9, C, C), (9 * C) ** -0.5, 0.1875)
    second_conv_bias = jnp.clip(jax.random.uniform(streams_of[4], (C,), jnp.float32, -0.5, 0.5), -0.5, 0.5)
    obs_weight = normal_values(streams_of[5], (F, C), F ** -0.5, 0.5)
    obs_values = normal_values(streams_of[6], (OBS, F), 1.0, 6.0, ((0, 128),))
    obs_owner_keys = jax.random.split(jax.random.fold_in(streams_of[7], 1), OBS // OBS_DEV)
    obs_owner_turns = jax.random.permutation(jax.random.fold_in(streams_of[7], 3), OBS // OBS_DEV)
    obs_owner = jax.vmap(lambda own, number: assign_block(jax.random.fold_in(streams_of[7], 2), own, number, OBS_DEV, TILES, 1, CAP, 2))(obs_owner_keys, obs_owner_turns).reshape((OBS, 1))
    obs_cells = with_ends(jax.random.randint(streams_of[8], (OBS,), 0, SIDE * SIDE), jax.random.fold_in(streams_of[8], 1), 0, (SIDE * SIDE) - 1).astype(jnp.int32)
    polar_neighbor_sector = draw_polar_neighbor_sector(jax.random.fold_in(streams_of[11], 71), 0)
    polar_link_reversal = with_ends(jax.random.randint(streams_of[10], (NFACES, 2), 0, 2), jax.random.fold_in(streams_of[10], 1), 0, 1).astype(jnp.int32)
    return dict(fields=fields, first_kernel_taps=first_kernel_taps, first_conv_bias=first_conv_bias, second_kernel_taps=second_kernel_taps, second_conv_bias=second_conv_bias, obs_weight=obs_weight, obs_values=obs_values, obs_owner=obs_owner, obs_cells=obs_cells, polar_neighbor_sector=polar_neighbor_sector, polar_link_reversal=polar_link_reversal)


def apply_stencil_taps(padded, kernel, bias_row, dilation, rows, cols):
    channels = padded.shape[-1]
    total = jnp.zeros((rows * cols, kernel.shape[-1]), jnp.float32)
    for tap_row in range(3):
        for tap_col in range(3):
            window = padded[tap_row * dilation: tap_row * dilation + rows, tap_col * dilation: tap_col * dilation + cols]
            total = total + jnp.dot(window.reshape(rows * cols, channels), kernel[tap_row * 3 + tap_col], preferred_element_type=jnp.float32)
    return total + bias_row.astype(jnp.float32)[None, :]


def spherical_convolve(grid, kernel, bias_row, dilation, polar_neighbor_sector, polar_link_reversal):
    lat_rows = grid.shape[0]
    lon_cols = grid.shape[1]
    sector_side_length = lon_cols // NFACES
    loop = jnp.concatenate([grid[:, lon_cols - dilation:], grid, grid[:, :dilation]], axis=1)
    outputs = []
    for sector in range(NFACES):
        strip = loop[:, sector * sector_side_length: sector * sector_side_length + sector_side_length + 2 * dilation]
        north_start = (polar_neighbor_sector[sector, 0] * sector_side_length).astype(jnp.int32)
        south_start = (polar_neighbor_sector[sector, 1] * sector_side_length).astype(jnp.int32)
        north = lax.dynamic_slice_in_dim(loop[:dilation], north_start, sector_side_length + 2 * dilation, 1)[::-1]
        north = jnp.where(polar_link_reversal[sector, 0] == 1, north[:, ::-1], north)
        south = lax.dynamic_slice_in_dim(loop[lat_rows - dilation:], south_start, sector_side_length + 2 * dilation, 1)[::-1]
        south = jnp.where(polar_link_reversal[sector, 1] == 1, south[:, ::-1], south)
        padded = jnp.concatenate([north, strip, south], axis=0)
        result = apply_stencil_taps(padded, kernel, bias_row, dilation, lat_rows, sector_side_length)
        outputs.append(result.reshape(lat_rows, sector_side_length, -1))
    return jnp.concatenate(outputs, axis=1)


def reference(fields, first_kernel_taps, first_conv_bias, second_kernel_taps, second_conv_bias, obs_weight, obs_values, obs_owner, obs_cells, polar_neighbor_sector, polar_link_reversal):
    lat_rows = fields.shape[0]
    lon_cols = fields.shape[1]
    sector_side_length = lon_cols // NFACES
    first_activation = jax.nn.gelu(spherical_convolve(fields, first_kernel_taps, first_conv_bias, FIRST_DILATION, polar_neighbor_sector, polar_link_reversal), approximate=True)
    encoded = jnp.dot(obs_values, obs_weight, preferred_element_type=jnp.float32)
    owner = obs_owner[:, 0]
    lat_index = (owner % NTILES) * sector_side_length + obs_cells // sector_side_length
    lon_index = (owner // NTILES) * sector_side_length + obs_cells % sector_side_length
    inject = jnp.zeros((lat_rows, lon_cols, encoded.shape[1]), jnp.float32).at[lat_index, lon_index].add(encoded)
    blended_features = (first_activation + inject).astype(jnp.bfloat16)
    second_activation = spherical_convolve(blended_features, second_kernel_taps, second_conv_bias, SECOND_DILATION, polar_neighbor_sector, polar_link_reversal)
    return (fields.astype(jnp.float32) + jax.nn.gelu(second_activation, approximate=True)).astype(jnp.bfloat16)
```

```python
import functools

import jax
import jax.numpy as jnp
from jax import lax
from jax.experimental import pallas as pl
from jax.experimental.pallas import tpu as pltpu
from jax.sharding import PartitionSpec as P

FIRST_DILATION = 2
SECOND_DILATION = 4
CAP = 16
META = 8

BF16 = jnp.bfloat16
F32 = jnp.float32
I32 = jnp.int32
VMEM = pltpu.VMEM


def full_spec(memory_space=None):
    return pl.BlockSpec(memory_space=VMEM if memory_space is None else memory_space)


def iota(shape, axis):
    return lax.broadcasted_iota(I32, shape, axis)


def pack_kernel(dests, side, owner_ref, cell_ref, vals_ref, send_ref):
    rows = vals_ref.shape[0]
    owner = owner_ref[...]
    cell = cell_ref[...]
    block = 256
    earlier = (iota((block, block), 0) < iota((block, block), 1)).astype(F32).astype(BF16)
    onehot_parts = []
    rank_parts = []
    carry = jnp.zeros((dests, 1), F32)
    for b in range(rows // block):
        hit = owner[:, b * block : (b + 1) * block] == iota((dests, block), 0)
        hit_f = jnp.where(hit, 1.0, 0.0)
        hit_b = hit_f.astype(BF16)
        before = jnp.dot(hit_b, earlier, preferred_element_type=F32) + carry
        rank_parts.append(jnp.sum(before * hit_f, axis=0, keepdims=True))
        carry = carry + jnp.sum(hit_f, axis=1, keepdims=True)
        onehot_parts.append(hit_b)
    rank = jnp.concatenate(rank_parts, axis=1).astype(I32)
    onehot = jnp.concatenate(onehot_parts, axis=1)
    target = owner * CAP + rank

    cell_row = ((cell.astype(F32) + 0.5) * (1.0 / side)).astype(I32)
    cell_col = cell - cell_row * side
    me = lax.axis_index("face") * lax.axis_size("tile") + lax.axis_index("tile")
    base_lane = lax.rem(me, 8) * CAP
    slot_hit = iota((128, rows), 0) == rank + base_lane
    row_map = jnp.where(slot_hit, cell_row.astype(F32), 0.0).astype(BF16)
    col_map = jnp.where(slot_hit, cell_col.astype(F32), 0.0).astype(BF16)
    contract = (((1,), (1,)), ((), ()))
    meta_row = lax.dot_general(onehot, row_map, contract, preferred_element_type=F32)
    meta_col = lax.dot_general(onehot, col_map, contract, preferred_element_type=F32)
    meta = jnp.where(
        iota((dests, META, 128), 1) == 0,
        jnp.broadcast_to(meta_row[:, None, :], (dests, META, 128)),
        jnp.broadcast_to(meta_col[:, None, :], (dests, META, 128)),
    )
    send_ref[:, CAP:, :] = meta.astype(BF16)

    chunk_dests = 16
    chunk = chunk_dests * CAP
    for c in range(dests // chunk_dests):
        match = target == iota((chunk, rows), 0) + c * chunk
        match = jnp.where(match, 1.0, 0.0).astype(BF16)
        placed = jnp.dot(match, vals_ref[...], preferred_element_type=F32).astype(BF16)
        send_ref[c * chunk_dests : (c + 1) * chunk_dests, :CAP, :] = placed.reshape(
            chunk_dests, CAP, placed.shape[-1]
        )


def pack(owner, cells, vals, dests, side):
    rows, features = vals.shape
    return pl.pallas_call(
        functools.partial(pack_kernel, dests, side),
        out_shape=jax.ShapeDtypeStruct((dests, CAP + META, features), BF16),
        in_specs=[full_spec()] * 3,
        out_specs=full_spec(),
        cost_estimate=pl.CostEstimate(
            flops=2 * dests * CAP * rows * features, bytes_accessed=2_000_000, transcendentals=0
        ),
        name="pack",
    )(owner.reshape(1, rows), cells.reshape(1, rows), vals)


def gelu(x):
    inner = 0.7978845608028654 * (x + 0.044715 * (x * x * x))
    return 0.5 * x * (1.0 + jnp.tanh(inner))


def conv_kernel(
    d,
    groups,
    has_residual,
    neighbor_ref,
    reversal_ref,
    grid_ref,
    left_ref,
    right_ref,
    above_ref,
    below_ref,
    p0_ref,
    p1_ref,
    p2_ref,
    p3_ref,
    taps_ref,
    bias_ref,
    *rest,
):
    if has_residual:
        fields_ref, out_ref, strip, weights = rest
    else:
        out_ref, strip, weights = rest
    rows, cols, ch = grid_ref.shape
    face = lax.axis_index("face")
    tile = lax.axis_index("tile")
    nface = lax.axis_size("face")
    last_tile = lax.axis_size("tile") - 1

    for a in range(4):
        for e in range(3):
            at = (a * 3 + e) * ch
            if a < 3:
                weights[at : at + ch, :ch] = taps_ref[a * 3 + e]
            else:
                weights[at : at + ch, :ch] = jnp.zeros((ch, ch), BF16)
            if a > 0:
                weights[at : at + ch, ch:] = taps_ref[(a - 1) * 3 + e]
            else:
                weights[at : at + ch, ch:] = jnp.zeros((ch, ch), BF16)

    def build(r, carry):
        v = grid_ref[r]
        p = r + d
        strip[p, :, ch : 2 * ch] = v
        strip[p, d:, :ch] = v[: cols - d]
        strip[p, :d, :ch] = left_ref[r]
        strip[p, : cols - d, 2 * ch :] = v[d:]
        strip[p, cols - d :, 2 * ch :] = right_ref[r]
        return carry

    lax.fori_loop(0, rows, build, 0, unroll=4)

    def plain_rows(source_ref, at):
        for r in range(d):
            for e in range(3):
                strip[at + r, :, e * ch : (e + 1) * ch] = source_ref[r, e * d : e * d + cols, :]

    def polar_rows(which, at):
        sector = neighbor_ref[face, which]
        flip = reversal_ref[face, which]
        for e in range(3):
            place = iota((cols, 1), 0) + e * d
            place = jnp.where(flip == 1, cols + 2 * d - 1 - place, place)
            column = place - d + cols
            step = jnp.where(column >= 2 * cols, 2, jnp.where(column >= cols, 1, 0))
            inside = column - step * cols
            shift = lax.rem(face - sector - (step - 1) + 2 * nface, nface)
            wanted = shift * cols + inside
            pick = jnp.where(iota((cols, nface * cols), 1) == wanted, 1.0, 0.0).astype(BF16)
            for r in range(d):
                source = jnp.concatenate(
                    [ref[d - 1 - r] for ref in (p0_ref, p1_ref, p2_ref, p3_ref)], axis=0
                )
                strip[at + r, :, e * ch : (e + 1) * ch] = jnp.dot(
                    pick, source, preferred_element_type=F32
                ).astype(BF16)

    @pl.when(tile > 0)
    def _():
        plain_rows(above_ref, 0)

    @pl.when(tile == 0)
    def _():
        polar_rows(0, 0)

    @pl.when(tile < last_tile)
    def _():
        plain_rows(below_ref, rows + d)

    @pl.when(tile == last_tile)
    def _():
        polar_rows(1, rows + d)

    bias = bias_ref[...]
    bias2 = jnp.concatenate([bias, bias], axis=1)
    m = d * cols

    def block(i, carry):
        base = i * (groups * 2 * d)
        parts = []
        for a in range(4):
            for_a = [
                strip[pl.ds(base + g * 2 * d + a * d, d)].reshape(m, 3 * ch) for g in range(groups)
            ]
            parts.append(jnp.concatenate(for_a, axis=0))
        lhs = jnp.concatenate(parts, axis=1)
        acc = jnp.dot(lhs, weights[...], preferred_element_type=F32) + bias2
        y = gelu(acc)
        for g in range(groups):
            for half in range(2):
                at = base + g * 2 * d + half * d
                piece = y[g * m : (g + 1) * m, half * ch : (half + 1) * ch].reshape(d, cols, ch)
                if has_residual:
                    piece = piece + fields_ref[pl.ds(at, d)].astype(F32)
                out_ref[pl.ds(at, d)] = piece.astype(out_ref.dtype)
        return carry

    lax.fori_loop(0, rows // (groups * 2 * d), block, 0)


def conv(grid, halo, polar, neighbor, reversal, taps, bias, d, groups, fields, out_dtype, name):
    rows, cols, ch = grid.shape
    left, right, above, below = halo
    operands = [neighbor, reversal, grid, left, right, above, below, *polar, taps]
    operands.append(bias.reshape(1, ch))
    smem = full_spec(pltpu.SMEM)
    in_specs = [smem, smem] + [full_spec()] * (len(operands) - 2)
    if fields is not None:
        operands.append(fields)
        in_specs.append(full_spec())
    return pl.pallas_call(
        functools.partial(conv_kernel, d, groups, fields is not None),
        out_shape=jax.ShapeDtypeStruct((rows, cols, ch), out_dtype),
        in_specs=in_specs,
        out_specs=full_spec(),
        scratch_shapes=[
            VMEM((rows + 2 * d, cols, 3 * ch), BF16),
            VMEM((12 * ch, 2 * ch), BF16),
        ],
        cost_estimate=pl.CostEstimate(
            flops=2 * 12 * rows * cols * ch * ch, bytes_accessed=9_000_000, transcendentals=0
        ),
        name=name,
    )(*operands)


def scatter_kernel(
    side, recv_ref, weight_ref, first_ref, mixed_ref, acc_ref, enc, cells_v, cells_s, sem, first_sem
):
    load = pltpu.make_async_copy(first_ref, acc_ref, first_sem)
    load.start()
    sources = recv_ref.shape[0]
    ch = weight_ref.shape[1]
    for g in range(sources // 8):
        meta = jnp.sum(recv_ref[g * 8 : (g + 1) * 8, CAP:, :].astype(F32), axis=0)
        cells_v[g : g + 1, :] = (meta[0:1, :] * side + meta[1:2, :]).astype(I32)
    copy = pltpu.make_async_copy(cells_v, cells_s, sem)
    copy.start()
    for g in range(sources // 8):
        rows = recv_ref[g * 8 : (g + 1) * 8, :CAP, :].reshape(8 * CAP, recv_ref.shape[2])
        enc[g * 128 : (g + 1) * 128, :] = jnp.dot(
            rows, weight_ref[...], preferred_element_type=F32
        )
    copy.wait()
    load.wait()

    def add_rows(g, carry):
        for j in range(128):
            c = cells_s[g, j]
            acc_ref[pl.ds(c, 1), :] += enc[pl.ds(g * 128 + j, 1), :]
        return carry

    lax.fori_loop(0, sources // 8, add_rows, 0)

    def rounding(r, carry):
        mixed_ref[r] = acc_ref[pl.ds(r * side, side), :].astype(BF16)
        return carry

    lax.fori_loop(0, side, rounding, 0, unroll=4)


def scatter(recv, weight, first):
    side, cols, ch = first.shape
    sources, height, features = recv.shape
    flat = first.reshape(side * cols, ch)
    return pl.pallas_call(
        functools.partial(scatter_kernel, side),
        out_shape=jax.ShapeDtypeStruct((side, cols, ch), BF16),
        in_specs=[full_spec(), full_spec(), full_spec(pl.ANY)],
        out_specs=full_spec(),
        scratch_shapes=[
            VMEM(flat.shape, F32),
            VMEM((sources * CAP, ch), F32),
            VMEM((sources // 8, 128), I32),
            pltpu.SMEM((sources // 8, 128), I32),
            pltpu.SemaphoreType.DMA,
            pltpu.SemaphoreType.DMA,
        ],
        cost_estimate=pl.CostEstimate(
            flops=200_000_000, bytes_accessed=12_000_000, transcendentals=0
        ),
        name="scatter",
    )(recv, weight, flat)


def exchange(grid, d):
    nface = lax.axis_size("face")
    ntile = lax.axis_size("tile")
    rows = grid.shape[0]
    left = lax.ppermute(grid[:, grid.shape[1] - d :], "face", [(f, (f + 1) % nface) for f in range(nface)])
    right = lax.ppermute(grid[:, :d], "face", [(f, (f - 1) % nface) for f in range(nface)])
    tile = lax.axis_index("tile")
    edge = jnp.where(tile == 0, grid[:d], grid[rows - d :])
    ends = (0, ntile - 1)
    polar = [edge]
    for k in range(1, nface):
        pairs = [(f * ntile + t, ((f + k) % nface) * ntile + t) for f in range(nface) for t in ends]
        polar.append(lax.ppermute(edge, ("face", "tile"), pairs))
    wide_top = jnp.concatenate([left[:d], grid[:d], right[:d]], axis=1)
    wide_bottom = jnp.concatenate([left[rows - d :], grid[rows - d :], right[rows - d :]], axis=1)
    above = lax.ppermute(wide_bottom, "tile", [(t, t + 1) for t in range(ntile - 1)])
    below = lax.ppermute(wide_top, "tile", [(t + 1, t) for t in range(ntile - 1)])
    return (left, right, above, below), polar


def local(
    fields,
    first_kernel_taps,
    first_conv_bias,
    second_kernel_taps,
    second_conv_bias,
    obs_weight,
    obs_values,
    obs_owner,
    obs_cells,
    polar_neighbor_sector,
    polar_link_reversal,
):
    side = fields.shape[0]
    dests = lax.axis_size("face") * lax.axis_size("tile")
    send = pack(obs_owner, obs_cells, obs_values, dests, side)
    recv = lax.all_to_all(send, ("face", "tile"), split_axis=0, concat_axis=0, tiled=True)
    halo, polar = exchange(fields, FIRST_DILATION)
    first = conv(
        fields, halo, polar, polar_neighbor_sector, polar_link_reversal,
        first_kernel_taps, first_conv_bias, FIRST_DILATION, 2, None, F32, "conv_first",
    )
    mixed = scatter(recv, obs_weight, first)
    halo, polar = exchange(mixed, SECOND_DILATION)
    return conv(
        mixed, halo, polar, polar_neighbor_sector, polar_link_reversal,
        second_kernel_taps, second_conv_bias, SECOND_DILATION, 1, fields, BF16, "conv_second",
    )


def solution(mesh):
    in_specs = (
        P("tile", "face", None),
        P(),
        P(),
        P(),
        P(),
        P(),
        P(("face", "tile"), None),
        P(("face", "tile"), None),
        P(("face", "tile")),
        P(),
        P(),
    )
    out_specs = P("tile", "face", None)
    return jax.shard_map(local, mesh=mesh, in_specs=in_specs, out_specs=out_specs, check_vma=False)
```

```python
import functools

import jax
import jax.numpy as jnp
from jax import lax
from jax.experimental import pallas as pl
from jax.experimental.pallas import tpu as pltpu
from jax.sharding import PartitionSpec as P

FIRST_DILATION = 2
SECOND_DILATION = 4
CAP = 16
META = 8

BF16 = jnp.bfloat16
F32 = jnp.float32
I32 = jnp.int32
VMEM = pltpu.VMEM


def full_spec(memory_space=None):
    return pl.BlockSpec(memory_space=VMEM if memory_space is None else memory_space)


def iota(shape, axis):
    return lax.broadcasted_iota(I32, shape, axis)


def pack_kernel(dests, side, owner_ref, cell_ref, vals_ref, send_ref):
    rows = vals_ref.shape[0]
    owner = owner_ref[...]
    cell = cell_ref[...]
    block = 256
    earlier = (iota((block, block), 0) < iota((block, block), 1)).astype(F32).astype(BF16)
    onehot_parts = []
    rank_parts = []
    carry = jnp.zeros((dests, 1), F32)
    for b in range(rows // block):
        hit = owner[:, b * block : (b + 1) * block] == iota((dests, block), 0)
        hit_f = jnp.where(hit, 1.0, 0.0)
        hit_b = hit_f.astype(BF16)
        before = jnp.dot(hit_b, earlier, preferred_element_type=F32) + carry
        rank_parts.append(jnp.sum(before * hit_f, axis=0, keepdims=True))
        carry = carry + jnp.sum(hit_f, axis=1, keepdims=True)
        onehot_parts.append(hit_b)
    rank = jnp.concatenate(rank_parts, axis=1).astype(I32)
    onehot = jnp.concatenate(onehot_parts, axis=1)
    target = owner * CAP + rank

    cell_row = ((cell.astype(F32) + 0.5) * (1.0 / side)).astype(I32)
    cell_col = cell - cell_row * side
    me = lax.axis_index("face") * lax.axis_size("tile") + lax.axis_index("tile")
    base_lane = lax.rem(me, 8) * CAP
    slot_hit = iota((128, rows), 0) == rank + base_lane
    row_map = jnp.where(slot_hit, cell_row.astype(F32), 0.0).astype(BF16)
    col_map = jnp.where(slot_hit, cell_col.astype(F32), 0.0).astype(BF16)
    contract = (((1,), (1,)), ((), ()))
    meta_row = lax.dot_general(onehot, row_map, contract, preferred_element_type=F32)
    meta_col = lax.dot_general(onehot, col_map, contract, preferred_element_type=F32)
    meta = jnp.where(
        iota((dests, META, 128), 1) == 0,
        jnp.broadcast_to(meta_row[:, None, :], (dests, META, 128)),
        jnp.broadcast_to(meta_col[:, None, :], (dests, META, 128)),
    )
    send_ref[:, CAP:, :] = meta.astype(BF16)

    chunk_dests = 16
    chunk = chunk_dests * CAP
    for c in range(dests // chunk_dests):
        match = target == iota((chunk, rows), 0) + c * chunk
        match = jnp.where(match, 1.0, 0.0).astype(BF16)
        placed = jnp.dot(match, vals_ref[...], preferred_element_type=F32).astype(BF16)
        send_ref[c * chunk_dests : (c + 1) * chunk_dests, :CAP, :] = placed.reshape(
            chunk_dests, CAP, placed.shape[-1]
        )


def pack(owner, cells, vals, dests, side):
    rows, features = vals.shape
    return pl.pallas_call(
        functools.partial(pack_kernel, dests, side),
        out_shape=jax.ShapeDtypeStruct((dests, CAP + META, features), BF16),
        in_specs=[full_spec()] * 3,
        out_specs=full_spec(),
        cost_estimate=pl.CostEstimate(
            flops=2 * dests * CAP * rows * features, bytes_accessed=2_000_000, transcendentals=0
        ),
        name="pack",
    )(owner.reshape(1, rows), cells.reshape(1, rows), vals)


def parities():
    face = lax.axis_index("face")
    tile = lax.axis_index("tile")
    return face, tile, lax.rem(face, 2) == 0, lax.rem(tile, 2) == 0


def edges_kernel(d, grid_ref, a_ref, b_ref, low, high, sems):
    rows, cols, ch = grid_ref.shape
    _, _, face_even, tile_even = parities()
    start = jnp.where(tile_even, 0, rows - d)
    copies = [
        pltpu.make_async_copy(grid_ref.at[:, pl.ds(0, 8), :], low, sems.at[0]),
        pltpu.make_async_copy(grid_ref.at[:, pl.ds(cols - 8, 8), :], high, sems.at[1]),
        pltpu.make_async_copy(grid_ref.at[pl.ds(start, d)], a_ref.at[pl.ds(d, d)], sems.at[2]),
        pltpu.make_async_copy(grid_ref.at[pl.ds(start, d)], b_ref.at[pl.ds(d, d)], sems.at[3]),
    ]
    for copy in copies:
        copy.start()
    for copy in copies:
        copy.wait()
    per = cols // d
    group = 8 // d

    def plane(p, carry):
        for r in range(0, per, group):
            at = [p * per + r + k for k in range(group)]
            west = jnp.concatenate([low[i].astype(F32)[:d] for i in at], axis=0)
            east = jnp.concatenate([high[i].astype(F32)[8 - d :] for i in at], axis=0)
            a_ref[p, r * d : r * d + 8, :] = jnp.where(face_even, east, west).astype(BF16)
            b_ref[p, r * d : r * d + 8, :] = jnp.where(face_even, west, east).astype(BF16)
        return carry

    lax.fori_loop(0, d, plane, 0)


def edges(grid, d):
    rows, cols, ch = grid.shape
    side = jax.ShapeDtypeStruct((2 * d, cols, ch), BF16)
    return pl.pallas_call(
        functools.partial(edges_kernel, d),
        out_shape=(side, side),
        in_specs=[full_spec(pl.ANY)],
        out_specs=(full_spec(), full_spec()),
        scratch_shapes=[
            VMEM((rows, 8, ch), BF16),
            VMEM((rows, 8, ch), BF16),
            pltpu.SemaphoreType.DMA((4,)),
        ],
        cost_estimate=pl.CostEstimate(flops=1_000_000, bytes_accessed=800_000, transcendentals=0),
        name="edges",
    )(grid)


def widen_kernel(d, grid_ref, ra_ref, rb_ref, wa_ref, wb_ref, ends, sems):
    rows, cols, ch = grid_ref.shape
    _, _, face_even, tile_even = parities()
    copies = [
        pltpu.make_async_copy(grid_ref.at[pl.ds(at, d)], ends.at[i], sems.at[i])
        for i, at in enumerate((0, rows - d))
    ]
    for copy in copies:
        copy.start()
    for copy in copies:
        copy.wait()
    per = cols // d
    for r in range(d):
        wide = []
        for i, row in enumerate((r, rows - d + r)):
            at = (row % per) * d
            tile_at = at // 8 * 8
            a = ra_ref[row // per, tile_at : tile_at + 8, :].astype(F32)[at - tile_at : at - tile_at + d]
            b = rb_ref[row // per, tile_at : tile_at + 8, :].astype(F32)[at - tile_at : at - tile_at + d]
            wide.append(
                jnp.concatenate(
                    [jnp.where(face_even, b, a), ends[i, r].astype(F32), jnp.where(face_even, a, b)],
                    axis=0,
                )
            )
        wa_ref[r] = jnp.where(tile_even, wide[1], wide[0]).astype(BF16)
        wb_ref[r] = jnp.where(tile_even, wide[0], wide[1]).astype(BF16)


def widen(grid, received, d):
    rows, cols, ch = grid.shape
    wide = jax.ShapeDtypeStruct((d, cols + 2 * d, ch), BF16)
    return pl.pallas_call(
        functools.partial(widen_kernel, d),
        out_shape=(wide, wide),
        in_specs=[full_spec(pl.ANY), full_spec(), full_spec()],
        out_specs=(full_spec(), full_spec()),
        scratch_shapes=[VMEM((2, d, cols, ch), BF16), pltpu.SemaphoreType.DMA((2,))],
        cost_estimate=pl.CostEstimate(flops=1_000_000, bytes_accessed=800_000, transcendentals=0),
        name="widen",
    )(grid, *received)


def face_partner(f, nface, odd_up):
    return (f + 1) % nface if (f % 2 == 1) == odd_up else (f - 1) % nface


def swap_faces(sides):
    nface = lax.axis_size("face")
    inner = [(f, face_partner(f, nface, False)) for f in range(nface)]
    outer = [(f, face_partner(f, nface, True)) for f in range(nface)]
    return lax.ppermute(sides[0], "face", inner), lax.ppermute(sides[1], "face", outer)


def swap_tiles(wide):
    nface = lax.axis_size("face")
    ntile = lax.axis_size("tile")
    inner = [(t, t ^ 1) for t in range(ntile)]
    outer = []
    for f in range(nface):
        for t in range(ntile):
            if t in (0, ntile - 1):
                to = ((f + 2) % nface) * ntile + t
            else:
                to = f * ntile + (t + 1 if t % 2 == 1 else t - 1)
            outer.append((f * ntile + t, to))
    return lax.ppermute(wide[0], "tile", inner), lax.ppermute(wide[1], ("face", "tile"), outer)


def gelu(x):
    half = 0.5 * x
    inner = x * (0.7978845608028654 + (0.7978845608028654 * 0.044715) * (x * x))
    return half + half * jnp.tanh(inner)


def conv_kernel(
    d,
    groups,
    has_residual,
    neighbor_ref,
    reversal_ref,
    grid_ref,
    ra_ref,
    rb_ref,
    wa_ref,
    wb_ref,
    taps_ref,
    bias_ref,
    *rest,
):
    if has_residual:
        fields_ref, out_ref, strip, weights, wide, acc, result, sems, out_sems, fields = rest
    else:
        out_ref, strip, weights, wide, acc, result, sems, out_sems = rest
    rows, cols, ch = grid_ref.shape
    face, tile, face_even, tile_even = parities()
    nface = lax.axis_size("face")
    last_tile = lax.axis_size("tile") - 1
    load = pltpu.make_async_copy(
        grid_ref, strip.at[pl.ds(d, rows), :, pl.ds(ch, ch)], sems.at[0]
    )
    load.start()
    if has_residual:
        load_fields = pltpu.make_async_copy(fields_ref, fields, sems.at[1])
        load_fields.start()

    for a in range(4):
        for e in range(3):
            at = (a * 3 + e) * ch
            if a < 3:
                weights[at : at + ch, :ch] = taps_ref[a * 3 + e]
            else:
                weights[at : at + ch, :ch] = jnp.zeros((ch, ch), BF16)
            if a > 0:
                weights[at : at + ch, ch:] = taps_ref[(a - 1) * 3 + e]
            else:
                weights[at : at + ch, ch:] = jnp.zeros((ch, ch), BF16)

    for r in range(d):
        wide[0, r] = jnp.where(tile_even, wb_ref[r].astype(F32), wa_ref[r].astype(F32)).astype(BF16)
        wide[1, r] = jnp.where(tile_even, wa_ref[r].astype(F32), wb_ref[r].astype(F32)).astype(BF16)
    load.wait()

    @pl.when((tile == 0) | (tile == last_tile))
    def _():
        which = jnp.where(tile == 0, 0, 1)
        sector = neighbor_ref[face, which]
        flip = reversal_ref[face, which]
        own = jnp.where(tile == 0, d, rows)
        width = cols + 2 * d

        def source_index(s):
            s = lax.rem(s + nface, nface)
            inner = jnp.where(face_even, face + 1, face - 1)
            outer = lax.rem(jnp.where(face_even, face - 1, face + 1) + nface, nface)
            return jnp.where(s == face, 0, jnp.where(s == inner, 1, jnp.where(s == outer, 2, 3)))

        place = iota((width, 1), 0)
        place = jnp.where(flip == 1, width - 1 - place, place)
        column = place - d + cols
        step = jnp.where(column >= 2 * cols, 2, jnp.where(column >= cols, 1, 0))
        inside = column - step * cols
        index = jnp.where(
            step == 0,
            source_index(sector - 1),
            jnp.where(step == 1, source_index(sector), source_index(sector + 1)),
        )
        wanted = index * cols + inside
        pick = jnp.where(iota((width, nface * cols), 1) == wanted, 1.0, 0.0).astype(BF16)
        for r in range(d):
            source = jnp.concatenate(
                [
                    strip[own + r, :, ch : 2 * ch],
                    ra_ref[d + r],
                    rb_ref[d + r],
                    wb_ref[r, d : d + cols, :],
                ],
                axis=0,
            )
            wide[which, d - 1 - r] = jnp.dot(pick, source, preferred_element_type=F32).astype(BF16)

    for side, at in ((0, 0), (1, rows + d)):
        for r in range(d):
            for e in range(3):
                strip[at + r, :, e * ch : (e + 1) * ch] = wide[side, r, e * d : e * d + cols, :]

    per = cols // d
    group = 8 // d

    def build(i, p):
        at = pl.multiple_of(i * 8, 8)
        a = ra_ref[p, pl.ds(at, 8), :].astype(F32)
        b = rb_ref[p, pl.ds(at, 8), :].astype(F32)
        west = jnp.where(face_even, b, a).astype(BF16)
        east = jnp.where(face_even, a, b).astype(BF16)
        for k in range(group):
            row = p * per + i * group + k + d
            v = strip[row, :, ch : 2 * ch]
            strip[row, d:, :ch] = v[: cols - d]
            strip[row, :d, :ch] = west[k * d : (k + 1) * d]
            strip[row, : cols - d, 2 * ch :] = v[d:]
            strip[row, cols - d :, 2 * ch :] = east[k * d : (k + 1) * d]
        return p

    def build_plane(p, carry):
        lax.fori_loop(0, per // group, build, p, unroll=2)
        return carry

    lax.fori_loop(0, d, build_plane, 0)
    if has_residual:
        load_fields.wait()

    bias = bias_ref[...]
    bias2 = jnp.concatenate([bias, bias], axis=1)
    m = d * cols
    step_rows = groups * 2 * d
    blocks = rows // step_rows

    def product(i):
        base = i * step_rows
        parts = []
        for a in range(4):
            of_a = [
                strip[pl.ds(base + g * 2 * d + a * d, d)].reshape(m, 3 * ch) for g in range(groups)
            ]
            parts.append(jnp.concatenate(of_a, axis=0))
        return jnp.dot(
            jnp.concatenate(parts, axis=1), weights[...], preferred_element_type=F32
        )

    def send(i):
        at = pl.ds(i * step_rows, step_rows)
        return pltpu.make_async_copy(result.at[at], out_ref.at[at], out_sems.at[i])

    def finish(i):
        y = gelu(acc[...] + bias2)
        for g in range(groups):
            for half in range(2):
                at = i * step_rows + g * 2 * d + half * d
                piece = y[g * m : (g + 1) * m, half * ch : (half + 1) * ch].reshape(d, cols, ch)
                if has_residual:
                    piece = piece + fields[pl.ds(at, d)].astype(F32)
                result[pl.ds(at, d)] = piece.astype(result.dtype)

    acc[...] = product(0)

    def block(i, carry):
        finish(i - 1)
        acc[...] = product(i)
        send(i - 1).start()
        return carry

    lax.fori_loop(1, blocks, block, 0)
    finish(blocks - 1)
    send(blocks - 1).start()
    for i in range(blocks):
        send(i).wait()


def conv(grid, sides, wide, neighbor, reversal, taps, bias, d, groups, fields, out_dtype, name):
    rows, cols, ch = grid.shape
    operands = [neighbor, reversal, grid, *sides, *wide, taps, bias.reshape(1, ch)]
    smem = full_spec(pltpu.SMEM)
    in_specs = [smem, smem, full_spec(pl.ANY)] + [full_spec()] * 6
    scratch = [
        VMEM((rows + 2 * d, cols, 3 * ch), BF16),
        VMEM((12 * ch, 2 * ch), BF16),
        VMEM((2, d, cols + 2 * d, ch), BF16),
        VMEM((groups * d * cols, 2 * ch), F32),
        VMEM((rows, cols, ch), out_dtype),
        pltpu.SemaphoreType.DMA((2,)),
        pltpu.SemaphoreType.DMA((rows // (groups * 2 * d),)),
    ]
    if fields is not None:
        operands.append(fields)
        in_specs.append(full_spec(pl.ANY))
        scratch.append(VMEM(fields.shape, BF16))
    return pl.pallas_call(
        functools.partial(conv_kernel, d, groups, fields is not None),
        out_shape=jax.ShapeDtypeStruct((rows, cols, ch), out_dtype),
        in_specs=in_specs,
        out_specs=full_spec(pl.ANY),
        scratch_shapes=scratch,
        cost_estimate=pl.CostEstimate(
            flops=2 * 12 * rows * cols * ch * ch, bytes_accessed=9_000_000, transcendentals=0
        ),
        name=name,
    )(*operands)


def scatter_kernel(
    d,
    recv_hbm,
    weight_ref,
    first_ref,
    mixed_ref,
    a_ref,
    b_ref,
    recv,
    acc,
    extra,
    enc,
    mixed,
    cells_v,
    cells_s,
    sems,
    out_sems,
):
    load = pltpu.make_async_copy(first_ref, acc, sems.at[0])
    load_recv = pltpu.make_async_copy(recv_hbm, recv, sems.at[1])
    load_recv.start()
    load.start()
    side, _, ch = mixed.shape
    sources = recv.shape[0]
    _, _, face_even, tile_even = parities()
    load_recv.wait()
    for g in range(sources // 8):
        meta = jnp.sum(recv[g * 8 : (g + 1) * 8, CAP:, :].astype(F32), axis=0)
        cells_v[g : g + 1, :] = (meta[0:1, :] * side + meta[1:2, :]).astype(I32)
    copy = pltpu.make_async_copy(cells_v, cells_s, sems.at[2])
    copy.start()
    for g in range(sources // 8):
        rows = recv[g * 8 : (g + 1) * 8, :CAP, :].reshape(8 * CAP, recv.shape[2])
        enc[g * 128 : (g + 1) * 128, :] = jnp.dot(
            rows, weight_ref[...], preferred_element_type=F32
        )

    def clear(r, carry):
        extra[pl.ds(r * side, side), :] = jnp.zeros((side, ch), F32)
        return carry

    lax.fori_loop(0, side, clear, 0, unroll=4)
    copy.wait()
    load.wait()

    def add_rows(g, carry):
        for j in range(0, 128, 2):
            for k, target in ((0, acc), (1, extra)):
                c = cells_s[g, j + k]
                target[pl.ds(c, 1), :] += enc[pl.ds(g * 128 + j + k, 1), :]
        return carry

    lax.fori_loop(0, sources // 8, add_rows, 0)

    per = side // d
    group = 8 // d

    def send(p):
        at = pl.ds(p * per, per)
        return pltpu.make_async_copy(mixed.at[at], mixed_ref.at[at], out_sems.at[p])

    def plane(p, carry):
        def rows_of(i, inner):
            west = []
            east = []
            for k in range(group):
                row = p * per + i * group + k
                at = pl.ds(pl.multiple_of(row * side, side), side)
                v = acc[at, :] + extra[at, :]
                mixed[row] = v.astype(BF16)
                west.append(v[:d])
                east.append(v[side - d :])
            west = jnp.concatenate(west, axis=0)
            east = jnp.concatenate(east, axis=0)
            at = pl.ds(pl.multiple_of(i * 8, 8), 8)
            a_ref[p, at, :] = jnp.where(face_even, east, west).astype(BF16)
            b_ref[p, at, :] = jnp.where(face_even, west, east).astype(BF16)
            return inner

        lax.fori_loop(0, per // group, rows_of, 0, unroll=2)
        send(p).start()
        return carry

    lax.fori_loop(0, d, plane, 0)
    start = jnp.where(tile_even, 0, side - d)
    for r in range(d):
        row = mixed[start + r]
        a_ref[d + r] = row
        b_ref[d + r] = row
    for p in range(d):
        send(p).wait()


def scatter(recv, weight, first, d):
    side, cols, ch = first.shape
    sources, height, features = recv.shape
    flat = first.reshape(side * cols, ch)
    out = jax.ShapeDtypeStruct((2 * d, cols, ch), BF16)
    return pl.pallas_call(
        functools.partial(scatter_kernel, d),
        out_shape=(jax.ShapeDtypeStruct((side, cols, ch), BF16), out, out),
        in_specs=[full_spec(pl.ANY), full_spec(), full_spec(pl.ANY)],
        out_specs=(full_spec(pl.ANY), full_spec(), full_spec()),
        scratch_shapes=[
            VMEM(recv.shape, BF16),
            VMEM(flat.shape, F32),
            VMEM(flat.shape, F32),
            VMEM((sources * CAP, ch), F32),
            VMEM((side, cols, ch), BF16),
            VMEM((sources // 8, 128), I32),
            pltpu.SMEM((sources // 8, 128), I32),
            pltpu.SemaphoreType.DMA((3,)),
            pltpu.SemaphoreType.DMA((d,)),
        ],
        cost_estimate=pl.CostEstimate(
            flops=200_000_000, bytes_accessed=12_000_000, transcendentals=0
        ),
        name="scatter",
    )(recv, weight, flat)


def local(
    fields,
    first_kernel_taps,
    first_conv_bias,
    second_kernel_taps,
    second_conv_bias,
    obs_weight,
    obs_values,
    obs_owner,
    obs_cells,
    polar_neighbor_sector,
    polar_link_reversal,
):
    side = fields.shape[0]
    dests = lax.axis_size("face") * lax.axis_size("tile")
    d = FIRST_DILATION
    sides = swap_faces(edges(fields, d))
    send = pack(obs_owner, obs_cells, obs_values, dests, side)
    recv = lax.all_to_all(send, ("face", "tile"), split_axis=0, concat_axis=0, tiled=True)
    wide = swap_tiles(widen(fields, sides, d))
    first = conv(
        fields, sides, wide, polar_neighbor_sector, polar_link_reversal,
        first_kernel_taps, first_conv_bias, d, 4, None, F32, "conv_first",
    )
    d = SECOND_DILATION
    mixed, side_a, side_b = scatter(recv, obs_weight, first, d)
    sides = swap_faces((side_a, side_b))
    wide = swap_tiles(widen(mixed, sides, d))
    return conv(
        mixed, sides, wide, polar_neighbor_sector, polar_link_reversal,
        second_kernel_taps, second_conv_bias, d, 2, fields, BF16, "conv_second",
    )


def solution(mesh):
    in_specs = (
        P("tile", "face", None),
        P(),
        P(),
        P(),
        P(),
        P(),
        P(("face", "tile"), None),
        P(("face", "tile"), None),
        P(("face", "tile")),
        P(),
        P(),
    )
    out_specs = P("tile", "face", None)
    return jax.shard_map(local, mesh=mesh, in_specs=in_specs, out_specs=out_specs, check_vma=False)
```

```python
import functools

import jax
import jax.numpy as jnp
from jax import lax
from jax.experimental import pallas as pl
from jax.experimental.pallas import tpu as pltpu
from jax.sharding import PartitionSpec as P

FIRST_DILATION = 2
SECOND_DILATION = 4
CAP = 16
META = 8

BF16 = jnp.bfloat16
F32 = jnp.float32
I32 = jnp.int32
VMEM = pltpu.VMEM


def full_spec(memory_space=None):
    return pl.BlockSpec(memory_space=VMEM if memory_space is None else memory_space)


def room(mebibytes):
    return pltpu.CompilerParams(vmem_limit_bytes=mebibytes << 20)


def far(x):
    return pltpu.with_memory_space_constraint(x, pltpu.HBM)


def keep(x):
    return pltpu.with_memory_space_constraint(x, VMEM)


def iota(shape, axis):
    return lax.broadcasted_iota(I32, shape, axis)


def pack_kernel(dests, side, owner_ref, cell_ref, vals_ref, send_ref):
    rows = vals_ref.shape[0]
    owner = owner_ref[...]
    cell = cell_ref[...]
    block = 256
    earlier = (iota((block, block), 0) < iota((block, block), 1)).astype(F32).astype(BF16)
    onehot_parts = []
    rank_parts = []
    carry = jnp.zeros((dests, 1), F32)
    for b in range(rows // block):
        hit = owner[:, b * block : (b + 1) * block] == iota((dests, block), 0)
        hit_f = jnp.where(hit, 1.0, 0.0)
        hit_b = hit_f.astype(BF16)
        before = jnp.dot(hit_b, earlier, preferred_element_type=F32) + carry
        rank_parts.append(jnp.sum(before * hit_f, axis=0, keepdims=True))
        carry = carry + jnp.sum(hit_f, axis=1, keepdims=True)
        onehot_parts.append(hit_b)
    rank = jnp.concatenate(rank_parts, axis=1).astype(I32)
    onehot = jnp.concatenate(onehot_parts, axis=1)
    target = owner * CAP + rank

    cell_row = ((cell.astype(F32) + 0.5) * (1.0 / side)).astype(I32)
    cell_col = cell - cell_row * side
    me = lax.axis_index("face") * lax.axis_size("tile") + lax.axis_index("tile")
    base_lane = lax.rem(me, 8) * CAP
    slot_hit = iota((128, rows), 0) == rank + base_lane
    row_map = jnp.where(slot_hit, cell_row.astype(F32), 0.0).astype(BF16)
    col_map = jnp.where(slot_hit, cell_col.astype(F32), 0.0).astype(BF16)
    contract = (((1,), (1,)), ((), ()))
    meta_row = lax.dot_general(onehot, row_map, contract, preferred_element_type=F32)
    meta_col = lax.dot_general(onehot, col_map, contract, preferred_element_type=F32)
    meta = jnp.where(
        iota((dests, META, 128), 1) == 0,
        jnp.broadcast_to(meta_row[:, None, :], (dests, META, 128)),
        jnp.broadcast_to(meta_col[:, None, :], (dests, META, 128)),
    )
    send_ref[:, CAP:, :] = meta.astype(BF16)

    chunk_dests = 16
    chunk = chunk_dests * CAP
    for c in range(dests // chunk_dests):
        match = target == iota((chunk, rows), 0) + c * chunk
        match = jnp.where(match, 1.0, 0.0).astype(BF16)
        placed = jnp.dot(match, vals_ref[...], preferred_element_type=F32).astype(BF16)
        send_ref[c * chunk_dests : (c + 1) * chunk_dests, :CAP, :] = placed.reshape(
            chunk_dests, CAP, placed.shape[-1]
        )


def pack(owner, cells, vals, dests, side):
    rows, features = vals.shape
    return pl.pallas_call(
        functools.partial(pack_kernel, dests, side),
        out_shape=jax.ShapeDtypeStruct((dests, CAP + META, features), BF16),
        in_specs=[full_spec()] * 3,
        out_specs=full_spec(),
        cost_estimate=pl.CostEstimate(
            flops=2 * dests * CAP * rows * features, bytes_accessed=2_000_000, transcendentals=0
        ),
        compiler_params=room(16),
        name="pack",
    )(owner.reshape(1, rows), cells.reshape(1, rows), vals)


def parities():
    face = lax.axis_index("face")
    tile = lax.axis_index("tile")
    return face, tile, lax.rem(face, 2) == 0, lax.rem(tile, 2) == 0


def edges_kernel(d, grid_ref, a_ref, b_ref, ends_ref, low, high, sems):
    rows, cols, _ = grid_ref.shape
    _, _, face_even, tile_even = parities()
    start = jnp.where(tile_even, 0, rows - d)
    copies = [
        pltpu.make_async_copy(grid_ref.at[:, pl.ds(0, 8), :], low, sems.at[0]),
        pltpu.make_async_copy(grid_ref.at[:, pl.ds(cols - 8, 8), :], high, sems.at[1]),
        pltpu.make_async_copy(grid_ref.at[pl.ds(start, d)], a_ref.at[pl.ds(d, d)], sems.at[2]),
        pltpu.make_async_copy(grid_ref.at[pl.ds(start, d)], b_ref.at[pl.ds(d, d)], sems.at[3]),
        pltpu.make_async_copy(grid_ref.at[pl.ds(0, d)], ends_ref.at[0], sems.at[4]),
        pltpu.make_async_copy(grid_ref.at[pl.ds(rows - d, d)], ends_ref.at[1], sems.at[5]),
    ]
    for copy in copies:
        copy.start()
    for copy in copies:
        copy.wait()
    per = cols // d
    group = 8 // d

    def plane(p, carry):
        for r in range(0, per, group):
            at = [p * per + r + k for k in range(group)]
            west = jnp.concatenate([low[i].astype(F32)[:d] for i in at], axis=0)
            east = jnp.concatenate([high[i].astype(F32)[8 - d :] for i in at], axis=0)
            a_ref[p, r * d : r * d + 8, :] = jnp.where(face_even, east, west).astype(BF16)
            b_ref[p, r * d : r * d + 8, :] = jnp.where(face_even, west, east).astype(BF16)
        return carry

    lax.fori_loop(0, d, plane, 0)


def edges(grid, d):
    rows, cols, ch = grid.shape
    side = VMEM((2 * d, cols, ch), BF16)
    return pl.pallas_call(
        functools.partial(edges_kernel, d),
        out_shape=(side, side, VMEM((2, d, cols, ch), BF16)),
        in_specs=[full_spec(pl.ANY)],
        out_specs=(full_spec(),) * 3,
        scratch_shapes=[
            VMEM((rows, 8, ch), BF16),
            VMEM((rows, 8, ch), BF16),
            pltpu.SemaphoreType.DMA((6,)),
        ],
        cost_estimate=pl.CostEstimate(flops=1_000_000, bytes_accessed=800_000, transcendentals=0),
        compiler_params=room(8),
        name="edges",
    )(far(grid))


def widen_kernel(d, ends_ref, ra_ref, rb_ref, wa_ref, wb_ref):
    cols = ends_ref.shape[2]
    rows = cols
    _, _, face_even, tile_even = parities()
    per = cols // d
    for r in range(d):
        wide = []
        for i, row in enumerate((r, rows - d + r)):
            at = (row % per) * d
            tile_at = at // 8 * 8
            a = ra_ref[row // per, tile_at : tile_at + 8, :].astype(F32)[at - tile_at : at - tile_at + d]
            b = rb_ref[row // per, tile_at : tile_at + 8, :].astype(F32)[at - tile_at : at - tile_at + d]
            wide.append(
                jnp.concatenate(
                    [
                        jnp.where(face_even, b, a),
                        ends_ref[i, r].astype(F32),
                        jnp.where(face_even, a, b),
                    ],
                    axis=0,
                )
            )
        wa_ref[r] = jnp.where(tile_even, wide[1], wide[0]).astype(BF16)
        wb_ref[r] = jnp.where(tile_even, wide[0], wide[1]).astype(BF16)


def widen(ends, received, d):
    _, _, cols, ch = ends.shape
    wide = VMEM((d, cols + 2 * d, ch), BF16)
    return pl.pallas_call(
        functools.partial(widen_kernel, d),
        out_shape=(wide, wide),
        in_specs=[full_spec()] * 3,
        out_specs=(full_spec(), full_spec()),
        cost_estimate=pl.CostEstimate(flops=1_000_000, bytes_accessed=800_000, transcendentals=0),
        compiler_params=room(8),
        name="widen",
    )(keep(ends), *[keep(x) for x in received])


def face_partner(f, nface, odd_up):
    return (f + 1) % nface if (f % 2 == 1) == odd_up else (f - 1) % nface


def swap_faces(sides):
    nface = lax.axis_size("face")
    inner = [(f, face_partner(f, nface, False)) for f in range(nface)]
    outer = [(f, face_partner(f, nface, True)) for f in range(nface)]
    return lax.ppermute(sides[0], "face", inner), lax.ppermute(sides[1], "face", outer)


def swap_tiles(wide):
    nface = lax.axis_size("face")
    ntile = lax.axis_size("tile")
    inner = [(t, t ^ 1) for t in range(ntile)]
    outer = []
    for f in range(nface):
        for t in range(ntile):
            if t in (0, ntile - 1):
                to = ((f + 2) % nface) * ntile + t
            else:
                to = f * ntile + (t + 1 if t % 2 == 1 else t - 1)
            outer.append((f * ntile + t, to))
    return lax.ppermute(wide[0], "tile", inner), lax.ppermute(wide[1], ("face", "tile"), outer)


def gelu(x):
    half = 0.5 * x
    inner = x * (0.7978845608028654 + (0.7978845608028654 * 0.044715) * (x * x))
    return half + half * jnp.tanh(inner)


def conv_kernel(
    d,
    groups,
    has_residual,
    neighbor_ref,
    reversal_ref,
    grid_ref,
    ra_ref,
    rb_ref,
    wa_ref,
    wb_ref,
    taps_ref,
    bias_ref,
    *rest,
):
    if has_residual:
        fields_ref, out_ref, strip, weights, wide, acc, result, sems, out_sems, fields = rest
    else:
        out_ref, strip, weights, wide, acc, result, sems, out_sems = rest
    rows, cols, ch = grid_ref.shape
    face, tile, face_even, tile_even = parities()
    nface = lax.axis_size("face")
    last_tile = lax.axis_size("tile") - 1
    load = pltpu.make_async_copy(
        grid_ref, strip.at[pl.ds(d, rows), :, pl.ds(ch, ch)], sems.at[0]
    )
    load.start()
    if has_residual:
        load_fields = pltpu.make_async_copy(fields_ref, fields, sems.at[1])
        load_fields.start()

    for a in range(4):
        for e in range(3):
            at = (a * 3 + e) * ch
            if a < 3:
                weights[at : at + ch, :ch] = taps_ref[a * 3 + e]
            else:
                weights[at : at + ch, :ch] = jnp.zeros((ch, ch), BF16)
            if a > 0:
                weights[at : at + ch, ch:] = taps_ref[(a - 1) * 3 + e]
            else:
                weights[at : at + ch, ch:] = jnp.zeros((ch, ch), BF16)

    for r in range(d):
        wide[0, r] = jnp.where(tile_even, wb_ref[r].astype(F32), wa_ref[r].astype(F32)).astype(BF16)
        wide[1, r] = jnp.where(tile_even, wa_ref[r].astype(F32), wb_ref[r].astype(F32)).astype(BF16)
    load.wait()

    @pl.when((tile == 0) | (tile == last_tile))
    def _():
        which = jnp.where(tile == 0, 0, 1)
        sector = neighbor_ref[which, face]
        flip = reversal_ref[which, face]
        own = jnp.where(tile == 0, d, rows)
        width = cols + 2 * d

        def source_index(s):
            s = lax.rem(s + nface, nface)
            inner = jnp.where(face_even, face + 1, face - 1)
            outer = lax.rem(jnp.where(face_even, face - 1, face + 1) + nface, nface)
            return jnp.where(s == face, 0, jnp.where(s == inner, 1, jnp.where(s == outer, 2, 3)))

        place = iota((width, 1), 0)
        place = jnp.where(flip == 1, width - 1 - place, place)
        column = place - d + cols
        step = jnp.where(column >= 2 * cols, 2, jnp.where(column >= cols, 1, 0))
        inside = column - step * cols
        index = jnp.where(
            step == 0,
            source_index(sector - 1),
            jnp.where(step == 1, source_index(sector), source_index(sector + 1)),
        )
        wanted = index * cols + inside
        pick = jnp.where(iota((width, nface * cols), 1) == wanted, 1.0, 0.0).astype(BF16)
        for r in range(d):
            source = jnp.concatenate(
                [
                    strip[own + r, :, ch : 2 * ch],
                    ra_ref[d + r],
                    rb_ref[d + r],
                    wb_ref[r, d : d + cols, :],
                ],
                axis=0,
            )
            wide[which, d - 1 - r] = jnp.dot(pick, source, preferred_element_type=F32).astype(BF16)

    for side, at in ((0, 0), (1, rows + d)):
        for r in range(d):
            for e in range(3):
                strip[at + r, :, e * ch : (e + 1) * ch] = wide[side, r, e * d : e * d + cols, :]

    per = cols // d
    group = 8 // d

    def build(i, p):
        at = pl.multiple_of(i * 8, 8)
        a = ra_ref[p, pl.ds(at, 8), :].astype(F32)
        b = rb_ref[p, pl.ds(at, 8), :].astype(F32)
        west = jnp.where(face_even, b, a).astype(BF16)
        east = jnp.where(face_even, a, b).astype(BF16)
        for k in range(group):
            row = p * per + i * group + k + d
            v = strip[row, :, ch : 2 * ch]
            strip[row, d:, :ch] = v[: cols - d]
            strip[row, :d, :ch] = west[k * d : (k + 1) * d]
            strip[row, : cols - d, 2 * ch :] = v[d:]
            strip[row, cols - d :, 2 * ch :] = east[k * d : (k + 1) * d]
        return p

    def build_plane(p, carry):
        lax.fori_loop(0, per // group, build, p, unroll=2)
        return carry

    lax.fori_loop(0, d, build_plane, 0)
    if has_residual:
        load_fields.wait()

    bias = bias_ref[...]
    bias2 = jnp.concatenate([bias, bias], axis=1)
    m = d * cols
    step_rows = groups * 2 * d
    blocks = rows // step_rows

    def product(i):
        base = i * step_rows
        parts = []
        for a in range(4):
            of_a = [
                strip[pl.ds(base + g * 2 * d + a * d, d)].reshape(m, 3 * ch) for g in range(groups)
            ]
            parts.append(jnp.concatenate(of_a, axis=0))
        return jnp.dot(
            jnp.concatenate(parts, axis=1), weights[...], preferred_element_type=F32
        )

    def send(i):
        unit = step_rows if has_residual else step_rows * cols
        at = pl.ds(i * unit, unit)
        return pltpu.make_async_copy(result.at[at], out_ref.at[at], out_sems.at[i])

    def finish(i):
        y = gelu(acc[...] + bias2)
        for g in range(groups):
            for half in range(2):
                at = i * step_rows + g * 2 * d + half * d
                piece = y[g * m : (g + 1) * m, half * ch : (half + 1) * ch]
                if has_residual:
                    piece = piece.reshape(d, cols, ch) + fields[pl.ds(at, d)].astype(F32)
                    result[pl.ds(at, d)] = piece.astype(BF16)
                else:
                    result[pl.ds(pl.multiple_of(at * cols, m), m), :] = piece

    acc[...] = product(0)

    def block(i, carry):
        finish(i - 1)
        acc[...] = product(i)
        send(i - 1).start()
        return carry

    lax.fori_loop(1, blocks, block, 0)
    finish(blocks - 1)
    send(blocks - 1).start()
    for i in range(blocks):
        send(i).wait()


def conv(grid, sides, wide, neighbor, reversal, taps, bias, d, groups, fields, out_dtype):
    rows, cols, ch = grid.shape
    operands = [neighbor.T, reversal.T, far(grid) if fields is None else keep(grid), *[keep(x) for x in (*sides, *wide)], taps, bias.reshape(1, ch)]
    smem = full_spec(pltpu.SMEM)
    in_specs = [smem, smem, full_spec(pl.ANY)] + [full_spec()] * 6
    scratch = [
        VMEM((rows + 2 * d, cols, 3 * ch), BF16),
        VMEM((12 * ch, 2 * ch), BF16),
        VMEM((2, d, cols + 2 * d, ch), BF16),
        VMEM((groups * d * cols, 2 * ch), F32),
        VMEM((rows, cols, ch), out_dtype),
        pltpu.SemaphoreType.DMA((2,)),
        pltpu.SemaphoreType.DMA((rows // (groups * 2 * d),)),
    ]
    if fields is not None:
        operands.append(far(fields))
        in_specs.append(full_spec(pl.ANY))
        scratch.append(VMEM(fields.shape, BF16))
    out = (rows, cols, ch) if fields is not None else (rows * cols, ch)
    scratch[4] = VMEM(out, out_dtype)
    out = pltpu.HBM(out, out_dtype)
    return pl.pallas_call(
        functools.partial(conv_kernel, d, groups, fields is not None),
        out_shape=out,
        in_specs=in_specs,
        out_specs=full_spec(pl.ANY),
        scratch_shapes=scratch,
        cost_estimate=pl.CostEstimate(
            flops=2 * 12 * rows * cols * ch * ch, bytes_accessed=9_000_000, transcendentals=0
        ),
        compiler_params=room(28),
    )(*operands)


def scatter_kernel(
    d,
    recv,
    weight_ref,
    first_ref,
    mixed,
    a_ref,
    b_ref,
    ends_ref,
    first,
    even,
    extra,
    enc,
    cells_v,
    cells_s,
    sems,
):
    load = pltpu.make_async_copy(first_ref, first, sems.at[0])
    load.start()
    side, _, ch = mixed.shape
    sources = recv.shape[0]
    _, _, face_even, tile_even = parities()
    for g in range(sources // 8):
        meta = jnp.sum(recv[g * 8 : (g + 1) * 8, CAP:, :].astype(F32), axis=0)
        cells_v[g : g + 1, :] = (meta[0:1, :] * side + meta[1:2, :]).astype(I32)
    copy = pltpu.make_async_copy(cells_v, cells_s, sems.at[1])
    copy.start()
    for g in range(sources // 8):
        rows = recv[g * 8 : (g + 1) * 8, :CAP, :].reshape(8 * CAP, recv.shape[2])
        enc[g * 128 : (g + 1) * 128, :] = jnp.dot(
            rows, weight_ref[...], preferred_element_type=F32
        )

    def clear(r, carry):
        even[pl.ds(r * side, side), :] = jnp.zeros((side, ch), F32)
        extra[pl.ds(r * side, side), :] = jnp.zeros((side, ch), F32)
        return carry

    lax.fori_loop(0, side, clear, 0, unroll=4)
    copy.wait()

    def add_rows(g, carry):
        for j in range(0, 128, 2):
            for k, target in ((0, even), (1, extra)):
                c = cells_s[g, j + k]
                target[pl.ds(c, 1), :] += enc[pl.ds(g * 128 + j + k, 1), :]
        return carry

    lax.fori_loop(0, sources // 8, add_rows, 0)
    load.wait()

    per = side // d
    group = 8 // d

    def plane(p, carry):
        def rows_of(i, inner):
            west = []
            east = []
            for k in range(group):
                row = p * per + i * group + k
                at = pl.ds(pl.multiple_of(row * side, side), side)
                v = first[at, :] + even[at, :] + extra[at, :]
                mixed[row] = v.astype(BF16)
                west.append(v[:d])
                east.append(v[side - d :])
            west = jnp.concatenate(west, axis=0)
            east = jnp.concatenate(east, axis=0)
            at = pl.ds(pl.multiple_of(i * 8, 8), 8)
            a_ref[p, at, :] = jnp.where(face_even, east, west).astype(BF16)
            b_ref[p, at, :] = jnp.where(face_even, west, east).astype(BF16)
            return inner

        lax.fori_loop(0, per // group, rows_of, 0, unroll=2)
        return carry

    lax.fori_loop(0, d, plane, 0)
    start = jnp.where(tile_even, 0, side - d)
    for r in range(d):
        row = mixed[start + r]
        a_ref[d + r] = row
        b_ref[d + r] = row
        ends_ref[0, r] = mixed[r]
        ends_ref[1, r] = mixed[side - d + r]


def scatter(recv, weight, first, d):
    cells, ch = first.shape
    side = cols = round(cells**0.5)
    sources = recv.shape[0]
    out = VMEM((2 * d, cols, ch), BF16)
    return pl.pallas_call(
        functools.partial(scatter_kernel, d),
        out_shape=(VMEM((side, cols, ch), BF16), out, out, VMEM((2, d, cols, ch), BF16)),
        in_specs=[full_spec(), full_spec(), full_spec(pl.ANY)],
        out_specs=(full_spec(),) * 4,
        scratch_shapes=[
            VMEM(first.shape, F32),
            VMEM(first.shape, F32),
            VMEM(first.shape, F32),
            VMEM((sources * CAP, ch), F32),
            VMEM((sources // 8, 128), I32),
            pltpu.SMEM((sources // 8, 128), I32),
            pltpu.SemaphoreType.DMA((2,)),
        ],
        cost_estimate=pl.CostEstimate(
            flops=200_000_000, bytes_accessed=12_000_000, transcendentals=0
        ),
        compiler_params=room(28),
        name="scatter",
    )(keep(recv), weight, far(first))


def local(
    fields,
    first_kernel_taps,
    first_conv_bias,
    second_kernel_taps,
    second_conv_bias,
    obs_weight,
    obs_values,
    obs_owner,
    obs_cells,
    polar_neighbor_sector,
    polar_link_reversal,
):
    side = fields.shape[0]
    dests = lax.axis_size("face") * lax.axis_size("tile")
    d = FIRST_DILATION
    a, b, ends = edges(fields, d)
    sides = swap_faces((a, b))
    send = pack(obs_owner, obs_cells, obs_values, dests, side)
    wide = widen(ends, sides, d)
    send, wide = lax.optimization_barrier((send, wide))
    wide = swap_tiles(wide)
    recv = lax.all_to_all(send, ("face", "tile"), split_axis=0, concat_axis=0, tiled=True)
    first = conv(
        fields, sides, wide, polar_neighbor_sector, polar_link_reversal,
        first_kernel_taps, first_conv_bias, d, 4, None, F32,
    )
    d = SECOND_DILATION
    mixed, a, b, ends = scatter(recv, obs_weight, first, d)
    sides = swap_faces((a, b))
    wide = swap_tiles(widen(ends, sides, d))
    return conv(
        mixed, sides, wide, polar_neighbor_sector, polar_link_reversal,
        second_kernel_taps, second_conv_bias, d, 2, fields, BF16,
    )


def solution(mesh):
    in_specs = (
        P("tile", "face", None),
        P(),
        P(),
        P(),
        P(),
        P(),
        P(("face", "tile"), None),
        P(("face", "tile"), None),
        P(("face", "tile")),
        P(),
        P(),
    )
    out_specs = P("tile", "face", None)
    return jax.shard_map(local, mesh=mesh, in_specs=in_specs, out_specs=out_specs, check_vma=False)
```

```python
import functools

import jax
import jax.numpy as jnp
from jax import lax
from jax.experimental import pallas as pl
from jax.experimental.pallas import tpu as pltpu
from jax.sharding import PartitionSpec as P

FIRST_DILATION = 2
SECOND_DILATION = 4
CAP = 16
META = 8

BF16 = jnp.bfloat16
F32 = jnp.float32
I32 = jnp.int32
VMEM = pltpu.VMEM


def full_spec(memory_space=None):
    return pl.BlockSpec(memory_space=VMEM if memory_space is None else memory_space)


def room(mebibytes):
    return pltpu.CompilerParams(vmem_limit_bytes=mebibytes << 20)


def far(x):
    return pltpu.with_memory_space_constraint(x, pltpu.HBM)


def keep(x):
    return pltpu.with_memory_space_constraint(x, VMEM)


def iota(shape, axis):
    return lax.broadcasted_iota(I32, shape, axis)


def pack_kernel(dests, side, owner_ref, cell_ref, vals_ref, send_ref):
    rows = vals_ref.shape[0]
    owner = owner_ref[...]
    cell = cell_ref[...]
    block = 256
    earlier = (iota((block, block), 0) < iota((block, block), 1)).astype(F32).astype(BF16)
    onehot_parts = []
    rank_parts = []
    carry = jnp.zeros((dests, 1), F32)
    for b in range(rows // block):
        hit = owner[:, b * block : (b + 1) * block] == iota((dests, block), 0)
        hit_f = jnp.where(hit, 1.0, 0.0)
        hit_b = hit_f.astype(BF16)
        before = jnp.dot(hit_b, earlier, preferred_element_type=F32) + carry
        rank_parts.append(jnp.sum(before * hit_f, axis=0, keepdims=True))
        carry = carry + jnp.sum(hit_f, axis=1, keepdims=True)
        onehot_parts.append(hit_b)
    rank = jnp.concatenate(rank_parts, axis=1).astype(I32)
    onehot = jnp.concatenate(onehot_parts, axis=1)
    target = owner * CAP + rank

    cell_row = ((cell.astype(F32) + 0.5) * (1.0 / side)).astype(I32)
    cell_col = cell - cell_row * side
    me = lax.axis_index("face") * lax.axis_size("tile") + lax.axis_index("tile")
    base_lane = lax.rem(me, 8) * CAP
    slot_hit = iota((128, rows), 0) == rank + base_lane
    row_map = jnp.where(slot_hit, cell_row.astype(F32), 0.0).astype(BF16)
    col_map = jnp.where(slot_hit, cell_col.astype(F32), 0.0).astype(BF16)
    contract = (((1,), (1,)), ((), ()))
    meta_row = lax.dot_general(onehot, row_map, contract, preferred_element_type=F32)
    meta_col = lax.dot_general(onehot, col_map, contract, preferred_element_type=F32)
    meta = jnp.where(
        iota((dests, META, 128), 1) == 0,
        jnp.broadcast_to(meta_row[:, None, :], (dests, META, 128)),
        jnp.broadcast_to(meta_col[:, None, :], (dests, META, 128)),
    )
    send_ref[:, CAP:, :] = meta.astype(BF16)

    chunk_dests = 16
    chunk = chunk_dests * CAP
    for c in range(dests // chunk_dests):
        match = target == iota((chunk, rows), 0) + c * chunk
        match = jnp.where(match, 1.0, 0.0).astype(BF16)
        placed = jnp.dot(match, vals_ref[...], preferred_element_type=F32).astype(BF16)
        send_ref[c * chunk_dests : (c + 1) * chunk_dests, :CAP, :] = placed.reshape(
            chunk_dests, CAP, placed.shape[-1]
        )


def pack(owner, cells, vals, dests, side):
    rows, features = vals.shape
    return pl.pallas_call(
        functools.partial(pack_kernel, dests, side),
        out_shape=jax.ShapeDtypeStruct((dests, CAP + META, features), BF16),
        in_specs=[full_spec()] * 3,
        out_specs=full_spec(),
        cost_estimate=pl.CostEstimate(
            flops=2 * dests * CAP * rows * features, bytes_accessed=2_000_000, transcendentals=0
        ),
        compiler_params=room(16),
        name="pack",
    )(owner.reshape(1, rows), cells.reshape(1, rows), vals)


def parities():
    face = lax.axis_index("face")
    tile = lax.axis_index("tile")
    return face, tile, lax.rem(face, 2) == 0, lax.rem(tile, 2) == 0


def edges_kernel(d, grid_ref, a_ref, b_ref, ends_ref, low, high, sems):
    rows, cols, _ = grid_ref.shape
    _, _, face_even, tile_even = parities()
    start = jnp.where(tile_even, 0, rows - d)
    copies = [
        pltpu.make_async_copy(grid_ref.at[:, pl.ds(0, 8), :], low, sems.at[0]),
        pltpu.make_async_copy(grid_ref.at[:, pl.ds(cols - 8, 8), :], high, sems.at[1]),
        pltpu.make_async_copy(grid_ref.at[pl.ds(start, d)], a_ref.at[pl.ds(d, d)], sems.at[2]),
        pltpu.make_async_copy(grid_ref.at[pl.ds(start, d)], b_ref.at[pl.ds(d, d)], sems.at[3]),
        pltpu.make_async_copy(grid_ref.at[pl.ds(0, d)], ends_ref.at[0], sems.at[4]),
        pltpu.make_async_copy(grid_ref.at[pl.ds(rows - d, d)], ends_ref.at[1], sems.at[5]),
    ]
    for copy in copies:
        copy.start()
    for copy in copies:
        copy.wait()
    per = cols // d
    group = 8 // d

    def plane(p, carry):
        for r in range(0, per, group):
            at = [p * per + r + k for k in range(group)]
            west = jnp.concatenate([low[i].astype(F32)[:d] for i in at], axis=0)
            east = jnp.concatenate([high[i].astype(F32)[8 - d :] for i in at], axis=0)
            a_ref[p, r * d : r * d + 8, :] = jnp.where(face_even, east, west).astype(BF16)
            b_ref[p, r * d : r * d + 8, :] = jnp.where(face_even, west, east).astype(BF16)
        return carry

    lax.fori_loop(0, d, plane, 0)


def edges(grid, d):
    rows, cols, ch = grid.shape
    side = VMEM((2 * d, cols, ch), BF16)
    return pl.pallas_call(
        functools.partial(edges_kernel, d),
        out_shape=(side, side, VMEM((2, d, cols, ch), BF16)),
        in_specs=[full_spec(pl.ANY)],
        out_specs=(full_spec(),) * 3,
        scratch_shapes=[
            VMEM((rows, 8, ch), BF16),
            VMEM((rows, 8, ch), BF16),
            pltpu.SemaphoreType.DMA((6,)),
        ],
        cost_estimate=pl.CostEstimate(flops=1_000_000, bytes_accessed=800_000, transcendentals=0),
        compiler_params=room(8),
        name="edges",
    )(far(grid))


def widen_kernel(d, ends_ref, ra_ref, rb_ref, wa_ref, wb_ref):
    cols = ends_ref.shape[2]
    rows = cols
    _, _, face_even, tile_even = parities()
    per = cols // d
    for r in range(d):
        wide = []
        for i, row in enumerate((r, rows - d + r)):
            at = (row % per) * d
            tile_at = at // 8 * 8
            a = ra_ref[row // per, tile_at : tile_at + 8, :].astype(F32)[at - tile_at : at - tile_at + d]
            b = rb_ref[row // per, tile_at : tile_at + 8, :].astype(F32)[at - tile_at : at - tile_at + d]
            wide.append(
                jnp.concatenate(
                    [
                        jnp.where(face_even, b, a),
                        ends_ref[i, r].astype(F32),
                        jnp.where(face_even, a, b),
                    ],
                    axis=0,
                )
            )
        wa_ref[r] = jnp.where(tile_even, wide[1], wide[0]).astype(BF16)
        wb_ref[r] = jnp.where(tile_even, wide[0], wide[1]).astype(BF16)


def widen(ends, received, d):
    _, _, cols, ch = ends.shape
    wide = VMEM((d, cols + 2 * d, ch), BF16)
    return pl.pallas_call(
        functools.partial(widen_kernel, d),
        out_shape=(wide, wide),
        in_specs=[full_spec()] * 3,
        out_specs=(full_spec(), full_spec()),
        cost_estimate=pl.CostEstimate(flops=1_000_000, bytes_accessed=800_000, transcendentals=0),
        compiler_params=room(8),
        name="widen",
    )(keep(ends), *[keep(x) for x in received])


def face_partner(f, nface, odd_up):
    return (f + 1) % nface if (f % 2 == 1) == odd_up else (f - 1) % nface


def swap_faces(sides):
    nface = lax.axis_size("face")
    inner = [(f, face_partner(f, nface, False)) for f in range(nface)]
    outer = [(f, face_partner(f, nface, True)) for f in range(nface)]
    return lax.ppermute(sides[0], "face", inner), lax.ppermute(sides[1], "face", outer)


def swap_tiles(wide):
    nface = lax.axis_size("face")
    ntile = lax.axis_size("tile")
    inner = [(t, t ^ 1) for t in range(ntile)]
    outer = []
    for f in range(nface):
        for t in range(ntile):
            if t in (0, ntile - 1):
                to = ((f + 2) % nface) * ntile + t
            else:
                to = f * ntile + (t + 1 if t % 2 == 1 else t - 1)
            outer.append((f * ntile + t, to))
    return lax.ppermute(wide[0], "tile", inner), lax.ppermute(wide[1], ("face", "tile"), outer)


def gelu(x):
    half = 0.5 * x
    inner = x * (0.7978845608028654 + (0.7978845608028654 * 0.044715) * (x * x))
    return half + half * jnp.tanh(inner)


def pair_weights_kernel(taps_ref, weights):
    ch = taps_ref.shape[1]
    for a in range(4):
        for e in range(3):
            at = (a * 3 + e) * ch
            if a < 3:
                weights[at : at + ch, :ch] = taps_ref[a * 3 + e]
            else:
                weights[at : at + ch, :ch] = jnp.zeros((ch, ch), BF16)
            if a > 0:
                weights[at : at + ch, ch:] = taps_ref[(a - 1) * 3 + e]
            else:
                weights[at : at + ch, ch:] = jnp.zeros((ch, ch), BF16)


def pair_weights(taps):
    ch = taps.shape[1]
    return pl.pallas_call(
        pair_weights_kernel,
        out_shape=VMEM((12 * ch, 2 * ch), BF16),
        in_specs=[full_spec()],
        out_specs=full_spec(),
        cost_estimate=pl.CostEstimate(flops=1_000_000, bytes_accessed=1_000_000, transcendentals=0),
        compiler_params=room(4),
        name="pair_weights",
    )(taps)


EDGE = 8


def shifted_copies(strip_row, west, east, d):
    cols = strip_row.shape[0]
    ch = strip_row.shape[1] // 3
    v = strip_row[:, ch : 2 * ch]
    strip_row[d:, :ch] = v[: cols - d]
    strip_row[:d, :ch] = west
    strip_row[: cols - d, 2 * ch :] = v[d:]
    strip_row[cols - d :, 2 * ch :] = east


def side_tile(ra_ref, rb_ref, p, at, face_even):
    a = ra_ref[p, at, :].astype(F32)
    b = rb_ref[p, at, :].astype(F32)
    west = jnp.where(face_even, b, a).astype(BF16)
    east = jnp.where(face_even, a, b).astype(BF16)
    return west, east


def pair_rows(strip, bases, d):
    _, cols, wide = strip.shape
    parts = []
    for a in range(4):
        of_a = [strip[pl.ds(base + a * d, d)].reshape(d * cols, wide) for base in bases]
        parts.append(jnp.concatenate(of_a, axis=0))
    return jnp.concatenate(parts, axis=1)


def rows_kernel(d, step_rows, has_residual, grid_ref, ra_ref, rb_ref, weights, bias_ref, *rest):
    if has_residual:
        fields_ref, out_ref, strip, acc, result, sems, out_sems, fields = rest
    else:
        out_ref, strip, acc, result, sems, out_sems = rest
    rows, cols, ch = grid_ref.shape
    _, _, face_even, _ = parities()
    inner = rows - 2 * EDGE
    first = EDGE - 4
    load = pltpu.make_async_copy(
        grid_ref.at[pl.ds(first, inner + 8)], strip.at[:, :, pl.ds(ch, ch)], sems.at[0]
    )
    load.start()
    if has_residual:
        load_fields = pltpu.make_async_copy(
            fields_ref.at[pl.ds(EDGE, inner)], fields, sems.at[1]
        )
        load_fields.start()
    load.wait()
    group = 8 // d
    per_plane = cols // 8

    def build(t, carry):
        p = lax.div(t, per_plane)
        at = pl.multiple_of((t - p * per_plane) * 8, 8)
        west, east = side_tile(ra_ref, rb_ref, p, pl.ds(at, 8), face_even)
        for k in range(group):
            shifted_copies(
                strip.at[t * group + k - first],
                west[k * d : (k + 1) * d],
                east[k * d : (k + 1) * d],
                d,
            )
        return carry

    lax.fori_loop(first // group, (first + inner + 8) // group, build, 0, unroll=2)
    if has_residual:
        load_fields.wait()

    bias = bias_ref[...]
    bias2 = jnp.concatenate([bias, bias], axis=1)
    m = d * cols
    groups = step_rows // (2 * d)
    blocks = inner // step_rows

    def product(i):
        base = i * step_rows + 4 - d
        lhs = pair_rows(strip, [base + g * 2 * d for g in range(groups)], d)
        return jnp.dot(lhs, weights[...], preferred_element_type=F32)

    def send(i):
        return pltpu.make_async_copy(
            result.at[pl.ds(i * step_rows, step_rows)],
            out_ref.at[pl.ds(EDGE + i * step_rows, step_rows)],
            out_sems.at[i],
        )

    def finish(i):
        y = gelu(acc[...] + bias2)
        for g in range(groups):
            for half in range(2):
                at = i * step_rows + g * 2 * d + half * d
                piece = y[g * m : (g + 1) * m, half * ch : (half + 1) * ch].reshape(d, cols, ch)
                if has_residual:
                    piece = piece + fields[pl.ds(at, d)].astype(F32)
                result[pl.ds(at, d)] = piece.astype(result.dtype)

    acc[...] = product(0)

    def block(i, carry):
        finish(i - 1)
        acc[...] = product(i)
        send(i - 1).start()
        return carry

    lax.fori_loop(1, blocks, block, 0)
    finish(blocks - 1)
    send(blocks - 1).start()
    for i in range(blocks):
        send(i).wait()


def conv_rows(grid, sides, weights, bias, d, fields, out_dtype):
    rows, cols, ch = grid.shape
    step_rows = 16
    inner = rows - 2 * EDGE
    operands = [far(grid) if fields is None else keep(grid), *[keep(x) for x in sides]]
    operands += [keep(weights), bias.reshape(1, ch)]
    in_specs = [full_spec(pl.ANY)] + [full_spec()] * 4
    scratch = [
        VMEM((inner + 8, cols, 3 * ch), BF16),
        VMEM((step_rows // 2 * cols, 2 * ch), F32),
        VMEM((inner, cols, ch), out_dtype),
        pltpu.SemaphoreType.DMA((2,)),
        pltpu.SemaphoreType.DMA((inner // step_rows,)),
    ]
    if fields is not None:
        operands.append(far(fields))
        in_specs.append(full_spec(pl.ANY))
        scratch.append(VMEM((inner, cols, ch), BF16))
    return pl.pallas_call(
        functools.partial(rows_kernel, d, step_rows, fields is not None),
        out_shape=pltpu.HBM((rows, cols, ch), out_dtype),
        in_specs=in_specs,
        out_specs=full_spec(pl.ANY),
        scratch_shapes=scratch,
        cost_estimate=pl.CostEstimate(
            flops=2 * 12 * rows * cols * ch * ch, bytes_accessed=9_000_000, transcendentals=0
        ),
        compiler_params=room(28),
        name="conv_rows",
    )(*operands)


def ends_kernel(
    d,
    has_residual,
    neighbor_ref,
    reversal_ref,
    grid_ref,
    ra_ref,
    rb_ref,
    wa_ref,
    wb_ref,
    weights,
    bias_ref,
    *rest,
):
    if has_residual:
        fields_ref, _, out_ref, strip, wide, result, sems, fields = rest
    else:
        _, out_ref, strip, wide, result, sems = rest
    rows, cols, ch = grid_ref.shape
    face, tile, face_even, tile_even = parities()
    nface = lax.axis_size("face")
    last_tile = lax.axis_size("tile") - 1
    span = EDGE + 2 * d
    own = EDGE + d
    loads = []
    for side, at, to in ((0, 0, d), (1, rows - own, span)):
        loads.append(
            pltpu.make_async_copy(
                grid_ref.at[pl.ds(at, own)],
                strip.at[pl.ds(to, own), :, pl.ds(ch, ch)],
                sems.at[side],
            )
        )
        loads[-1].start()
    if has_residual:
        for side, at in ((0, 0), (1, rows - EDGE)):
            loads.append(
                pltpu.make_async_copy(
                    fields_ref.at[pl.ds(at, EDGE)],
                    fields.at[pl.ds(side * EDGE, EDGE)],
                    sems.at[2 + side],
                )
            )
            loads[-1].start()
    for r in range(d):
        a = wa_ref[r].astype(F32)
        b = wb_ref[r].astype(F32)
        wide[0, r] = jnp.where(tile_even, b, a).astype(BF16)
        wide[1, r] = jnp.where(tile_even, a, b).astype(BF16)
    for load in loads:
        load.wait()

    @pl.when((tile == 0) | (tile == last_tile))
    def _():
        which = jnp.where(tile == 0, 0, 1)
        sector = neighbor_ref[which, face]
        flip = reversal_ref[which, face]
        mine = jnp.where(tile == 0, d, span + EDGE)
        width = cols + 2 * d

        def source_index(s):
            s = lax.rem(s + nface, nface)
            inner = jnp.where(face_even, face + 1, face - 1)
            outer = lax.rem(jnp.where(face_even, face - 1, face + 1) + nface, nface)
            return jnp.where(s == face, 0, jnp.where(s == inner, 1, jnp.where(s == outer, 2, 3)))

        place = iota((width, 1), 0)
        place = jnp.where(flip == 1, width - 1 - place, place)
        column = place - d + cols
        step = jnp.where(column >= 2 * cols, 2, jnp.where(column >= cols, 1, 0))
        inside = column - step * cols
        index = jnp.where(
            step == 0,
            source_index(sector - 1),
            jnp.where(step == 1, source_index(sector), source_index(sector + 1)),
        )
        wanted = index * cols + inside
        pick = jnp.where(iota((width, nface * cols), 1) == wanted, 1.0, 0.0).astype(BF16)
        for r in range(d):
            source = jnp.concatenate(
                [
                    strip[mine + r, :, ch : 2 * ch],
                    ra_ref[d + r],
                    rb_ref[d + r],
                    wb_ref[r, d : d + cols, :],
                ],
                axis=0,
            )
            wide[which, d - 1 - r] = jnp.dot(pick, source, preferred_element_type=F32).astype(BF16)

    for side, at in ((0, 0), (1, span + own)):
        for r in range(d):
            for e in range(3):
                strip[at + r, :, e * ch : (e + 1) * ch] = wide[side, r, e * d : e * d + cols, :]

    group = 8 // d
    per_plane = cols // 8
    for low, high, to in ((0, own, d), (rows - own, rows, span)):
        for t in range(low // group, -(-high // group)):
            p, at = divmod(t, per_plane)
            west, east = side_tile(ra_ref, rb_ref, p, slice(at * 8, at * 8 + 8), face_even)
            for k in range(group):
                row = t * group + k
                if low <= row < high:
                    shifted_copies(
                        strip.at[row - low + to],
                        west[k * d : (k + 1) * d],
                        east[k * d : (k + 1) * d],
                        d,
                    )

    bias = bias_ref[...]
    bias2 = jnp.concatenate([bias, bias], axis=1)
    m = d * cols
    starts = [(side, g * 2 * d) for side in range(2) for g in range(EDGE // (2 * d))]
    lhs = pair_rows(strip, [side * span + at for side, at in starts], d)
    y = gelu(jnp.dot(lhs, weights[...], preferred_element_type=F32) + bias2)
    for g, (side, at) in enumerate(starts):
        for half in range(2):
            to = side * EDGE + at + half * d
            piece = y[g * m : (g + 1) * m, half * ch : (half + 1) * ch].reshape(d, cols, ch)
            if has_residual:
                piece = piece + fields[to : to + d].astype(F32)
            result[to : to + d] = piece.astype(result.dtype)
    stores = [
        pltpu.make_async_copy(
            result.at[pl.ds(side * EDGE, EDGE)], out_ref.at[pl.ds(at, EDGE)], sems.at[4 + side]
        )
        for side, at in ((0, 0), (1, rows - EDGE))
    ]
    for store in stores:
        store.start()
    for store in stores:
        store.wait()


def conv_ends(out, grid, sides, wide, neighbor, reversal, weights, bias, d, fields):
    _, cols, ch = grid.shape
    operands = [neighbor.T, reversal.T, far(grid) if fields is None else keep(grid)]
    operands += [keep(x) for x in (*sides, *wide, weights)] + [bias.reshape(1, ch)]
    smem = full_spec(pltpu.SMEM)
    in_specs = [smem, smem, full_spec(pl.ANY)] + [full_spec()] * 6
    scratch = [
        VMEM((2 * (EDGE + 2 * d), cols, 3 * ch), BF16),
        VMEM((2, d, cols + 2 * d, ch), BF16),
        VMEM((2 * EDGE, cols, ch), out.dtype),
        pltpu.SemaphoreType.DMA((6,)),
    ]
    if fields is not None:
        operands.append(far(fields))
        in_specs.append(full_spec(pl.ANY))
        scratch.append(VMEM((2 * EDGE, cols, ch), BF16))
    operands.append(far(out))
    in_specs.append(full_spec(pl.ANY))
    return pl.pallas_call(
        functools.partial(ends_kernel, d, fields is not None),
        out_shape=pltpu.HBM(out.shape, out.dtype),
        in_specs=in_specs,
        out_specs=full_spec(pl.ANY),
        scratch_shapes=scratch,
        input_output_aliases={len(operands) - 1: 0},
        cost_estimate=pl.CostEstimate(
            flops=4 * 12 * EDGE * cols * ch * ch, bytes_accessed=1_000_000, transcendentals=0
        ),
        compiler_params=room(16),
        name="conv_ends",
    )(*operands)


def scatter_kernel(
    d,
    recv,
    weight_ref,
    first_ref,
    mixed,
    a_ref,
    b_ref,
    ends_ref,
    first,
    even,
    extra,
    enc,
    cells_v,
    cells_s,
    sems,
):
    load = pltpu.make_async_copy(first_ref, first, sems.at[0])
    load.start()
    side, _, ch = mixed.shape
    sources = recv.shape[0]
    _, _, face_even, tile_even = parities()
    for g in range(sources // 8):
        meta = jnp.sum(recv[g * 8 : (g + 1) * 8, CAP:, :].astype(F32), axis=0)
        cells_v[g : g + 1, :] = (meta[0:1, :] * side + meta[1:2, :]).astype(I32)
    copy = pltpu.make_async_copy(cells_v, cells_s, sems.at[1])
    copy.start()
    for g in range(sources // 8):
        rows = recv[g * 8 : (g + 1) * 8, :CAP, :].reshape(8 * CAP, recv.shape[2])
        enc[g * 128 : (g + 1) * 128, :] = jnp.dot(
            rows, weight_ref[...], preferred_element_type=F32
        )

    def clear(r, carry):
        even[pl.ds(r * side, side), :] = jnp.zeros((side, ch), F32)
        extra[pl.ds(r * side, side), :] = jnp.zeros((side, ch), F32)
        return carry

    lax.fori_loop(0, side, clear, 0, unroll=4)
    copy.wait()

    def add_rows(g, carry):
        for j in range(0, 128, 2):
            for k, target in ((0, even), (1, extra)):
                c = cells_s[g, j + k]
                target[pl.ds(c, 1), :] += enc[pl.ds(g * 128 + j + k, 1), :]
        return carry

    lax.fori_loop(0, sources // 8, add_rows, 0)
    load.wait()

    per = side // d
    group = 8 // d

    def plane(p, carry):
        def rows_of(i, inner):
            west = []
            east = []
            for k in range(group):
                row = p * per + i * group + k
                at = pl.ds(pl.multiple_of(row * side, side), side)
                v = first[row] + even[at, :] + extra[at, :]
                mixed[row] = v.astype(BF16)
                west.append(v[:d])
                east.append(v[side - d :])
            west = jnp.concatenate(west, axis=0)
            east = jnp.concatenate(east, axis=0)
            at = pl.ds(pl.multiple_of(i * 8, 8), 8)
            a_ref[p, at, :] = jnp.where(face_even, east, west).astype(BF16)
            b_ref[p, at, :] = jnp.where(face_even, west, east).astype(BF16)
            return inner

        lax.fori_loop(0, per // group, rows_of, 0, unroll=2)
        return carry

    lax.fori_loop(0, d, plane, 0)
    start = jnp.where(tile_even, 0, side - d)
    for r in range(d):
        row = mixed[start + r]
        a_ref[d + r] = row
        b_ref[d + r] = row
        ends_ref[0, r] = mixed[r]
        ends_ref[1, r] = mixed[side - d + r]


def scatter(recv, weight, first, d):
    side, cols, ch = first.shape
    sources = recv.shape[0]
    out = VMEM((2 * d, cols, ch), BF16)
    return pl.pallas_call(
        functools.partial(scatter_kernel, d),
        out_shape=(VMEM((side, cols, ch), BF16), out, out, VMEM((2, d, cols, ch), BF16)),
        in_specs=[full_spec(), full_spec(), full_spec(pl.ANY)],
        out_specs=(full_spec(),) * 4,
        scratch_shapes=[
            VMEM(first.shape, F32),
            VMEM((side * cols, ch), F32),
            VMEM((side * cols, ch), F32),
            VMEM((sources * CAP, ch), F32),
            VMEM((sources // 8, 128), I32),
            pltpu.SMEM((sources // 8, 128), I32),
            pltpu.SemaphoreType.DMA((2,)),
        ],
        cost_estimate=pl.CostEstimate(
            flops=200_000_000, bytes_accessed=12_000_000, transcendentals=0
        ),
        compiler_params=room(28),
        name="scatter",
    )(keep(recv), weight, far(first))


def local(
    fields,
    first_kernel_taps,
    first_conv_bias,
    second_kernel_taps,
    second_conv_bias,
    obs_weight,
    obs_values,
    obs_owner,
    obs_cells,
    polar_neighbor_sector,
    polar_link_reversal,
):
    side = fields.shape[0]
    dests = lax.axis_size("face") * lax.axis_size("tile")
    d = FIRST_DILATION
    weights = pair_weights(first_kernel_taps)
    a, b, ends = edges(fields, d)
    sides = swap_faces((a, b))
    send = pack(obs_owner, obs_cells, obs_values, dests, side)
    recv = lax.all_to_all(send, ("face", "tile"), split_axis=0, concat_axis=0, tiled=True)
    wide = swap_tiles(widen(ends, sides, d))
    first = conv_rows(fields, sides, weights, first_conv_bias, d, None, F32)
    first = conv_ends(
        first, fields, sides, wide, polar_neighbor_sector, polar_link_reversal,
        weights, first_conv_bias, d, None,
    )
    d = SECOND_DILATION
    weights = pair_weights(second_kernel_taps)
    mixed, a, b, ends = scatter(recv, obs_weight, first, d)
    sides = swap_faces((a, b))
    wide = swap_tiles(widen(ends, sides, d))
    out = conv_rows(mixed, sides, weights, second_conv_bias, d, fields, BF16)
    return conv_ends(
        out, mixed, sides, wide, polar_neighbor_sector, polar_link_reversal,
        weights, second_conv_bias, d, fields,
    )


def solution(mesh):
    in_specs = (
        P("tile", "face", None),
        P(),
        P(),
        P(),
        P(),
        P(),
        P(("face", "tile"), None),
        P(("face", "tile"), None),
        P(("face", "tile")),
        P(),
        P(),
    )
    out_specs = P("tile", "face", None)
    return jax.shard_map(local, mesh=mesh, in_specs=in_specs, out_specs=out_specs, check_vma=False)
```

```python
import functools

import jax
import jax.numpy as jnp
from jax import lax
from jax.experimental import pallas as pl
from jax.experimental.pallas import tpu as pltpu
from jax.sharding import PartitionSpec as P

FIRST_DILATION = 2
SECOND_DILATION = 4
CAP = 16
META = 8

BF16 = jnp.bfloat16
F32 = jnp.float32
I32 = jnp.int32
VMEM = pltpu.VMEM


def full_spec(memory_space=None):
    return pl.BlockSpec(memory_space=VMEM if memory_space is None else memory_space)


def room(mebibytes):
    return pltpu.CompilerParams(vmem_limit_bytes=mebibytes << 20)


def far(x):
    return pltpu.with_memory_space_constraint(x, pltpu.HBM)


def keep(x):
    return pltpu.with_memory_space_constraint(x, VMEM)


def iota(shape, axis):
    return lax.broadcasted_iota(I32, shape, axis)


def pack_kernel(dests, side, owner_ref, cell_ref, vals_ref, send_ref):
    rows = vals_ref.shape[0]
    owner = owner_ref[...]
    cell = cell_ref[...]
    block = 256
    earlier = (iota((block, block), 0) < iota((block, block), 1)).astype(F32).astype(BF16)
    onehot_parts = []
    rank_parts = []
    carry = jnp.zeros((dests, 1), F32)
    for b in range(rows // block):
        hit = owner[:, b * block : (b + 1) * block] == iota((dests, block), 0)
        hit_f = jnp.where(hit, 1.0, 0.0)
        hit_b = hit_f.astype(BF16)
        before = jnp.dot(hit_b, earlier, preferred_element_type=F32) + carry
        rank_parts.append(jnp.sum(before * hit_f, axis=0, keepdims=True))
        carry = carry + jnp.sum(hit_f, axis=1, keepdims=True)
        onehot_parts.append(hit_b)
    rank = jnp.concatenate(rank_parts, axis=1).astype(I32)
    onehot = jnp.concatenate(onehot_parts, axis=1)
    target = owner * CAP + rank

    cell_row = ((cell.astype(F32) + 0.5) * (1.0 / side)).astype(I32)
    cell_col = cell - cell_row * side
    me = lax.axis_index("face") * lax.axis_size("tile") + lax.axis_index("tile")
    base_lane = lax.rem(me, 8) * CAP
    slot_hit = iota((128, rows), 0) == rank + base_lane
    row_map = jnp.where(slot_hit, cell_row.astype(F32), 0.0).astype(BF16)
    col_map = jnp.where(slot_hit, cell_col.astype(F32), 0.0).astype(BF16)
    contract = (((1,), (1,)), ((), ()))
    meta_row = lax.dot_general(onehot, row_map, contract, preferred_element_type=F32)
    meta_col = lax.dot_general(onehot, col_map, contract, preferred_element_type=F32)
    meta = jnp.where(
        iota((dests, META, 128), 1) == 0,
        jnp.broadcast_to(meta_row[:, None, :], (dests, META, 128)),
        jnp.broadcast_to(meta_col[:, None, :], (dests, META, 128)),
    )
    send_ref[:, CAP:, :] = meta.astype(BF16)

    chunk_dests = 16
    chunk = chunk_dests * CAP
    for c in range(dests // chunk_dests):
        match = target == iota((chunk, rows), 0) + c * chunk
        match = jnp.where(match, 1.0, 0.0).astype(BF16)
        placed = jnp.dot(match, vals_ref[...], preferred_element_type=F32).astype(BF16)
        send_ref[c * chunk_dests : (c + 1) * chunk_dests, :CAP, :] = placed.reshape(
            chunk_dests, CAP, placed.shape[-1]
        )


def pack(owner, cells, vals, dests, side):
    rows, features = vals.shape
    return pl.pallas_call(
        functools.partial(pack_kernel, dests, side),
        out_shape=jax.ShapeDtypeStruct((dests, CAP + META, features), BF16),
        in_specs=[full_spec()] * 3,
        out_specs=full_spec(),
        cost_estimate=pl.CostEstimate(
            flops=2 * dests * CAP * rows * features, bytes_accessed=2_000_000, transcendentals=0
        ),
        compiler_params=room(16),
        name="pack",
    )(owner.reshape(1, rows), cells.reshape(1, rows), vals)


def parities():
    face = lax.axis_index("face")
    tile = lax.axis_index("tile")
    return face, tile, lax.rem(face, 2) == 0, lax.rem(tile, 2) == 0


def edges_kernel(d, grid_ref, a_ref, b_ref, ends_ref, low, high, sems):
    rows, cols, _ = grid_ref.shape
    _, _, face_even, tile_even = parities()
    start = jnp.where(tile_even, 0, rows - d)
    copies = [
        pltpu.make_async_copy(grid_ref.at[:, pl.ds(0, 8), :], low, sems.at[0]),
        pltpu.make_async_copy(grid_ref.at[:, pl.ds(cols - 8, 8), :], high, sems.at[1]),
        pltpu.make_async_copy(grid_ref.at[pl.ds(start, d)], a_ref.at[pl.ds(d, d)], sems.at[2]),
        pltpu.make_async_copy(grid_ref.at[pl.ds(start, d)], b_ref.at[pl.ds(d, d)], sems.at[3]),
        pltpu.make_async_copy(grid_ref.at[pl.ds(0, d)], ends_ref.at[0], sems.at[4]),
        pltpu.make_async_copy(grid_ref.at[pl.ds(rows - d, d)], ends_ref.at[1], sems.at[5]),
    ]
    for copy in copies:
        copy.start()
    for copy in copies:
        copy.wait()
    per = cols // d
    group = 8 // d

    def plane(p, carry):
        for r in range(0, per, group):
            at = [p * per + r + k for k in range(group)]
            west = jnp.concatenate([low[i].astype(F32)[:d] for i in at], axis=0)
            east = jnp.concatenate([high[i].astype(F32)[8 - d :] for i in at], axis=0)
            a_ref[p, r * d : r * d + 8, :] = jnp.where(face_even, east, west).astype(BF16)
            b_ref[p, r * d : r * d + 8, :] = jnp.where(face_even, west, east).astype(BF16)
        return carry

    lax.fori_loop(0, d, plane, 0)


def edges(grid, d):
    rows, cols, ch = grid.shape
    side = VMEM((2 * d, cols, ch), BF16)
    return pl.pallas_call(
        functools.partial(edges_kernel, d),
        out_shape=(side, side, VMEM((2, d, cols, ch), BF16)),
        in_specs=[full_spec(pl.ANY)],
        out_specs=(full_spec(),) * 3,
        scratch_shapes=[
            VMEM((rows, 8, ch), BF16),
            VMEM((rows, 8, ch), BF16),
            pltpu.SemaphoreType.DMA((6,)),
        ],
        cost_estimate=pl.CostEstimate(flops=1_000_000, bytes_accessed=800_000, transcendentals=0),
        compiler_params=room(8),
        name="edges",
    )(far(grid))


def widen_kernel(d, ends_ref, ra_ref, rb_ref, wa_ref, wb_ref):
    cols = ends_ref.shape[2]
    rows = cols
    _, _, face_even, tile_even = parities()
    per = cols // d
    for r in range(d):
        wide = []
        for i, row in enumerate((r, rows - d + r)):
            at = (row % per) * d
            tile_at = at // 8 * 8
            a = ra_ref[row // per, tile_at : tile_at + 8, :].astype(F32)[at - tile_at : at - tile_at + d]
            b = rb_ref[row // per, tile_at : tile_at + 8, :].astype(F32)[at - tile_at : at - tile_at + d]
            wide.append(
                jnp.concatenate(
                    [
                        jnp.where(face_even, b, a),
                        ends_ref[i, r].astype(F32),
                        jnp.where(face_even, a, b),
                    ],
                    axis=0,
                )
            )
        wa_ref[r] = jnp.where(tile_even, wide[1], wide[0]).astype(BF16)
        wb_ref[r] = jnp.where(tile_even, wide[0], wide[1]).astype(BF16)


def widen(ends, received, d):
    _, _, cols, ch = ends.shape
    wide = VMEM((d, cols + 2 * d, ch), BF16)
    return pl.pallas_call(
        functools.partial(widen_kernel, d),
        out_shape=(wide, wide),
        in_specs=[full_spec()] * 3,
        out_specs=(full_spec(), full_spec()),
        cost_estimate=pl.CostEstimate(flops=1_000_000, bytes_accessed=800_000, transcendentals=0),
        compiler_params=room(8),
        name="widen",
    )(keep(ends), *[keep(x) for x in received])


def face_partner(f, nface, odd_up):
    return (f + 1) % nface if (f % 2 == 1) == odd_up else (f - 1) % nface


def swap_faces(sides):
    nface = lax.axis_size("face")
    inner = [(f, face_partner(f, nface, False)) for f in range(nface)]
    outer = [(f, face_partner(f, nface, True)) for f in range(nface)]
    return lax.ppermute(sides[0], "face", inner), lax.ppermute(sides[1], "face", outer)


def swap_tiles(wide):
    nface = lax.axis_size("face")
    ntile = lax.axis_size("tile")
    inner = [(t, t ^ 1) for t in range(ntile)]
    outer = []
    for f in range(nface):
        for t in range(ntile):
            if t in (0, ntile - 1):
                to = ((f + 2) % nface) * ntile + t
            else:
                to = f * ntile + (t + 1 if t % 2 == 1 else t - 1)
            outer.append((f * ntile + t, to))
    return lax.ppermute(wide[0], "tile", inner), lax.ppermute(wide[1], ("face", "tile"), outer)


def gelu(x):
    half = 0.5 * x
    inner = x * (0.7978845608028654 + (0.7978845608028654 * 0.044715) * (x * x))
    return half + half * jnp.tanh(inner)


def pair_weights_kernel(taps_ref, weights):
    ch = taps_ref.shape[1]
    for a in range(4):
        for e in range(3):
            at = (a * 3 + e) * ch
            if a < 3:
                weights[at : at + ch, :ch] = taps_ref[a * 3 + e]
            else:
                weights[at : at + ch, :ch] = jnp.zeros((ch, ch), BF16)
            if a > 0:
                weights[at : at + ch, ch:] = taps_ref[(a - 1) * 3 + e]
            else:
                weights[at : at + ch, ch:] = jnp.zeros((ch, ch), BF16)


def pair_weights(taps):
    ch = taps.shape[1]
    return pl.pallas_call(
        pair_weights_kernel,
        out_shape=VMEM((12 * ch, 2 * ch), BF16),
        in_specs=[full_spec()],
        out_specs=full_spec(),
        cost_estimate=pl.CostEstimate(flops=1_000_000, bytes_accessed=1_000_000, transcendentals=0),
        compiler_params=room(4),
        name="pair_weights",
    )(taps)


EDGE = 8


def shifted_copies(strip_row, west, east, d):
    cols = strip_row.shape[0]
    ch = strip_row.shape[1] // 3
    v = strip_row[:, ch : 2 * ch]
    strip_row[d:, :ch] = v[: cols - d]
    strip_row[:d, :ch] = west
    strip_row[: cols - d, 2 * ch :] = v[d:]
    strip_row[cols - d :, 2 * ch :] = east


def side_tile(ra_ref, rb_ref, p, at, face_even):
    a = ra_ref[p, at, :].astype(F32)
    b = rb_ref[p, at, :].astype(F32)
    west = jnp.where(face_even, b, a).astype(BF16)
    east = jnp.where(face_even, a, b).astype(BF16)
    return west, east


def pair_rows(strip, bases, d):
    _, cols, wide = strip.shape
    parts = []
    for a in range(4):
        of_a = [strip[pl.ds(base + a * d, d)].reshape(d * cols, wide) for base in bases]
        parts.append(jnp.concatenate(of_a, axis=0))
    return jnp.concatenate(parts, axis=1)


def rows_kernel(d, step_rows, has_residual, grid_ref, ra_ref, rb_ref, weights, bias_ref, *rest):
    if has_residual:
        fields_ref, out_ref, strip, acc, result, sems, out_sems, fields = rest
    else:
        out_ref, strip, acc, result, sems, out_sems = rest
    rows, cols, ch = grid_ref.shape
    _, _, face_even, _ = parities()
    inner = rows - 2 * EDGE
    first = EDGE - 4
    load = pltpu.make_async_copy(
        grid_ref.at[pl.ds(first, inner + 8)], strip.at[:, :, pl.ds(ch, ch)], sems.at[0]
    )
    load.start()
    if has_residual:
        load_fields = pltpu.make_async_copy(
            fields_ref.at[pl.ds(EDGE, inner)], fields, sems.at[1]
        )
        load_fields.start()
    load.wait()
    group = 8 // d
    per_plane = cols // 8

    def build(t, carry):
        p = lax.div(t, per_plane)
        at = pl.multiple_of((t - p * per_plane) * 8, 8)
        west, east = side_tile(ra_ref, rb_ref, p, pl.ds(at, 8), face_even)
        for k in range(group):
            shifted_copies(
                strip.at[t * group + k - first],
                west[k * d : (k + 1) * d],
                east[k * d : (k + 1) * d],
                d,
            )
        return carry

    lax.fori_loop(first // group, (first + inner + 8) // group, build, 0, unroll=2)
    if has_residual:
        load_fields.wait()

    bias = bias_ref[...]
    bias2 = jnp.concatenate([bias, bias], axis=1)
    m = d * cols
    groups = step_rows // (2 * d)
    blocks = inner // step_rows

    def product(i):
        base = i * step_rows + 4 - d
        lhs = pair_rows(strip, [base + g * 2 * d for g in range(groups)], d)
        return jnp.dot(lhs, weights[...], preferred_element_type=F32)

    def send(i):
        return pltpu.make_async_copy(
            result.at[pl.ds(i * step_rows, step_rows)],
            out_ref.at[pl.ds(EDGE + i * step_rows, step_rows)],
            out_sems.at[i],
        )

    def finish(i):
        y = gelu(acc[...] + bias2)
        for g in range(groups):
            for half in range(2):
                at = i * step_rows + g * 2 * d + half * d
                piece = y[g * m : (g + 1) * m, half * ch : (half + 1) * ch].reshape(d, cols, ch)
                if has_residual:
                    piece = piece + fields[pl.ds(at, d)].astype(F32)
                result[pl.ds(at, d)] = piece.astype(result.dtype)

    acc[...] = product(0)

    def block(i, carry):
        finish(i - 1)
        acc[...] = product(i)
        send(i - 1).start()
        return carry

    lax.fori_loop(1, blocks, block, 0)
    finish(blocks - 1)
    send(blocks - 1).start()
    for i in range(blocks):
        send(i).wait()


def conv_rows(grid, sides, weights, bias, d, fields, out_dtype):
    rows, cols, ch = grid.shape
    step_rows = 16
    inner = rows - 2 * EDGE
    operands = [far(grid) if fields is None else keep(grid), *[keep(x) for x in sides]]
    operands += [keep(weights), bias.reshape(1, ch)]
    in_specs = [full_spec(pl.ANY)] + [full_spec()] * 4
    scratch = [
        VMEM((inner + 8, cols, 3 * ch), BF16),
        VMEM((step_rows // 2 * cols, 2 * ch), F32),
        VMEM((inner, cols, ch), out_dtype),
        pltpu.SemaphoreType.DMA((2,)),
        pltpu.SemaphoreType.DMA((inner // step_rows,)),
    ]
    if fields is not None:
        operands.append(far(fields))
        in_specs.append(full_spec(pl.ANY))
        scratch.append(VMEM((inner, cols, ch), BF16))
    return pl.pallas_call(
        functools.partial(rows_kernel, d, step_rows, fields is not None),
        out_shape=pltpu.HBM((rows, cols, ch), out_dtype),
        in_specs=in_specs,
        out_specs=full_spec(pl.ANY),
        scratch_shapes=scratch,
        cost_estimate=pl.CostEstimate(
            flops=2 * 12 * rows * cols * ch * ch, bytes_accessed=9_000_000, transcendentals=0
        ),
        compiler_params=room(28),
        name="conv_rows",
    )(*operands)


def core_kernel(d, step_rows, grid_ref, weights, bias_ref, fields_ref, out_ref, strip, acc, result, sems, out_sems, fields):
    rows, cols, ch = grid_ref.shape
    inner = rows - 2 * EDGE
    width = cols - 2 * EDGE
    low = EDGE - d
    load = pltpu.make_async_copy(
        grid_ref.at[pl.ds(low, inner + 2 * d), pl.ds(EDGE, width), :],
        strip.at[:, :, pl.ds(ch, ch)],
        sems.at[0],
    )
    load.start()
    load_fields = pltpu.make_async_copy(
        fields_ref.at[pl.ds(EDGE, inner), pl.ds(EDGE, width), :], fields, sems.at[1]
    )
    load_fields.start()

    def build(p, carry):
        v = grid_ref[p + low]
        strip[p, :, :ch] = v[EDGE - d : EDGE - d + width]
        strip[p, :, 2 * ch :] = v[EDGE + d : EDGE + d + width]
        return carry

    lax.fori_loop(0, inner + 2 * d, build, 0, unroll=4)
    load.wait()
    load_fields.wait()
    bias = bias_ref[...]
    bias2 = jnp.concatenate([bias, bias], axis=1)
    m = d * width
    groups = step_rows // (2 * d)
    blocks = inner // step_rows

    def product(i):
        lhs = pair_rows(strip, [i * step_rows + g * 2 * d for g in range(groups)], d)
        return jnp.dot(lhs, weights[...], preferred_element_type=F32)

    def send(i):
        return pltpu.make_async_copy(
            result.at[pl.ds(i * step_rows, step_rows)],
            out_ref.at[pl.ds(EDGE + i * step_rows, step_rows), pl.ds(EDGE, width), :],
            out_sems.at[i],
        )

    def finish(i):
        y = gelu(acc[...] + bias2)
        for g in range(groups):
            for half in range(2):
                at = i * step_rows + g * 2 * d + half * d
                piece = y[g * m : (g + 1) * m, half * ch : (half + 1) * ch].reshape(d, width, ch)
                piece = piece + fields[pl.ds(at, d)].astype(F32)
                result[pl.ds(at, d)] = piece.astype(result.dtype)

    acc[...] = product(0)

    def block(i, carry):
        finish(i - 1)
        acc[...] = product(i)
        send(i - 1).start()
        return carry

    lax.fori_loop(1, blocks, block, 0)
    finish(blocks - 1)
    send(blocks - 1).start()
    for i in range(blocks):
        send(i).wait()


def conv_core(grid, weights, bias, d, fields):
    rows, cols, ch = grid.shape
    step_rows = 16
    inner = rows - 2 * EDGE
    width = cols - 2 * EDGE
    return pl.pallas_call(
        functools.partial(core_kernel, d, step_rows),
        out_shape=pltpu.HBM(grid.shape, BF16),
        in_specs=[full_spec(), full_spec(), full_spec(), full_spec(pl.ANY)],
        out_specs=full_spec(pl.ANY),
        scratch_shapes=[
            VMEM((inner + 2 * d, width, 3 * ch), BF16),
            VMEM((step_rows // 2 * width, 2 * ch), F32),
            VMEM((inner, width, ch), BF16),
            pltpu.SemaphoreType.DMA((2,)),
            pltpu.SemaphoreType.DMA((inner // step_rows,)),
            VMEM((inner, width, ch), BF16),
        ],
        cost_estimate=pl.CostEstimate(
            flops=2 * 12 * inner * width * ch * ch, bytes_accessed=4_000_000, transcendentals=0
        ),
        compiler_params=room(20),
        name="conv_core",
    )(keep(grid), keep(weights), bias.reshape(1, ch), far(fields))


def columns_kernel(d, grid_ref, ra_ref, rb_ref, weights, bias_ref, fields_ref, _, out_ref, strip, result, sems, fields):
    rows, cols, ch = grid_ref.shape
    _, _, face_even, _ = parities()
    inner = rows - 2 * EDGE
    low = EDGE - d
    ends = ((0, 0), (1, cols - EDGE))
    loads = [
        pltpu.make_async_copy(
            fields_ref.at[pl.ds(EDGE, inner), pl.ds(at, EDGE), :],
            fields.at[:, pl.ds(side * EDGE, EDGE), :],
            sems.at[side],
        )
        for side, at in ends
    ]
    for load in loads:
        load.start()
    group = 8 // d
    per_plane = cols // 8

    def build(t, carry):
        p = lax.div(t, per_plane)
        at = pl.ds(pl.multiple_of((t - p * per_plane) * 8, 8), 8)
        a = ra_ref[p, at, :].astype(F32)
        b = rb_ref[p, at, :].astype(F32)
        west = jnp.where(face_even, b, a)
        east = jnp.where(face_even, a, b)
        for k in range(group):
            row = t * group + k
            left = grid_ref[row, :16, :].astype(F32)
            right = grid_ref[row, cols - 16 :, :].astype(F32)
            first = [west[k * d : (k + 1) * d], left[: 8 - d], right[8 - d : 16 - d]]
            middle = [left[:8], right[8:]]
            last = [left[d : 8 + d], right[8 + d :], east[k * d : (k + 1) * d]]
            for e, parts in enumerate((first, middle, last)):
                strip[row - low, :, e * ch : (e + 1) * ch] = jnp.concatenate(parts, axis=0).astype(BF16)
        return carry

    lax.fori_loop(low // group, (low + inner + 2 * d) // group, build, 0, unroll=2)
    bias = bias_ref[...]
    bias2 = jnp.concatenate([bias, bias], axis=1)
    m = d * 2 * EDGE
    groups = inner // (2 * d)
    lhs = pair_rows(strip, [g * 2 * d for g in range(groups)], d)
    y = gelu(jnp.dot(lhs, weights[...], preferred_element_type=F32) + bias2)
    for load in loads:
        load.wait()
    for g in range(groups):
        for half in range(2):
            at = g * 2 * d + half * d
            piece = y[g * m : (g + 1) * m, half * ch : (half + 1) * ch].reshape(d, 2 * EDGE, ch)
            result[at : at + d] = (piece + fields[at : at + d].astype(F32)).astype(BF16)
    stores = [
        pltpu.make_async_copy(
            result.at[:, pl.ds(side * EDGE, EDGE), :],
            out_ref.at[pl.ds(EDGE, inner), pl.ds(at, EDGE), :],
            sems.at[2 + side],
        )
        for side, at in ends
    ]
    for store in stores:
        store.start()
    for store in stores:
        store.wait()


def conv_columns(out, grid, sides, weights, bias, d, fields):
    rows, _, ch = grid.shape
    inner = rows - 2 * EDGE
    return pl.pallas_call(
        functools.partial(columns_kernel, d),
        out_shape=pltpu.HBM(out.shape, out.dtype),
        in_specs=[full_spec()] * 5 + [full_spec(pl.ANY)] * 2,
        out_specs=full_spec(pl.ANY),
        scratch_shapes=[
            VMEM((inner + 2 * d, 2 * EDGE, 3 * ch), BF16),
            VMEM((inner, 2 * EDGE, ch), BF16),
            pltpu.SemaphoreType.DMA((4,)),
            VMEM((inner, 2 * EDGE, ch), BF16),
        ],
        input_output_aliases={6: 0},
        cost_estimate=pl.CostEstimate(
            flops=4 * 12 * inner * EDGE * ch * ch, bytes_accessed=2_000_000, transcendentals=0
        ),
        compiler_params=room(16),
        name="conv_columns",
    )(
        keep(grid), *[keep(x) for x in sides], keep(weights), bias.reshape(1, ch), far(fields), far(out)
    )


def ends_kernel(
    d,
    has_residual,
    neighbor_ref,
    reversal_ref,
    grid_ref,
    ra_ref,
    rb_ref,
    wa_ref,
    wb_ref,
    weights,
    bias_ref,
    *rest,
):
    if has_residual:
        fields_ref, _, out_ref, strip, wide, result, sems, fields = rest
    else:
        _, out_ref, strip, wide, result, sems = rest
    rows, cols, ch = grid_ref.shape
    face, tile, face_even, tile_even = parities()
    nface = lax.axis_size("face")
    last_tile = lax.axis_size("tile") - 1
    span = EDGE + 2 * d
    own = EDGE + d
    loads = []
    for side, at, to in ((0, 0, d), (1, rows - own, span)):
        loads.append(
            pltpu.make_async_copy(
                grid_ref.at[pl.ds(at, own)],
                strip.at[pl.ds(to, own), :, pl.ds(ch, ch)],
                sems.at[side],
            )
        )
        loads[-1].start()
    if has_residual:
        for side, at in ((0, 0), (1, rows - EDGE)):
            loads.append(
                pltpu.make_async_copy(
                    fields_ref.at[pl.ds(at, EDGE)],
                    fields.at[pl.ds(side * EDGE, EDGE)],
                    sems.at[2 + side],
                )
            )
            loads[-1].start()
    for r in range(d):
        a = wa_ref[r].astype(F32)
        b = wb_ref[r].astype(F32)
        wide[0, r] = jnp.where(tile_even, b, a).astype(BF16)
        wide[1, r] = jnp.where(tile_even, a, b).astype(BF16)
    for load in loads:
        load.wait()

    @pl.when((tile == 0) | (tile == last_tile))
    def _():
        which = jnp.where(tile == 0, 0, 1)
        sector = neighbor_ref[which, face]
        flip = reversal_ref[which, face]
        mine = jnp.where(tile == 0, d, span + EDGE)
        width = cols + 2 * d

        def source_index(s):
            s = lax.rem(s + nface, nface)
            inner = jnp.where(face_even, face + 1, face - 1)
            outer = lax.rem(jnp.where(face_even, face - 1, face + 1) + nface, nface)
            return jnp.where(s == face, 0, jnp.where(s == inner, 1, jnp.where(s == outer, 2, 3)))

        place = iota((width, 1), 0)
        place = jnp.where(flip == 1, width - 1 - place, place)
        column = place - d + cols
        step = jnp.where(column >= 2 * cols, 2, jnp.where(column >= cols, 1, 0))
        inside = column - step * cols
        index = jnp.where(
            step == 0,
            source_index(sector - 1),
            jnp.where(step == 1, source_index(sector), source_index(sector + 1)),
        )
        wanted = index * cols + inside
        pick = jnp.where(iota((width, nface * cols), 1) == wanted, 1.0, 0.0).astype(BF16)
        for r in range(d):
            source = jnp.concatenate(
                [
                    strip[mine + r, :, ch : 2 * ch],
                    ra_ref[d + r],
                    rb_ref[d + r],
                    wb_ref[r, d : d + cols, :],
                ],
                axis=0,
            )
            wide[which, d - 1 - r] = jnp.dot(pick, source, preferred_element_type=F32).astype(BF16)

    for side, at in ((0, 0), (1, span + own)):
        for r in range(d):
            for e in range(3):
                strip[at + r, :, e * ch : (e + 1) * ch] = wide[side, r, e * d : e * d + cols, :]

    group = 8 // d
    per_plane = cols // 8
    for low, high, to in ((0, own, d), (rows - own, rows, span)):
        for t in range(low // group, -(-high // group)):
            p, at = divmod(t, per_plane)
            west, east = side_tile(ra_ref, rb_ref, p, slice(at * 8, at * 8 + 8), face_even)
            for k in range(group):
                row = t * group + k
                if low <= row < high:
                    shifted_copies(
                        strip.at[row - low + to],
                        west[k * d : (k + 1) * d],
                        east[k * d : (k + 1) * d],
                        d,
                    )

    bias = bias_ref[...]
    bias2 = jnp.concatenate([bias, bias], axis=1)
    m = d * cols
    starts = [(side, g * 2 * d) for side in range(2) for g in range(EDGE // (2 * d))]
    lhs = pair_rows(strip, [side * span + at for side, at in starts], d)
    y = gelu(jnp.dot(lhs, weights[...], preferred_element_type=F32) + bias2)
    for g, (side, at) in enumerate(starts):
        for half in range(2):
            to = side * EDGE + at + half * d
            piece = y[g * m : (g + 1) * m, half * ch : (half + 1) * ch].reshape(d, cols, ch)
            if has_residual:
                piece = piece + fields[to : to + d].astype(F32)
            result[to : to + d] = piece.astype(result.dtype)
    stores = [
        pltpu.make_async_copy(
            result.at[pl.ds(side * EDGE, EDGE)], out_ref.at[pl.ds(at, EDGE)], sems.at[4 + side]
        )
        for side, at in ((0, 0), (1, rows - EDGE))
    ]
    for store in stores:
        store.start()
    for store in stores:
        store.wait()


def conv_ends(out, grid, sides, wide, neighbor, reversal, weights, bias, d, fields):
    _, cols, ch = grid.shape
    operands = [neighbor.T, reversal.T, far(grid) if fields is None else keep(grid)]
    operands += [keep(x) for x in (*sides, *wide, weights)] + [bias.reshape(1, ch)]
    smem = full_spec(pltpu.SMEM)
    in_specs = [smem, smem, full_spec(pl.ANY)] + [full_spec()] * 6
    scratch = [
        VMEM((2 * (EDGE + 2 * d), cols, 3 * ch), BF16),
        VMEM((2, d, cols + 2 * d, ch), BF16),
        VMEM((2 * EDGE, cols, ch), out.dtype),
        pltpu.SemaphoreType.DMA((6,)),
    ]
    if fields is not None:
        operands.append(far(fields))
        in_specs.append(full_spec(pl.ANY))
        scratch.append(VMEM((2 * EDGE, cols, ch), BF16))
    operands.append(far(out))
    in_specs.append(full_spec(pl.ANY))
    return pl.pallas_call(
        functools.partial(ends_kernel, d, fields is not None),
        out_shape=pltpu.HBM(out.shape, out.dtype),
        in_specs=in_specs,
        out_specs=full_spec(pl.ANY),
        scratch_shapes=scratch,
        input_output_aliases={len(operands) - 1: 0},
        cost_estimate=pl.CostEstimate(
            flops=4 * 12 * EDGE * cols * ch * ch, bytes_accessed=1_000_000, transcendentals=0
        ),
        compiler_params=room(16),
        name="conv_ends",
    )(*operands)


def scatter_kernel(
    d,
    recv,
    weight_ref,
    first_ref,
    mixed,
    a_ref,
    b_ref,
    ends_ref,
    first,
    even,
    extra,
    enc,
    cells_v,
    cells_s,
    sems,
):
    load = pltpu.make_async_copy(first_ref, first, sems.at[0])
    load.start()
    side, _, ch = mixed.shape
    sources = recv.shape[0]
    _, _, face_even, tile_even = parities()
    for g in range(sources // 8):
        meta = jnp.sum(recv[g * 8 : (g + 1) * 8, CAP:, :].astype(F32), axis=0)
        cells_v[g : g + 1, :] = (meta[0:1, :] * side + meta[1:2, :]).astype(I32)
    copy = pltpu.make_async_copy(cells_v, cells_s, sems.at[1])
    copy.start()
    for g in range(sources // 8):
        rows = recv[g * 8 : (g + 1) * 8, :CAP, :].reshape(8 * CAP, recv.shape[2])
        enc[g * 128 : (g + 1) * 128, :] = jnp.dot(
            rows, weight_ref[...], preferred_element_type=F32
        )

    def clear(r, carry):
        even[pl.ds(r * side, side), :] = jnp.zeros((side, ch), F32)
        extra[pl.ds(r * side, side), :] = jnp.zeros((side, ch), F32)
        return carry

    lax.fori_loop(0, side, clear, 0, unroll=4)
    copy.wait()

    def add_rows(g, carry):
        for j in range(0, 128, 2):
            for k, target in ((0, even), (1, extra)):
                c = cells_s[g, j + k]
                target[pl.ds(c, 1), :] += enc[pl.ds(g * 128 + j + k, 1), :]
        return carry

    lax.fori_loop(0, sources // 8, add_rows, 0)
    load.wait()

    per = side // d
    group = 8 // d

    def plane(p, carry):
        def rows_of(i, inner):
            west = []
            east = []
            for k in range(group):
                row = p * per + i * group + k
                at = pl.ds(pl.multiple_of(row * side, side), side)
                v = first[row] + even[at, :] + extra[at, :]
                mixed[row] = v.astype(BF16)
                west.append(v[:d])
                east.append(v[side - d :])
            west = jnp.concatenate(west, axis=0)
            east = jnp.concatenate(east, axis=0)
            at = pl.ds(pl.multiple_of(i * 8, 8), 8)
            a_ref[p, at, :] = jnp.where(face_even, east, west).astype(BF16)
            b_ref[p, at, :] = jnp.where(face_even, west, east).astype(BF16)
            return inner

        lax.fori_loop(0, per // group, rows_of, 0, unroll=2)
        return carry

    lax.fori_loop(0, d, plane, 0)
    start = jnp.where(tile_even, 0, side - d)
    for r in range(d):
        row = mixed[start + r]
        a_ref[d + r] = row
        b_ref[d + r] = row
        ends_ref[0, r] = mixed[r]
        ends_ref[1, r] = mixed[side - d + r]


def scatter(recv, weight, first, d):
    side, cols, ch = first.shape
    sources = recv.shape[0]
    out = VMEM((2 * d, cols, ch), BF16)
    return pl.pallas_call(
        functools.partial(scatter_kernel, d),
        out_shape=(VMEM((side, cols, ch), BF16), out, out, VMEM((2, d, cols, ch), BF16)),
        in_specs=[full_spec(), full_spec(), full_spec(pl.ANY)],
        out_specs=(full_spec(),) * 4,
        scratch_shapes=[
            VMEM(first.shape, F32),
            VMEM((side * cols, ch), F32),
            VMEM((side * cols, ch), F32),
            VMEM((sources * CAP, ch), F32),
            VMEM((sources // 8, 128), I32),
            pltpu.SMEM((sources // 8, 128), I32),
            pltpu.SemaphoreType.DMA((2,)),
        ],
        cost_estimate=pl.CostEstimate(
            flops=200_000_000, bytes_accessed=12_000_000, transcendentals=0
        ),
        compiler_params=room(28),
        name="scatter",
    )(keep(recv), weight, far(first))


def local(
    fields,
    first_kernel_taps,
    first_conv_bias,
    second_kernel_taps,
    second_conv_bias,
    obs_weight,
    obs_values,
    obs_owner,
    obs_cells,
    polar_neighbor_sector,
    polar_link_reversal,
):
    side = fields.shape[0]
    dests = lax.axis_size("face") * lax.axis_size("tile")
    d = FIRST_DILATION
    weights = pair_weights(first_kernel_taps)
    a, b, ends = edges(fields, d)
    sides = swap_faces((a, b))
    send = pack(obs_owner, obs_cells, obs_values, dests, side)
    recv = lax.all_to_all(send, ("face", "tile"), split_axis=0, concat_axis=0, tiled=True)
    wide = swap_tiles(widen(ends, sides, d))
    first = conv_rows(fields, sides, weights, first_conv_bias, d, None, F32)
    first = conv_ends(
        first, fields, sides, wide, polar_neighbor_sector, polar_link_reversal,
        weights, first_conv_bias, d, None,
    )
    d = SECOND_DILATION
    weights = pair_weights(second_kernel_taps)
    mixed, a, b, ends = scatter(recv, obs_weight, first, d)
    sides = swap_faces((a, b))
    out = conv_core(mixed, weights, second_conv_bias, d, fields)
    wide = swap_tiles(widen(ends, sides, d))
    out = conv_columns(out, mixed, sides, weights, second_conv_bias, d, fields)
    return conv_ends(
        out, mixed, sides, wide, polar_neighbor_sector, polar_link_reversal,
        weights, second_conv_bias, d, fields,
    )


def solution(mesh):
    in_specs = (
        P("tile", "face", None),
        P(),
        P(),
        P(),
        P(),
        P(),
        P(("face", "tile"), None),
        P(("face", "tile"), None),
        P(("face", "tile")),
        P(),
        P(),
    )
    out_specs = P("tile", "face", None)
    return jax.shard_map(local, mesh=mesh, in_specs=in_specs, out_specs=out_specs, check_vma=False)
```

```python
import functools

import jax
import jax.numpy as jnp
from jax import lax
from jax.experimental import pallas as pl
from jax.experimental.pallas import tpu as pltpu
from jax.sharding import PartitionSpec as P

FIRST_DILATION = 2
SECOND_DILATION = 4
CAP = 16
META = 8

BF16 = jnp.bfloat16
F32 = jnp.float32
I32 = jnp.int32
VMEM = pltpu.VMEM


def full_spec(memory_space=None):
    return pl.BlockSpec(memory_space=VMEM if memory_space is None else memory_space)


def room(mebibytes):
    return pltpu.CompilerParams(vmem_limit_bytes=mebibytes << 20)


def far(x):
    return pltpu.with_memory_space_constraint(x, pltpu.HBM)


def keep(x):
    return pltpu.with_memory_space_constraint(x, VMEM)


def iota(shape, axis):
    return lax.broadcasted_iota(I32, shape, axis)


def pack_kernel(dests, side, owner_ref, cell_ref, vals_ref, send_ref):
    rows = vals_ref.shape[0]
    owner = owner_ref[...]
    cell = cell_ref[...]
    block = 256
    earlier = (iota((block, block), 0) < iota((block, block), 1)).astype(F32).astype(BF16)
    onehot_parts = []
    rank_parts = []
    carry = jnp.zeros((dests, 1), F32)
    for b in range(rows // block):
        hit = owner[:, b * block : (b + 1) * block] == iota((dests, block), 0)
        hit_f = jnp.where(hit, 1.0, 0.0)
        hit_b = hit_f.astype(BF16)
        before = jnp.dot(hit_b, earlier, preferred_element_type=F32) + carry
        rank_parts.append(jnp.sum(before * hit_f, axis=0, keepdims=True))
        carry = carry + jnp.sum(hit_f, axis=1, keepdims=True)
        onehot_parts.append(hit_b)
    rank = jnp.concatenate(rank_parts, axis=1).astype(I32)
    onehot = jnp.concatenate(onehot_parts, axis=1)

    cell_row = ((cell.astype(F32) + 0.5) * (1.0 / side)).astype(I32)
    cell_col = cell - cell_row * side
    me = lax.axis_index("face") * lax.axis_size("tile") + lax.axis_index("tile")
    base_lane = lax.rem(me, 8) * CAP
    slot_hit = iota((128, rows), 0) == rank + base_lane
    row_map = jnp.where(slot_hit, cell_row.astype(F32), 0.0).astype(BF16)
    col_map = jnp.where(slot_hit, cell_col.astype(F32), 0.0).astype(BF16)
    contract = (((1,), (1,)), ((), ()))
    meta_row = lax.dot_general(onehot, row_map, contract, preferred_element_type=F32)
    meta_col = lax.dot_general(onehot, col_map, contract, preferred_element_type=F32)
    meta = jnp.where(
        iota((dests, META, 128), 1) == 0,
        jnp.broadcast_to(meta_row[:, None, :], (dests, META, 128)),
        jnp.broadcast_to(meta_col[:, None, :], (dests, META, 128)),
    )
    send_ref[:, CAP:, :] = meta.astype(BF16)

    chunk_dests = 16
    at_rank = jnp.where(iota((CAP, rows), 0) == rank, 1.0, 0.0).astype(BF16)
    for c in range(dests // chunk_dests):
        match = jnp.concatenate(
            [
                jnp.broadcast_to(onehot[t : t + 1, :], (CAP, rows)) * at_rank
                for t in range(c * chunk_dests, (c + 1) * chunk_dests)
            ],
            axis=0,
        )
        placed = jnp.dot(match, vals_ref[...], preferred_element_type=F32).astype(BF16)
        send_ref[c * chunk_dests : (c + 1) * chunk_dests, :CAP, :] = placed.reshape(
            chunk_dests, CAP, placed.shape[-1]
        )


def pack(owner, cells, vals, dests, side):
    rows, features = vals.shape
    return pl.pallas_call(
        functools.partial(pack_kernel, dests, side),
        out_shape=jax.ShapeDtypeStruct((dests, CAP + META, features), BF16),
        in_specs=[full_spec()] * 3,
        out_specs=full_spec(),
        cost_estimate=pl.CostEstimate(
            flops=2 * dests * CAP * rows * features, bytes_accessed=2_000_000, transcendentals=0
        ),
        compiler_params=room(16),
        name="pack",
    )(owner.reshape(1, rows), cells.reshape(1, rows), vals)


def parities():
    face = lax.axis_index("face")
    tile = lax.axis_index("tile")
    return face, tile, lax.rem(face, 2) == 0, lax.rem(tile, 2) == 0


def edges_kernel(d, grid_ref, a_ref, b_ref, ends_ref, low, high, sems):
    rows, cols, _ = grid_ref.shape
    _, _, face_even, tile_even = parities()
    start = jnp.where(tile_even, 0, rows - d)
    copies = [
        pltpu.make_async_copy(grid_ref.at[:, pl.ds(0, 8), :], low, sems.at[0]),
        pltpu.make_async_copy(grid_ref.at[:, pl.ds(cols - 8, 8), :], high, sems.at[1]),
        pltpu.make_async_copy(grid_ref.at[pl.ds(start, d)], a_ref.at[pl.ds(d, d)], sems.at[2]),
        pltpu.make_async_copy(grid_ref.at[pl.ds(start, d)], b_ref.at[pl.ds(d, d)], sems.at[3]),
        pltpu.make_async_copy(grid_ref.at[pl.ds(0, d)], ends_ref.at[0], sems.at[4]),
        pltpu.make_async_copy(grid_ref.at[pl.ds(rows - d, d)], ends_ref.at[1], sems.at[5]),
    ]
    for copy in copies:
        copy.start()
    for copy in copies:
        copy.wait()
    per = cols // d
    group = 8 // d

    def plane(p, carry):
        for r in range(0, per, group):
            at = [p * per + r + k for k in range(group)]
            west = jnp.concatenate([low[i].astype(F32)[:d] for i in at], axis=0)
            east = jnp.concatenate([high[i].astype(F32)[8 - d :] for i in at], axis=0)
            a_ref[p, r * d : r * d + 8, :] = jnp.where(face_even, east, west).astype(BF16)
            b_ref[p, r * d : r * d + 8, :] = jnp.where(face_even, west, east).astype(BF16)
        return carry

    lax.fori_loop(0, d, plane, 0)


def edges(grid, d):
    rows, cols, ch = grid.shape
    side = VMEM((2 * d, cols, ch), BF16)
    return pl.pallas_call(
        functools.partial(edges_kernel, d),
        out_shape=(side, side, VMEM((2, d, cols, ch), BF16)),
        in_specs=[full_spec(pl.ANY)],
        out_specs=(full_spec(),) * 3,
        scratch_shapes=[
            VMEM((rows, 8, ch), BF16),
            VMEM((rows, 8, ch), BF16),
            pltpu.SemaphoreType.DMA((6,)),
        ],
        cost_estimate=pl.CostEstimate(flops=1_000_000, bytes_accessed=800_000, transcendentals=0),
        compiler_params=room(8),
        name="edges",
    )(far(grid))


def widen_kernel(d, ends_ref, ra_ref, rb_ref, wa_ref, wb_ref):
    cols = ends_ref.shape[2]
    rows = cols
    _, _, face_even, tile_even = parities()
    per = cols // d
    for r in range(d):
        wide = []
        for i, row in enumerate((r, rows - d + r)):
            at = (row % per) * d
            tile_at = at // 8 * 8
            a = ra_ref[row // per, tile_at : tile_at + 8, :].astype(F32)[at - tile_at : at - tile_at + d]
            b = rb_ref[row // per, tile_at : tile_at + 8, :].astype(F32)[at - tile_at : at - tile_at + d]
            wide.append(
                jnp.concatenate(
                    [
                        jnp.where(face_even, b, a),
                        ends_ref[i, r].astype(F32),
                        jnp.where(face_even, a, b),
                    ],
                    axis=0,
                )
            )
        wa_ref[r] = jnp.where(tile_even, wide[1], wide[0]).astype(BF16)
        wb_ref[r] = jnp.where(tile_even, wide[0], wide[1]).astype(BF16)


def widen(ends, received, d):
    _, _, cols, ch = ends.shape
    wide = VMEM((d, cols + 2 * d, ch), BF16)
    return pl.pallas_call(
        functools.partial(widen_kernel, d),
        out_shape=(wide, wide),
        in_specs=[full_spec()] * 3,
        out_specs=(full_spec(), full_spec()),
        cost_estimate=pl.CostEstimate(flops=1_000_000, bytes_accessed=800_000, transcendentals=0),
        compiler_params=room(8),
        name="widen",
    )(keep(ends), *[keep(x) for x in received])


def face_partner(f, nface, odd_up):
    return (f + 1) % nface if (f % 2 == 1) == odd_up else (f - 1) % nface


def swap_faces(sides):
    nface = lax.axis_size("face")
    inner = [(f, face_partner(f, nface, False)) for f in range(nface)]
    outer = [(f, face_partner(f, nface, True)) for f in range(nface)]
    return lax.ppermute(sides[0], "face", inner), lax.ppermute(sides[1], "face", outer)


def swap_tiles(wide):
    nface = lax.axis_size("face")
    ntile = lax.axis_size("tile")
    inner = [(t, t ^ 1) for t in range(ntile)]
    outer = []
    for f in range(nface):
        for t in range(ntile):
            if t in (0, ntile - 1):
                to = ((f + 2) % nface) * ntile + t
            else:
                to = f * ntile + (t + 1 if t % 2 == 1 else t - 1)
            outer.append((f * ntile + t, to))
    return lax.ppermute(wide[0], "tile", inner), lax.ppermute(wide[1], ("face", "tile"), outer)


def gelu(x):
    half = 0.5 * x
    inner = x * (0.7978845608028654 + (0.7978845608028654 * 0.044715) * (x * x))
    return half + half * jnp.tanh(inner)


def pair_weights_kernel(taps_ref, weights):
    ch = taps_ref.shape[1]
    for a in range(4):
        for e in range(3):
            at = (a * 3 + e) * ch
            if a < 3:
                weights[at : at + ch, :ch] = taps_ref[a * 3 + e]
            else:
                weights[at : at + ch, :ch] = jnp.zeros((ch, ch), BF16)
            if a > 0:
                weights[at : at + ch, ch:] = taps_ref[(a - 1) * 3 + e]
            else:
                weights[at : at + ch, ch:] = jnp.zeros((ch, ch), BF16)


def pair_weights(taps):
    ch = taps.shape[1]
    return pl.pallas_call(
        pair_weights_kernel,
        out_shape=VMEM((12 * ch, 2 * ch), BF16),
        in_specs=[full_spec()],
        out_specs=full_spec(),
        cost_estimate=pl.CostEstimate(flops=1_000_000, bytes_accessed=1_000_000, transcendentals=0),
        compiler_params=room(4),
        name="pair_weights",
    )(taps)


EDGE = 8


def shifted_copies(strip_row, west, east, d):
    cols = strip_row.shape[0]
    ch = strip_row.shape[1] // 3
    v = strip_row[:, ch : 2 * ch]
    strip_row[d:, :ch] = v[: cols - d]
    strip_row[:d, :ch] = west
    strip_row[: cols - d, 2 * ch :] = v[d:]
    strip_row[cols - d :, 2 * ch :] = east


def side_tile(ra_ref, rb_ref, p, at, face_even):
    a = ra_ref[p, at, :].astype(F32)
    b = rb_ref[p, at, :].astype(F32)
    west = jnp.where(face_even, b, a).astype(BF16)
    east = jnp.where(face_even, a, b).astype(BF16)
    return west, east


def pair_rows(strip, bases, d):
    _, cols, wide = strip.shape
    parts = []
    for a in range(4):
        of_a = [strip[pl.ds(base + a * d, d)].reshape(d * cols, wide) for base in bases]
        parts.append(jnp.concatenate(of_a, axis=0))
    return jnp.concatenate(parts, axis=1)


def rows_kernel(d, step_rows, has_residual, grid_ref, ra_ref, rb_ref, weights, bias_ref, *rest):
    if has_residual:
        fields_ref, out_ref, strip, acc, result, sems, out_sems, fields = rest
    else:
        out_ref, strip, acc, result, sems, out_sems = rest
    rows, cols, ch = grid_ref.shape
    _, _, face_even, _ = parities()
    inner = rows - 2 * EDGE
    first = EDGE - 4
    load = pltpu.make_async_copy(
        grid_ref.at[pl.ds(first, inner + 8)], strip.at[:, :, pl.ds(ch, ch)], sems.at[0]
    )
    load.start()
    if has_residual:
        load_fields = pltpu.make_async_copy(
            fields_ref.at[pl.ds(EDGE, inner)], fields, sems.at[1]
        )
        load_fields.start()
    load.wait()
    group = 8 // d
    per_plane = cols // 8

    def build(t, carry):
        p = lax.div(t, per_plane)
        at = pl.multiple_of((t - p * per_plane) * 8, 8)
        west, east = side_tile(ra_ref, rb_ref, p, pl.ds(at, 8), face_even)
        for k in range(group):
            shifted_copies(
                strip.at[t * group + k - first],
                west[k * d : (k + 1) * d],
                east[k * d : (k + 1) * d],
                d,
            )
        return carry

    lax.fori_loop(first // group, (first + inner + 8) // group, build, 0, unroll=2)
    if has_residual:
        load_fields.wait()

    bias = bias_ref[...]
    bias2 = jnp.concatenate([bias, bias], axis=1)
    m = d * cols
    groups = step_rows // (2 * d)
    blocks = inner // step_rows

    def product(i):
        base = i * step_rows + 4 - d
        lhs = pair_rows(strip, [base + g * 2 * d for g in range(groups)], d)
        return jnp.dot(lhs, weights[...], preferred_element_type=F32)

    def send(i):
        return pltpu.make_async_copy(
            result.at[pl.ds(i * step_rows, step_rows)],
            out_ref.at[pl.ds(EDGE + i * step_rows, step_rows)],
            out_sems.at[i],
        )

    def finish(i):
        y = gelu(acc[...] + bias2)
        for g in range(groups):
            for half in range(2):
                at = i * step_rows + g * 2 * d + half * d
                piece = y[g * m : (g + 1) * m, half * ch : (half + 1) * ch].reshape(d, cols, ch)
                if has_residual:
                    piece = piece + fields[pl.ds(at, d)].astype(F32)
                result[pl.ds(at, d)] = piece.astype(result.dtype)

    acc[...] = product(0)

    def block(i, carry):
        finish(i - 1)
        acc[...] = product(i)
        send(i - 1).start()
        return carry

    lax.fori_loop(1, blocks, block, 0)
    finish(blocks - 1)
    send(blocks - 1).start()
    for i in range(blocks):
        send(i).wait()


def conv_rows(grid, sides, weights, bias, d, fields, out_dtype):
    rows, cols, ch = grid.shape
    step_rows = 16
    inner = rows - 2 * EDGE
    operands = [far(grid) if fields is None else keep(grid), *[keep(x) for x in sides]]
    operands += [keep(weights), bias.reshape(1, ch)]
    in_specs = [full_spec(pl.ANY)] + [full_spec()] * 4
    scratch = [
        VMEM((inner + 8, cols, 3 * ch), BF16),
        VMEM((step_rows // 2 * cols, 2 * ch), F32),
        VMEM((inner, cols, ch), out_dtype),
        pltpu.SemaphoreType.DMA((2,)),
        pltpu.SemaphoreType.DMA((inner // step_rows,)),
    ]
    if fields is not None:
        operands.append(far(fields))
        in_specs.append(full_spec(pl.ANY))
        scratch.append(VMEM((inner, cols, ch), BF16))
    return pl.pallas_call(
        functools.partial(rows_kernel, d, step_rows, fields is not None),
        out_shape=pltpu.HBM((rows, cols, ch), out_dtype),
        in_specs=in_specs,
        out_specs=full_spec(pl.ANY),
        scratch_shapes=scratch,
        cost_estimate=pl.CostEstimate(
            flops=2 * 12 * rows * cols * ch * ch, bytes_accessed=9_000_000, transcendentals=0
        ),
        compiler_params=room(28),
        name="conv_rows",
    )(*operands)


def core_kernel(d, step_rows, grid_ref, weights, bias_ref, fields_ref, out_ref, strip, acc, result, sems, out_sems, fields):
    rows, cols, ch = grid_ref.shape
    inner = rows - 2 * EDGE
    width = cols - 2 * EDGE
    low = EDGE - d
    load = pltpu.make_async_copy(
        grid_ref.at[pl.ds(low, inner + 2 * d), pl.ds(EDGE, width), :],
        strip.at[:, :, pl.ds(ch, ch)],
        sems.at[0],
    )
    load.start()
    load_fields = pltpu.make_async_copy(
        fields_ref.at[pl.ds(EDGE, inner), pl.ds(EDGE, width), :], fields, sems.at[1]
    )
    load_fields.start()

    def build(p, carry):
        v = grid_ref[p + low]
        strip[p, :, :ch] = v[EDGE - d : EDGE - d + width]
        strip[p, :, 2 * ch :] = v[EDGE + d : EDGE + d + width]
        return carry

    lax.fori_loop(0, inner + 2 * d, build, 0, unroll=4)
    load.wait()
    load_fields.wait()
    bias = bias_ref[...]
    bias2 = jnp.concatenate([bias, bias], axis=1)
    m = d * width
    groups = step_rows // (2 * d)
    blocks = inner // step_rows

    def product(i):
        lhs = pair_rows(strip, [i * step_rows + g * 2 * d for g in range(groups)], d)
        return jnp.dot(lhs, weights[...], preferred_element_type=F32)

    def send(i):
        return pltpu.make_async_copy(
            result.at[pl.ds(i * step_rows, step_rows)],
            out_ref.at[pl.ds(EDGE + i * step_rows, step_rows), pl.ds(EDGE, width), :],
            out_sems.at[i],
        )

    def finish(i):
        y = gelu(acc[...] + bias2)
        for g in range(groups):
            for half in range(2):
                at = i * step_rows + g * 2 * d + half * d
                piece = y[g * m : (g + 1) * m, half * ch : (half + 1) * ch].reshape(d, width, ch)
                piece = piece + fields[pl.ds(at, d)].astype(F32)
                result[pl.ds(at, d)] = piece.astype(result.dtype)

    acc[...] = product(0)

    def block(i, carry):
        finish(i - 1)
        acc[...] = product(i)
        send(i - 1).start()
        return carry

    lax.fori_loop(1, blocks, block, 0)
    finish(blocks - 1)
    send(blocks - 1).start()
    for i in range(blocks):
        send(i).wait()


def conv_core(grid, weights, bias, d, fields):
    rows, cols, ch = grid.shape
    step_rows = 16
    inner = rows - 2 * EDGE
    width = cols - 2 * EDGE
    return pl.pallas_call(
        functools.partial(core_kernel, d, step_rows),
        out_shape=pltpu.HBM(grid.shape, BF16),
        in_specs=[full_spec(), full_spec(), full_spec(), full_spec(pl.ANY)],
        out_specs=full_spec(pl.ANY),
        scratch_shapes=[
            VMEM((inner + 2 * d, width, 3 * ch), BF16),
            VMEM((step_rows // 2 * width, 2 * ch), F32),
            VMEM((inner, width, ch), BF16),
            pltpu.SemaphoreType.DMA((2,)),
            pltpu.SemaphoreType.DMA((inner // step_rows,)),
            VMEM((inner, width, ch), BF16),
        ],
        cost_estimate=pl.CostEstimate(
            flops=2 * 12 * inner * width * ch * ch, bytes_accessed=4_000_000, transcendentals=0
        ),
        compiler_params=room(20),
        name="conv_core",
    )(keep(grid), keep(weights), bias.reshape(1, ch), far(fields))


def columns_kernel(d, grid_ref, ra_ref, rb_ref, weights, bias_ref, fields_ref, _, out_ref, strip, result, sems, fields):
    rows, cols, ch = grid_ref.shape
    _, _, face_even, _ = parities()
    inner = rows - 2 * EDGE
    low = EDGE - d
    ends = ((0, 0), (1, cols - EDGE))
    loads = [
        pltpu.make_async_copy(
            fields_ref.at[pl.ds(EDGE, inner), pl.ds(at, EDGE), :],
            fields.at[:, pl.ds(side * EDGE, EDGE), :],
            sems.at[side],
        )
        for side, at in ends
    ]
    for load in loads:
        load.start()
    group = 8 // d
    per_plane = cols // 8

    def build(t, carry):
        p = lax.div(t, per_plane)
        at = pl.ds(pl.multiple_of((t - p * per_plane) * 8, 8), 8)
        a = ra_ref[p, at, :].astype(F32)
        b = rb_ref[p, at, :].astype(F32)
        west = jnp.where(face_even, b, a)
        east = jnp.where(face_even, a, b)
        for k in range(group):
            row = t * group + k
            left = grid_ref[row, :16, :].astype(F32)
            right = grid_ref[row, cols - 16 :, :].astype(F32)
            first = [west[k * d : (k + 1) * d], left[: 8 - d], right[8 - d : 16 - d]]
            middle = [left[:8], right[8:]]
            last = [left[d : 8 + d], right[8 + d :], east[k * d : (k + 1) * d]]
            for e, parts in enumerate((first, middle, last)):
                strip[row - low, :, e * ch : (e + 1) * ch] = jnp.concatenate(parts, axis=0).astype(BF16)
        return carry

    lax.fori_loop(low // group, (low + inner + 2 * d) // group, build, 0, unroll=2)
    bias = bias_ref[...]
    bias2 = jnp.concatenate([bias, bias], axis=1)
    m = d * 2 * EDGE
    groups = inner // (2 * d)
    lhs = pair_rows(strip, [g * 2 * d for g in range(groups)], d)
    y = gelu(jnp.dot(lhs, weights[...], preferred_element_type=F32) + bias2)
    for load in loads:
        load.wait()
    for g in range(groups):
        for half in range(2):
            at = g * 2 * d + half * d
            piece = y[g * m : (g + 1) * m, half * ch : (half + 1) * ch].reshape(d, 2 * EDGE, ch)
            result[at : at + d] = (piece + fields[at : at + d].astype(F32)).astype(BF16)
    stores = [
        pltpu.make_async_copy(
            result.at[:, pl.ds(side * EDGE, EDGE), :],
            out_ref.at[pl.ds(EDGE, inner), pl.ds(at, EDGE), :],
            sems.at[2 + side],
        )
        for side, at in ends
    ]
    for store in stores:
        store.start()
    for store in stores:
        store.wait()


def conv_columns(out, grid, sides, weights, bias, d, fields):
    rows, _, ch = grid.shape
    inner = rows - 2 * EDGE
    return pl.pallas_call(
        functools.partial(columns_kernel, d),
        out_shape=pltpu.HBM(out.shape, out.dtype),
        in_specs=[full_spec()] * 5 + [full_spec(pl.ANY)] * 2,
        out_specs=full_spec(pl.ANY),
        scratch_shapes=[
            VMEM((inner + 2 * d, 2 * EDGE, 3 * ch), BF16),
            VMEM((inner, 2 * EDGE, ch), BF16),
            pltpu.SemaphoreType.DMA((4,)),
            VMEM((inner, 2 * EDGE, ch), BF16),
        ],
        input_output_aliases={6: 0},
        cost_estimate=pl.CostEstimate(
            flops=4 * 12 * inner * EDGE * ch * ch, bytes_accessed=2_000_000, transcendentals=0
        ),
        compiler_params=room(16),
        name="conv_columns",
    )(
        keep(grid), *[keep(x) for x in sides], keep(weights), bias.reshape(1, ch), far(fields), far(out)
    )


def ends_kernel(
    d,
    has_residual,
    neighbor_ref,
    reversal_ref,
    grid_ref,
    ra_ref,
    rb_ref,
    wa_ref,
    wb_ref,
    weights,
    bias_ref,
    *rest,
):
    if has_residual:
        fields_ref, _, out_ref, strip, wide, result, sems, fields = rest
    else:
        _, out_ref, strip, wide, result, sems = rest
    rows, cols, ch = grid_ref.shape
    face, tile, face_even, tile_even = parities()
    nface = lax.axis_size("face")
    last_tile = lax.axis_size("tile") - 1
    span = EDGE + 2 * d
    own = EDGE + d
    loads = []
    for side, at, to in ((0, 0, d), (1, rows - own, span)):
        loads.append(
            pltpu.make_async_copy(
                grid_ref.at[pl.ds(at, own)],
                strip.at[pl.ds(to, own), :, pl.ds(ch, ch)],
                sems.at[side],
            )
        )
        loads[-1].start()
    if has_residual:
        for side, at in ((0, 0), (1, rows - EDGE)):
            loads.append(
                pltpu.make_async_copy(
                    fields_ref.at[pl.ds(at, EDGE)],
                    fields.at[pl.ds(side * EDGE, EDGE)],
                    sems.at[2 + side],
                )
            )
            loads[-1].start()
    for r in range(d):
        a = wa_ref[r].astype(F32)
        b = wb_ref[r].astype(F32)
        wide[0, r] = jnp.where(tile_even, b, a).astype(BF16)
        wide[1, r] = jnp.where(tile_even, a, b).astype(BF16)
    for load in loads:
        load.wait()

    @pl.when((tile == 0) | (tile == last_tile))
    def _():
        which = jnp.where(tile == 0, 0, 1)
        sector = neighbor_ref[which, face]
        flip = reversal_ref[which, face]
        mine = jnp.where(tile == 0, d, span + EDGE)
        width = cols + 2 * d

        def source_index(s):
            s = lax.rem(s + nface, nface)
            inner = jnp.where(face_even, face + 1, face - 1)
            outer = lax.rem(jnp.where(face_even, face - 1, face + 1) + nface, nface)
            return jnp.where(s == face, 0, jnp.where(s == inner, 1, jnp.where(s == outer, 2, 3)))

        place = iota((width, 1), 0)
        place = jnp.where(flip == 1, width - 1 - place, place)
        column = place - d + cols
        step = jnp.where(column >= 2 * cols, 2, jnp.where(column >= cols, 1, 0))
        inside = column - step * cols
        index = jnp.where(
            step == 0,
            source_index(sector - 1),
            jnp.where(step == 1, source_index(sector), source_index(sector + 1)),
        )
        wanted = index * cols + inside
        pick = jnp.where(iota((width, nface * cols), 1) == wanted, 1.0, 0.0).astype(BF16)
        for r in range(d):
            source = jnp.concatenate(
                [
                    strip[mine + r, :, ch : 2 * ch],
                    ra_ref[d + r],
                    rb_ref[d + r],
                    wb_ref[r, d : d + cols, :],
                ],
                axis=0,
            )
            wide[which, d - 1 - r] = jnp.dot(pick, source, preferred_element_type=F32).astype(BF16)

    for side, at in ((0, 0), (1, span + own)):
        for r in range(d):
            for e in range(3):
                strip[at + r, :, e * ch : (e + 1) * ch] = wide[side, r, e * d : e * d + cols, :]

    group = 8 // d
    per_plane = cols // 8
    for low, high, to in ((0, own, d), (rows - own, rows, span)):
        for t in range(low // group, -(-high // group)):
            p, at = divmod(t, per_plane)
            west, east = side_tile(ra_ref, rb_ref, p, slice(at * 8, at * 8 + 8), face_even)
            for k in range(group):
                row = t * group + k
                if low <= row < high:
                    shifted_copies(
                        strip.at[row - low + to],
                        west[k * d : (k + 1) * d],
                        east[k * d : (k + 1) * d],
                        d,
                    )

    bias = bias_ref[...]
    bias2 = jnp.concatenate([bias, bias], axis=1)
    m = d * cols
    starts = [(side, g * 2 * d) for side in range(2) for g in range(EDGE // (2 * d))]
    lhs = pair_rows(strip, [side * span + at for side, at in starts], d)
    y = gelu(jnp.dot(lhs, weights[...], preferred_element_type=F32) + bias2)
    stores = []
    for g, (side, at) in enumerate(starts):
        for half in range(2):
            to = side * EDGE + at + half * d
            piece = y[g * m : (g + 1) * m, half * ch : (half + 1) * ch].reshape(d, cols, ch)
            if has_residual:
                piece = piece + fields[to : to + d].astype(F32)
            result[to : to + d] = piece.astype(result.dtype)
        if at + 2 * d == EDGE:
            stores.append(
                pltpu.make_async_copy(
                    result.at[pl.ds(side * EDGE, EDGE)],
                    out_ref.at[pl.ds(side * (rows - EDGE), EDGE)],
                    sems.at[4 + side],
                )
            )
            stores[-1].start()
    for store in stores:
        store.wait()


def conv_ends(out, grid, sides, wide, neighbor, reversal, weights, bias, d, fields):
    _, cols, ch = grid.shape
    operands = [neighbor.T, reversal.T, far(grid) if fields is None else keep(grid)]
    operands += [keep(x) for x in (*sides, *wide, weights)] + [bias.reshape(1, ch)]
    smem = full_spec(pltpu.SMEM)
    in_specs = [smem, smem, full_spec(pl.ANY)] + [full_spec()] * 6
    scratch = [
        VMEM((2 * (EDGE + 2 * d), cols, 3 * ch), BF16),
        VMEM((2, d, cols + 2 * d, ch), BF16),
        VMEM((2 * EDGE, cols, ch), out.dtype),
        pltpu.SemaphoreType.DMA((6,)),
    ]
    if fields is not None:
        operands.append(far(fields))
        in_specs.append(full_spec(pl.ANY))
        scratch.append(VMEM((2 * EDGE, cols, ch), BF16))
    operands.append(far(out))
    in_specs.append(full_spec(pl.ANY))
    return pl.pallas_call(
        functools.partial(ends_kernel, d, fields is not None),
        out_shape=pltpu.HBM(out.shape, out.dtype),
        in_specs=in_specs,
        out_specs=full_spec(pl.ANY),
        scratch_shapes=scratch,
        input_output_aliases={len(operands) - 1: 0},
        cost_estimate=pl.CostEstimate(
            flops=4 * 12 * EDGE * cols * ch * ch, bytes_accessed=1_000_000, transcendentals=0
        ),
        compiler_params=room(16),
        name="conv_ends",
    )(*operands)


def scatter_kernel(
    d,
    recv,
    weight_ref,
    first_ref,
    mixed,
    a_ref,
    b_ref,
    ends_ref,
    first,
    even,
    extra,
    enc,
    cells_v,
    cells_s,
    sems,
):
    load = pltpu.make_async_copy(first_ref, first, sems.at[0])
    load.start()
    side, _, ch = mixed.shape
    sources = recv.shape[0]
    _, _, face_even, tile_even = parities()
    for g in range(sources // 8):
        meta = jnp.sum(recv[g * 8 : (g + 1) * 8, CAP:, :].astype(F32), axis=0)
        cells_v[g : g + 1, :] = (meta[0:1, :] * side + meta[1:2, :]).astype(I32)
    copy = pltpu.make_async_copy(cells_v, cells_s, sems.at[1])
    copy.start()
    for g in range(sources // 8):
        rows = recv[g * 8 : (g + 1) * 8, :CAP, :].reshape(8 * CAP, recv.shape[2])
        enc[g * 128 : (g + 1) * 128, :] = jnp.dot(
            rows, weight_ref[...], preferred_element_type=F32
        )

    def clear(r, carry):
        even[pl.ds(r * side, side), :] = jnp.zeros((side, ch), F32)
        extra[pl.ds(r * side, side), :] = jnp.zeros((side, ch), F32)
        return carry

    lax.fori_loop(0, side, clear, 0, unroll=4)
    copy.wait()

    for g in range(sources // 8):
        for j in range(0, 128, 2):
            for k, target in ((0, even), (1, extra)):
                c = cells_s[g, j + k]
                target[pl.ds(c, 1), :] += enc[pl.ds(g * 128 + j + k, 1), :]
    load.wait()

    per = side // d
    group = 8 // d

    def plane(p, carry):
        def rows_of(i, inner):
            west = []
            east = []
            for k in range(group):
                row = p * per + i * group + k
                at = pl.ds(pl.multiple_of(row * side, side), side)
                v = first[row] + even[at, :] + extra[at, :]
                mixed[row] = v.astype(BF16)
                west.append(v[:d])
                east.append(v[side - d :])
            west = jnp.concatenate(west, axis=0)
            east = jnp.concatenate(east, axis=0)
            at = pl.ds(pl.multiple_of(i * 8, 8), 8)
            a_ref[p, at, :] = jnp.where(face_even, east, west).astype(BF16)
            b_ref[p, at, :] = jnp.where(face_even, west, east).astype(BF16)
            return inner

        lax.fori_loop(0, per // group, rows_of, 0, unroll=2)
        return carry

    lax.fori_loop(0, d, plane, 0)
    start = jnp.where(tile_even, 0, side - d)
    for r in range(d):
        row = mixed[start + r]
        a_ref[d + r] = row
        b_ref[d + r] = row
        ends_ref[0, r] = mixed[r]
        ends_ref[1, r] = mixed[side - d + r]


def scatter(recv, weight, first, d):
    side, cols, ch = first.shape
    sources = recv.shape[0]
    out = VMEM((2 * d, cols, ch), BF16)
    return pl.pallas_call(
        functools.partial(scatter_kernel, d),
        out_shape=(VMEM((side, cols, ch), BF16), out, out, VMEM((2, d, cols, ch), BF16)),
        in_specs=[full_spec(), full_spec(), full_spec(pl.ANY)],
        out_specs=(full_spec(),) * 4,
        scratch_shapes=[
            VMEM(first.shape, F32),
            VMEM((side * cols, ch), F32),
            VMEM((side * cols, ch), F32),
            VMEM((sources * CAP, ch), F32),
            VMEM((sources // 8, 128), I32),
            pltpu.SMEM((sources // 8, 128), I32),
            pltpu.SemaphoreType.DMA((2,)),
        ],
        cost_estimate=pl.CostEstimate(
            flops=200_000_000, bytes_accessed=12_000_000, transcendentals=0
        ),
        compiler_params=room(28),
        name="scatter",
    )(keep(recv), weight, far(first))


def local(
    fields,
    first_kernel_taps,
    first_conv_bias,
    second_kernel_taps,
    second_conv_bias,
    obs_weight,
    obs_values,
    obs_owner,
    obs_cells,
    polar_neighbor_sector,
    polar_link_reversal,
):
    side = fields.shape[0]
    dests = lax.axis_size("face") * lax.axis_size("tile")
    d = FIRST_DILATION
    weights = pair_weights(first_kernel_taps)
    a, b, ends = edges(fields, d)
    sides = swap_faces((a, b))
    send = pack(obs_owner, obs_cells, obs_values, dests, side)
    recv = lax.all_to_all(send, ("face", "tile"), split_axis=0, concat_axis=0, tiled=True)
    wide = swap_tiles(widen(ends, sides, d))
    first = conv_rows(fields, sides, weights, first_conv_bias, d, None, F32)
    first = conv_ends(
        first, fields, sides, wide, polar_neighbor_sector, polar_link_reversal,
        weights, first_conv_bias, d, None,
    )
    d = SECOND_DILATION
    weights = pair_weights(second_kernel_taps)
    mixed, a, b, ends = scatter(recv, obs_weight, first, d)
    sides = swap_faces((a, b))
    out = conv_core(mixed, weights, second_conv_bias, d, fields)
    wide = swap_tiles(widen(ends, sides, d))
    out = conv_columns(out, mixed, sides, weights, second_conv_bias, d, fields)
    return conv_ends(
        out, mixed, sides, wide, polar_neighbor_sector, polar_link_reversal,
        weights, second_conv_bias, d, fields,
    )


def solution(mesh):
    in_specs = (
        P("tile", "face", None),
        P(),
        P(),
        P(),
        P(),
        P(),
        P(("face", "tile"), None),
        P(("face", "tile"), None),
        P(("face", "tile")),
        P(),
        P(),
    )
    out_specs = P("tile", "face", None)
    return jax.shard_map(local, mesh=mesh, in_specs=in_specs, out_specs=out_specs, check_vma=False)
```

```python
import functools

import jax
import jax.numpy as jnp
from jax import lax
from jax.experimental import pallas as pl
from jax.experimental.pallas import tpu as pltpu
from jax.sharding import PartitionSpec as P

FIRST_DILATION = 2
SECOND_DILATION = 4
CAP = 16
META = 8

BF16 = jnp.bfloat16
F32 = jnp.float32
I32 = jnp.int32
VMEM = pltpu.VMEM


def full_spec(memory_space=None):
    return pl.BlockSpec(memory_space=VMEM if memory_space is None else memory_space)


def room(mebibytes):
    return pltpu.CompilerParams(vmem_limit_bytes=mebibytes << 20)


def far(x):
    return pltpu.with_memory_space_constraint(x, pltpu.HBM)


def keep(x):
    return pltpu.with_memory_space_constraint(x, VMEM)


def iota(shape, axis):
    return lax.broadcasted_iota(I32, shape, axis)


def pack_kernel(dests, side, owner_ref, cell_ref, vals_ref, send_ref):
    rows = vals_ref.shape[0]
    owner = owner_ref[...]
    cell = cell_ref[...]
    block = 256
    earlier = (iota((block, block), 0) < iota((block, block), 1)).astype(F32).astype(BF16)
    onehot_parts = []
    rank_parts = []
    carry = jnp.zeros((dests, 1), F32)
    for b in range(rows // block):
        hit = owner[:, b * block : (b + 1) * block] == iota((dests, block), 0)
        hit_f = jnp.where(hit, 1.0, 0.0)
        hit_b = hit_f.astype(BF16)
        before = jnp.dot(hit_b, earlier, preferred_element_type=F32) + carry
        rank_parts.append(jnp.sum(before * hit_f, axis=0, keepdims=True))
        carry = carry + jnp.sum(hit_f, axis=1, keepdims=True)
        onehot_parts.append(hit_b)
    rank = jnp.concatenate(rank_parts, axis=1).astype(I32)
    onehot = jnp.concatenate(onehot_parts, axis=1)

    cell_row = ((cell.astype(F32) + 0.5) * (1.0 / side)).astype(I32)
    cell_col = cell - cell_row * side
    me = lax.axis_index("face") * lax.axis_size("tile") + lax.axis_index("tile")
    base_lane = lax.rem(me, 8) * CAP
    slot_hit = iota((128, rows), 0) == rank + base_lane
    row_map = jnp.where(slot_hit, cell_row.astype(F32), 0.0).astype(BF16)
    col_map = jnp.where(slot_hit, cell_col.astype(F32), 0.0).astype(BF16)
    contract = (((1,), (1,)), ((), ()))
    meta_row = lax.dot_general(onehot, row_map, contract, preferred_element_type=F32)
    meta_col = lax.dot_general(onehot, col_map, contract, preferred_element_type=F32)
    meta = jnp.where(
        iota((dests, META, 128), 1) == 0,
        jnp.broadcast_to(meta_row[:, None, :], (dests, META, 128)),
        jnp.broadcast_to(meta_col[:, None, :], (dests, META, 128)),
    )
    send_ref[:, CAP:, :] = meta.astype(BF16)

    chunk_dests = 16
    at_rank = jnp.where(iota((CAP, rows), 0) == rank, 1.0, 0.0).astype(BF16)
    for c in range(dests // chunk_dests):
        match = jnp.concatenate(
            [
                jnp.broadcast_to(onehot[t : t + 1, :], (CAP, rows)) * at_rank
                for t in range(c * chunk_dests, (c + 1) * chunk_dests)
            ],
            axis=0,
        )
        placed = jnp.dot(match, vals_ref[...], preferred_element_type=F32).astype(BF16)
        send_ref[c * chunk_dests : (c + 1) * chunk_dests, :CAP, :] = placed.reshape(
            chunk_dests, CAP, placed.shape[-1]
        )


def pack(owner, cells, vals, dests, side):
    rows, features = vals.shape
    return pl.pallas_call(
        functools.partial(pack_kernel, dests, side),
        out_shape=jax.ShapeDtypeStruct((dests, CAP + META, features), BF16),
        in_specs=[full_spec()] * 3,
        out_specs=full_spec(),
        cost_estimate=pl.CostEstimate(
            flops=2 * dests * CAP * rows * features, bytes_accessed=2_000_000, transcendentals=0
        ),
        compiler_params=room(16),
        name="pack",
    )(owner.reshape(1, rows), cells.reshape(1, rows), vals)


def parities():
    face = lax.axis_index("face")
    tile = lax.axis_index("tile")
    return face, tile, lax.rem(face, 2) == 0, lax.rem(tile, 2) == 0


def edges_kernel(d, grid_ref, a_ref, b_ref, ends_ref, low, high, sems):
    rows, cols, _ = grid_ref.shape
    _, _, face_even, tile_even = parities()
    start = jnp.where(tile_even, 0, rows - d)
    copies = [
        pltpu.make_async_copy(grid_ref.at[:, pl.ds(0, 8), :], low, sems.at[0]),
        pltpu.make_async_copy(grid_ref.at[:, pl.ds(cols - 8, 8), :], high, sems.at[1]),
        pltpu.make_async_copy(grid_ref.at[pl.ds(start, d)], a_ref.at[pl.ds(d, d)], sems.at[2]),
        pltpu.make_async_copy(grid_ref.at[pl.ds(start, d)], b_ref.at[pl.ds(d, d)], sems.at[3]),
        pltpu.make_async_copy(grid_ref.at[pl.ds(0, d)], ends_ref.at[0], sems.at[4]),
        pltpu.make_async_copy(grid_ref.at[pl.ds(rows - d, d)], ends_ref.at[1], sems.at[5]),
    ]
    for copy in copies:
        copy.start()
    for copy in copies:
        copy.wait()
    per = cols // d
    group = 8 // d

    def plane(p, carry):
        for r in range(0, per, group):
            at = [p * per + r + k for k in range(group)]
            west = jnp.concatenate([low[i].astype(F32)[:d] for i in at], axis=0)
            east = jnp.concatenate([high[i].astype(F32)[8 - d :] for i in at], axis=0)
            a_ref[p, r * d : r * d + 8, :] = jnp.where(face_even, east, west).astype(BF16)
            b_ref[p, r * d : r * d + 8, :] = jnp.where(face_even, west, east).astype(BF16)
        return carry

    lax.fori_loop(0, d, plane, 0)


def edges(grid, d):
    rows, cols, ch = grid.shape
    side = VMEM((2 * d, cols, ch), BF16)
    return pl.pallas_call(
        functools.partial(edges_kernel, d),
        out_shape=(side, side, VMEM((2, d, cols, ch), BF16)),
        in_specs=[full_spec(pl.ANY)],
        out_specs=(full_spec(),) * 3,
        scratch_shapes=[
            VMEM((rows, 8, ch), BF16),
            VMEM((rows, 8, ch), BF16),
            pltpu.SemaphoreType.DMA((6,)),
        ],
        cost_estimate=pl.CostEstimate(flops=1_000_000, bytes_accessed=800_000, transcendentals=0),
        compiler_params=room(8),
        name="edges",
    )(far(grid))


def widen_kernel(d, ends_ref, ra_ref, rb_ref, wa_ref, wb_ref):
    cols = ends_ref.shape[2]
    rows = cols
    _, _, face_even, tile_even = parities()
    per = cols // d
    for r in range(d):
        wide = []
        for i, row in enumerate((r, rows - d + r)):
            at = (row % per) * d
            tile_at = at // 8 * 8
            a = ra_ref[row // per, tile_at : tile_at + 8, :].astype(F32)[at - tile_at : at - tile_at + d]
            b = rb_ref[row // per, tile_at : tile_at + 8, :].astype(F32)[at - tile_at : at - tile_at + d]
            wide.append(
                jnp.concatenate(
                    [
                        jnp.where(face_even, b, a),
                        ends_ref[i, r].astype(F32),
                        jnp.where(face_even, a, b),
                    ],
                    axis=0,
                )
            )
        wa_ref[r] = jnp.where(tile_even, wide[1], wide[0]).astype(BF16)
        wb_ref[r] = jnp.where(tile_even, wide[0], wide[1]).astype(BF16)


def widen(ends, received, d):
    _, _, cols, ch = ends.shape
    wide = VMEM((d, cols + 2 * d, ch), BF16)
    return pl.pallas_call(
        functools.partial(widen_kernel, d),
        out_shape=(wide, wide),
        in_specs=[full_spec()] * 3,
        out_specs=(full_spec(), full_spec()),
        cost_estimate=pl.CostEstimate(flops=1_000_000, bytes_accessed=800_000, transcendentals=0),
        compiler_params=room(8),
        name="widen",
    )(keep(ends), *[keep(x) for x in received])


def face_partner(f, nface, odd_up):
    return (f + 1) % nface if (f % 2 == 1) == odd_up else (f - 1) % nface


def swap_faces(sides):
    nface = lax.axis_size("face")
    inner = [(f, face_partner(f, nface, False)) for f in range(nface)]
    outer = [(f, face_partner(f, nface, True)) for f in range(nface)]
    return lax.ppermute(sides[0], "face", inner), lax.ppermute(sides[1], "face", outer)


def swap_tiles(wide):
    nface = lax.axis_size("face")
    ntile = lax.axis_size("tile")
    inner = [(t, t ^ 1) for t in range(ntile)]
    outer = []
    for f in range(nface):
        for t in range(ntile):
            if t in (0, ntile - 1):
                to = ((f + 2) % nface) * ntile + t
            else:
                to = f * ntile + (t + 1 if t % 2 == 1 else t - 1)
            outer.append((f * ntile + t, to))
    return lax.ppermute(wide[0], "tile", inner), lax.ppermute(wide[1], ("face", "tile"), outer)


def gelu(x):
    half = 0.5 * x
    inner = x * (0.7978845608028654 + (0.7978845608028654 * 0.044715) * (x * x))
    return half + half * jnp.tanh(inner)


def pair_weights_kernel(taps_ref, weights):
    ch = taps_ref.shape[1]
    for a in range(4):
        for e in range(3):
            at = (a * 3 + e) * ch
            if a < 3:
                weights[at : at + ch, :ch] = taps_ref[a * 3 + e]
            else:
                weights[at : at + ch, :ch] = jnp.zeros((ch, ch), BF16)
            if a > 0:
                weights[at : at + ch, ch:] = taps_ref[(a - 1) * 3 + e]
            else:
                weights[at : at + ch, ch:] = jnp.zeros((ch, ch), BF16)


def pair_weights(taps):
    ch = taps.shape[1]
    return pl.pallas_call(
        pair_weights_kernel,
        out_shape=VMEM((12 * ch, 2 * ch), BF16),
        in_specs=[full_spec()],
        out_specs=full_spec(),
        cost_estimate=pl.CostEstimate(flops=1_000_000, bytes_accessed=1_000_000, transcendentals=0),
        compiler_params=room(4),
        name="pair_weights",
    )(taps)


EDGE = 8


def shifted_copies(strip_row, west, east, d):
    cols = strip_row.shape[0]
    ch = strip_row.shape[1] // 3
    v = strip_row[:, ch : 2 * ch]
    strip_row[d:, :ch] = v[: cols - d]
    strip_row[:d, :ch] = west
    strip_row[: cols - d, 2 * ch :] = v[d:]
    strip_row[cols - d :, 2 * ch :] = east


def side_tile(ra_ref, rb_ref, p, at, face_even):
    a = ra_ref[p, at, :].astype(F32)
    b = rb_ref[p, at, :].astype(F32)
    west = jnp.where(face_even, b, a).astype(BF16)
    east = jnp.where(face_even, a, b).astype(BF16)
    return west, east


def pair_rows(strip, bases, d):
    _, cols, wide = strip.shape
    parts = []
    for a in range(4):
        of_a = [strip[pl.ds(base + a * d, d)].reshape(d * cols, wide) for base in bases]
        parts.append(jnp.concatenate(of_a, axis=0))
    return jnp.concatenate(parts, axis=1)


def rows_kernel(d, step_rows, has_residual, grid_ref, ra_ref, rb_ref, weights, bias_ref, *rest):
    if has_residual:
        fields_ref, out_ref, strip, acc, result, sems, out_sems, fields = rest
    else:
        out_ref, strip, acc, result, sems, out_sems = rest
    rows, cols, ch = grid_ref.shape
    _, _, face_even, _ = parities()
    inner = rows - 2 * EDGE
    first = EDGE - 4
    load = pltpu.make_async_copy(
        grid_ref.at[pl.ds(first, inner + 8)], strip.at[:, :, pl.ds(ch, ch)], sems.at[0]
    )
    load.start()
    if has_residual:
        load_fields = pltpu.make_async_copy(
            fields_ref.at[pl.ds(EDGE, inner)], fields, sems.at[1]
        )
        load_fields.start()
    load.wait()
    group = 8 // d
    per_plane = cols // 8

    def build(t, carry):
        p = lax.div(t, per_plane)
        at = pl.multiple_of((t - p * per_plane) * 8, 8)
        west, east = side_tile(ra_ref, rb_ref, p, pl.ds(at, 8), face_even)
        for k in range(group):
            shifted_copies(
                strip.at[t * group + k - first],
                west[k * d : (k + 1) * d],
                east[k * d : (k + 1) * d],
                d,
            )
        return carry

    lax.fori_loop(first // group, (first + inner + 8) // group, build, 0, unroll=2)
    if has_residual:
        load_fields.wait()

    bias = bias_ref[...]
    bias2 = jnp.concatenate([bias, bias], axis=1)
    m = d * cols
    groups = step_rows // (2 * d)
    blocks = inner // step_rows

    def product(i):
        base = i * step_rows + 4 - d
        lhs = pair_rows(strip, [base + g * 2 * d for g in range(groups)], d)
        return jnp.dot(lhs, weights[...], preferred_element_type=F32)

    def send(i):
        return pltpu.make_async_copy(
            result.at[pl.ds(i * step_rows, step_rows)],
            out_ref.at[pl.ds(EDGE + i * step_rows, step_rows)],
            out_sems.at[i],
        )

    def finish(i):
        y = gelu(acc[...] + bias2)
        for g in range(groups):
            for half in range(2):
                at = i * step_rows + g * 2 * d + half * d
                piece = y[g * m : (g + 1) * m, half * ch : (half + 1) * ch].reshape(d, cols, ch)
                if has_residual:
                    piece = piece + fields[pl.ds(at, d)].astype(F32)
                result[pl.ds(at, d)] = piece.astype(result.dtype)

    acc[...] = product(0)

    def block(i, carry):
        finish(i - 1)
        acc[...] = product(i)
        send(i - 1).start()
        return carry

    lax.fori_loop(1, blocks, block, 0)
    finish(blocks - 1)
    send(blocks - 1).start()
    for i in range(blocks):
        send(i).wait()


def conv_rows(grid, sides, weights, bias, d, fields, out_dtype):
    rows, cols, ch = grid.shape
    step_rows = 16
    inner = rows - 2 * EDGE
    operands = [far(grid) if fields is None else keep(grid), *[keep(x) for x in sides]]
    operands += [keep(weights), bias.reshape(1, ch)]
    in_specs = [full_spec(pl.ANY)] + [full_spec()] * 4
    scratch = [
        VMEM((inner + 8, cols, 3 * ch), BF16),
        VMEM((step_rows // 2 * cols, 2 * ch), F32),
        VMEM((inner, cols, ch), out_dtype),
        pltpu.SemaphoreType.DMA((2,)),
        pltpu.SemaphoreType.DMA((inner // step_rows,)),
    ]
    if fields is not None:
        operands.append(far(fields))
        in_specs.append(full_spec(pl.ANY))
        scratch.append(VMEM((inner, cols, ch), BF16))
    return pl.pallas_call(
        functools.partial(rows_kernel, d, step_rows, fields is not None),
        out_shape=pltpu.HBM((rows, cols, ch), out_dtype),
        in_specs=in_specs,
        out_specs=full_spec(pl.ANY),
        scratch_shapes=scratch,
        cost_estimate=pl.CostEstimate(
            flops=2 * 12 * rows * cols * ch * ch, bytes_accessed=9_000_000, transcendentals=0
        ),
        compiler_params=room(28),
        name="conv_rows",
    )(*operands)


def core_kernel(d, step_rows, grid_ref, weights, bias_ref, fields_ref, out_ref, strip, acc, result, sems, out_sems, fields):
    rows, cols, ch = grid_ref.shape
    inner = rows - 2 * EDGE
    width = cols - 2 * EDGE
    low = EDGE - d
    load = pltpu.make_async_copy(
        grid_ref.at[pl.ds(low, inner + 2 * d), pl.ds(EDGE, width), :],
        strip.at[:, :, pl.ds(ch, ch)],
        sems.at[0],
    )
    load.start()
    load_fields = pltpu.make_async_copy(
        fields_ref.at[pl.ds(EDGE, inner), pl.ds(EDGE, width), :], fields, sems.at[1]
    )
    load_fields.start()

    def build(p, carry):
        v = grid_ref[p + low]
        strip[p, :, :ch] = v[EDGE - d : EDGE - d + width]
        strip[p, :, 2 * ch :] = v[EDGE + d : EDGE + d + width]
        return carry

    lax.fori_loop(0, inner + 2 * d, build, 0, unroll=4)
    load.wait()
    load_fields.wait()
    bias = bias_ref[...]
    bias2 = jnp.concatenate([bias, bias], axis=1)
    m = d * width
    groups = step_rows // (2 * d)
    blocks = inner // step_rows

    def product(i):
        lhs = pair_rows(strip, [i * step_rows + g * 2 * d for g in range(groups)], d)
        return jnp.dot(lhs, weights[...], preferred_element_type=F32)

    def send(i):
        return pltpu.make_async_copy(
            result.at[pl.ds(i * step_rows, step_rows)],
            out_ref.at[pl.ds(EDGE + i * step_rows, step_rows), pl.ds(EDGE, width), :],
            out_sems.at[i],
        )

    def finish(i):
        y = gelu(acc[...] + bias2)
        for g in range(groups):
            for half in range(2):
                at = i * step_rows + g * 2 * d + half * d
                piece = y[g * m : (g + 1) * m, half * ch : (half + 1) * ch].reshape(d, width, ch)
                piece = piece + fields[pl.ds(at, d)].astype(F32)
                result[pl.ds(at, d)] = piece.astype(result.dtype)

    acc[...] = product(0)

    def block(i, carry):
        finish(i - 1)
        acc[...] = product(i)
        send(i - 1).start()
        return carry

    lax.fori_loop(1, blocks, block, 0)
    finish(blocks - 1)
    send(blocks - 1).start()
    for i in range(blocks):
        send(i).wait()


def conv_core(grid, weights, bias, d, fields):
    rows, cols, ch = grid.shape
    step_rows = 16
    inner = rows - 2 * EDGE
    width = cols - 2 * EDGE
    return pl.pallas_call(
        functools.partial(core_kernel, d, step_rows),
        out_shape=pltpu.HBM(grid.shape, BF16),
        in_specs=[full_spec(), full_spec(), full_spec(), full_spec(pl.ANY)],
        out_specs=full_spec(pl.ANY),
        scratch_shapes=[
            VMEM((inner + 2 * d, width, 3 * ch), BF16),
            VMEM((step_rows // 2 * width, 2 * ch), F32),
            VMEM((inner, width, ch), BF16),
            pltpu.SemaphoreType.DMA((2,)),
            pltpu.SemaphoreType.DMA((inner // step_rows,)),
            VMEM((inner, width, ch), BF16),
        ],
        cost_estimate=pl.CostEstimate(
            flops=2 * 12 * inner * width * ch * ch, bytes_accessed=4_000_000, transcendentals=0
        ),
        compiler_params=room(20),
        name="conv_core",
    )(keep(grid), keep(weights), bias.reshape(1, ch), far(fields))


def columns_kernel(d, grid_ref, ra_ref, rb_ref, weights, bias_ref, fields_ref, _, out_ref, own_ref, strip, result, sems, fields):
    rows, cols, ch = grid_ref.shape
    _, _, face_even, _ = parities()
    inner = rows - 2 * EDGE
    low = EDGE - d
    ends = ((0, 0), (1, cols - EDGE))
    loads = [
        pltpu.make_async_copy(
            fields_ref.at[pl.ds(EDGE, inner), pl.ds(at, EDGE), :],
            fields.at[:, pl.ds(side * EDGE, EDGE), :],
            sems.at[side],
        )
        for side, at in ends
    ]
    for load in loads:
        load.start()
    group = 8 // d
    per_plane = cols // 8

    def build(t, carry):
        p = lax.div(t, per_plane)
        at = pl.ds(pl.multiple_of((t - p * per_plane) * 8, 8), 8)
        a = ra_ref[p, at, :].astype(F32)
        b = rb_ref[p, at, :].astype(F32)
        west = jnp.where(face_even, b, a)
        east = jnp.where(face_even, a, b)
        for k in range(group):
            row = t * group + k
            left = grid_ref[row, :16, :].astype(F32)
            right = grid_ref[row, cols - 16 :, :].astype(F32)
            first = [west[k * d : (k + 1) * d], left[: 8 - d], right[8 - d : 16 - d]]
            middle = [left[:8], right[8:]]
            last = [left[d : 8 + d], right[8 + d :], east[k * d : (k + 1) * d]]
            for e, parts in enumerate((first, middle, last)):
                strip[row - low, :, e * ch : (e + 1) * ch] = jnp.concatenate(parts, axis=0).astype(BF16)
        return carry

    lax.fori_loop(low // group, (low + inner + 2 * d) // group, build, 0, unroll=2)
    bias = bias_ref[...]
    bias2 = jnp.concatenate([bias, bias], axis=1)
    m = d * 2 * EDGE
    groups = inner // (2 * d)
    lhs = pair_rows(strip, [g * 2 * d for g in range(groups)], d)
    y = gelu(jnp.dot(lhs, weights[...], preferred_element_type=F32) + bias2)
    for load in loads:
        load.wait()
    for g in range(groups):
        for half in range(2):
            at = g * 2 * d + half * d
            piece = y[g * m : (g + 1) * m, half * ch : (half + 1) * ch].reshape(d, 2 * EDGE, ch)
            result[at : at + d] = (piece + fields[at : at + d].astype(F32)).astype(BF16)
    stores = [
        pltpu.make_async_copy(
            result.at[:, pl.ds(side * EDGE, EDGE), :],
            out_ref.at[pl.ds(EDGE, inner), pl.ds(at, EDGE), :],
            sems.at[2 + side],
        )
        for side, at in ends
    ]
    for store in stores:
        store.start()
    own = EDGE + d
    for low_row, high_row, to in ((0, own, 0), (rows - own, rows, own)):
        for t in range(low_row // group, high_row // group):
            p, at = divmod(t, per_plane)
            west, east = side_tile(ra_ref, rb_ref, p, slice(at * 8, at * 8 + 8), face_even)
            for k in range(group):
                row = t * group + k
                target = own_ref.at[row - low_row + to]
                target[:, ch : 2 * ch] = grid_ref[row]
                shifted_copies(target, west[k * d : (k + 1) * d], east[k * d : (k + 1) * d], d)
    for store in stores:
        store.wait()


def conv_columns(out, grid, sides, weights, bias, d, fields):
    rows, cols, ch = grid.shape
    inner = rows - 2 * EDGE
    return pl.pallas_call(
        functools.partial(columns_kernel, d),
        out_shape=(
            pltpu.HBM(out.shape, out.dtype),
            VMEM((2 * (EDGE + d), cols, 3 * ch), BF16),
        ),
        in_specs=[full_spec()] * 5 + [full_spec(pl.ANY)] * 2,
        out_specs=(full_spec(pl.ANY), full_spec()),
        scratch_shapes=[
            VMEM((inner + 2 * d, 2 * EDGE, 3 * ch), BF16),
            VMEM((inner, 2 * EDGE, ch), BF16),
            pltpu.SemaphoreType.DMA((4,)),
            VMEM((inner, 2 * EDGE, ch), BF16),
        ],
        input_output_aliases={6: 0},
        cost_estimate=pl.CostEstimate(
            flops=4 * 12 * inner * EDGE * ch * ch, bytes_accessed=2_000_000, transcendentals=0
        ),
        compiler_params=room(16),
        name="conv_columns",
    )(
        keep(grid), *[keep(x) for x in sides], keep(weights), bias.reshape(1, ch), far(fields), far(out)
    )


def ends_kernel(
    d,
    has_residual,
    neighbor_ref,
    reversal_ref,
    grid_ref,
    ra_ref,
    rb_ref,
    wa_ref,
    wb_ref,
    weights,
    bias_ref,
    *rest,
):
    if has_residual:
        fields_ref, own_ref, _, out_ref, strip, wide, result, sems, fields = rest
    else:
        _, out_ref, strip, wide, result, sems = rest
    rows, cols, ch = grid_ref.shape
    face, tile, face_even, tile_even = parities()
    nface = lax.axis_size("face")
    last_tile = lax.axis_size("tile") - 1
    span = EDGE + 2 * d
    own = EDGE + d
    loads = []
    for side, at, to in () if has_residual else ((0, 0, d), (1, rows - own, span)):
        loads.append(
            pltpu.make_async_copy(
                grid_ref.at[pl.ds(at, own)],
                strip.at[pl.ds(to, own), :, pl.ds(ch, ch)],
                sems.at[side],
            )
        )
        loads[-1].start()
    if has_residual:
        for side, at in ((0, 0), (1, rows - EDGE)):
            loads.append(
                pltpu.make_async_copy(
                    fields_ref.at[pl.ds(at, EDGE)],
                    fields.at[pl.ds(side * EDGE, EDGE)],
                    sems.at[2 + side],
                )
            )
            loads[-1].start()
    for r in range(d):
        a = wa_ref[r].astype(F32)
        b = wb_ref[r].astype(F32)
        wide[0, r] = jnp.where(tile_even, b, a).astype(BF16)
        wide[1, r] = jnp.where(tile_even, a, b).astype(BF16)
    for load in loads:
        load.wait()

    @pl.when((tile == 0) | (tile == last_tile))
    def _():
        which = jnp.where(tile == 0, 0, 1)
        sector = neighbor_ref[which, face]
        flip = reversal_ref[which, face]
        if has_residual:
            mine = jnp.where(tile == 0, 0, own + EDGE)
        else:
            mine = jnp.where(tile == 0, d, span + EDGE)
        width = cols + 2 * d

        def source_index(s):
            s = lax.rem(s + nface, nface)
            inner = jnp.where(face_even, face + 1, face - 1)
            outer = lax.rem(jnp.where(face_even, face - 1, face + 1) + nface, nface)
            return jnp.where(s == face, 0, jnp.where(s == inner, 1, jnp.where(s == outer, 2, 3)))

        place = iota((width, 1), 0)
        place = jnp.where(flip == 1, width - 1 - place, place)
        column = place - d + cols
        step = jnp.where(column >= 2 * cols, 2, jnp.where(column >= cols, 1, 0))
        inside = column - step * cols
        index = jnp.where(
            step == 0,
            source_index(sector - 1),
            jnp.where(step == 1, source_index(sector), source_index(sector + 1)),
        )
        wanted = index * cols + inside
        pick = jnp.where(iota((width, nface * cols), 1) == wanted, 1.0, 0.0).astype(BF16)
        for r in range(d):
            source = jnp.concatenate(
                [
                    (own_ref if has_residual else strip)[mine + r, :, ch : 2 * ch],
                    ra_ref[d + r],
                    rb_ref[d + r],
                    wb_ref[r, d : d + cols, :],
                ],
                axis=0,
            )
            wide[which, d - 1 - r] = jnp.dot(pick, source, preferred_element_type=F32).astype(BF16)

    for side, at in ((0, 0), (1, span + own)):
        for r in range(d):
            for e in range(3):
                strip[at + r, :, e * ch : (e + 1) * ch] = wide[side, r, e * d : e * d + cols, :]

    group = 8 // d
    per_plane = cols // 8
    for low, high, to in () if has_residual else ((0, own, d), (rows - own, rows, span)):
        for t in range(low // group, -(-high // group)):
            p, at = divmod(t, per_plane)
            west, east = side_tile(ra_ref, rb_ref, p, slice(at * 8, at * 8 + 8), face_even)
            for k in range(group):
                row = t * group + k
                if low <= row < high:
                    shifted_copies(
                        strip.at[row - low + to],
                        west[k * d : (k + 1) * d],
                        east[k * d : (k + 1) * d],
                        d,
                    )

    bias = bias_ref[...]
    bias2 = jnp.concatenate([bias, bias], axis=1)
    m = d * cols
    starts = [(side, g * 2 * d) for side in range(2) for g in range(EDGE // (2 * d))]
    if has_residual:
        parts = []
        for a in range(4):
            of_a = []
            for side, at in starts:
                at = at + a * d
                inside = d <= at if side == 0 else at < own
                if inside:
                    here = side * own + at - (0 if side else d)
                    slab = own_ref[here : here + d]
                else:
                    slab = strip[side * span + at : side * span + at + d]
                of_a.append(slab.reshape(m, 3 * ch))
            parts.append(jnp.concatenate(of_a, axis=0))
        lhs = jnp.concatenate(parts, axis=1)
    else:
        lhs = pair_rows(strip, [side * span + at for side, at in starts], d)
    y = gelu(jnp.dot(lhs, weights[...], preferred_element_type=F32) + bias2)
    stores = []
    for g, (side, at) in enumerate(starts):
        for half in range(2):
            to = side * EDGE + at + half * d
            piece = y[g * m : (g + 1) * m, half * ch : (half + 1) * ch].reshape(d, cols, ch)
            if has_residual:
                piece = piece + fields[to : to + d].astype(F32)
            result[to : to + d] = piece.astype(result.dtype)
        if at + 2 * d == EDGE:
            stores.append(
                pltpu.make_async_copy(
                    result.at[pl.ds(side * EDGE, EDGE)],
                    out_ref.at[pl.ds(side * (rows - EDGE), EDGE)],
                    sems.at[4 + side],
                )
            )
            stores[-1].start()
    for store in stores:
        store.wait()


def conv_ends(out, grid, sides, wide, neighbor, reversal, weights, bias, d, fields, own=None):
    _, cols, ch = grid.shape
    operands = [neighbor.T, reversal.T, far(grid) if fields is None else keep(grid)]
    operands += [keep(x) for x in (*sides, *wide, weights)] + [bias.reshape(1, ch)]
    smem = full_spec(pltpu.SMEM)
    in_specs = [smem, smem, full_spec(pl.ANY)] + [full_spec()] * 6
    scratch = [
        VMEM((2 * (EDGE + 2 * d), cols, 3 * ch), BF16),
        VMEM((2, d, cols + 2 * d, ch), BF16),
        VMEM((2 * EDGE, cols, ch), out.dtype),
        pltpu.SemaphoreType.DMA((6,)),
    ]
    if fields is not None:
        operands.append(far(fields))
        in_specs.append(full_spec(pl.ANY))
        scratch.append(VMEM((2 * EDGE, cols, ch), BF16))
        operands.append(keep(own))
        in_specs.append(full_spec())
    operands.append(far(out))
    in_specs.append(full_spec(pl.ANY))
    return pl.pallas_call(
        functools.partial(ends_kernel, d, fields is not None),
        out_shape=pltpu.HBM(out.shape, out.dtype),
        in_specs=in_specs,
        out_specs=full_spec(pl.ANY),
        scratch_shapes=scratch,
        input_output_aliases={len(operands) - 1: 0},
        cost_estimate=pl.CostEstimate(
            flops=4 * 12 * EDGE * cols * ch * ch, bytes_accessed=1_000_000, transcendentals=0
        ),
        compiler_params=room(16),
        name="conv_ends",
    )(*operands)


def scatter_kernel(
    d,
    recv,
    weight_ref,
    first_ref,
    mixed,
    a_ref,
    b_ref,
    ends_ref,
    first,
    even,
    extra,
    enc,
    cells_v,
    cells_s,
    sems,
):
    load = pltpu.make_async_copy(first_ref, first, sems.at[0])
    load.start()
    side, _, ch = mixed.shape
    sources = recv.shape[0]
    _, _, face_even, tile_even = parities()
    for g in range(sources // 8):
        meta = jnp.sum(recv[g * 8 : (g + 1) * 8, CAP:, :].astype(F32), axis=0)
        cells_v[g : g + 1, :] = (meta[0:1, :] * side + meta[1:2, :]).astype(I32)
    copy = pltpu.make_async_copy(cells_v, cells_s, sems.at[1])
    copy.start()
    for g in range(sources // 8):
        rows = recv[g * 8 : (g + 1) * 8, :CAP, :].reshape(8 * CAP, recv.shape[2])
        enc[g * 128 : (g + 1) * 128, :] = jnp.dot(
            rows, weight_ref[...], preferred_element_type=F32
        )

    def clear(r, carry):
        even[pl.ds(r * side, side), :] = jnp.zeros((side, ch), F32)
        extra[pl.ds(r * side, side), :] = jnp.zeros((side, ch), F32)
        return carry

    lax.fori_loop(0, side, clear, 0, unroll=4)
    copy.wait()

    for g in range(sources // 8):
        for j in range(0, 128, 2):
            for k, target in ((0, even), (1, extra)):
                c = cells_s[g, j + k]
                target[pl.ds(c, 1), :] += enc[pl.ds(g * 128 + j + k, 1), :]
    load.wait()

    per = side // d
    group = 8 // d

    def plane(p, carry):
        def rows_of(i, inner):
            west = []
            east = []
            for k in range(group):
                row = p * per + i * group + k
                at = pl.ds(pl.multiple_of(row * side, side), side)
                v = first[row] + even[at, :] + extra[at, :]
                mixed[row] = v.astype(BF16)
                west.append(v[:d])
                east.append(v[side - d :])
            west = jnp.concatenate(west, axis=0)
            east = jnp.concatenate(east, axis=0)
            at = pl.ds(pl.multiple_of(i * 8, 8), 8)
            a_ref[p, at, :] = jnp.where(face_even, east, west).astype(BF16)
            b_ref[p, at, :] = jnp.where(face_even, west, east).astype(BF16)
            return inner

        lax.fori_loop(0, per // group, rows_of, 0, unroll=2)
        return carry

    lax.fori_loop(0, d, plane, 0)
    start = jnp.where(tile_even, 0, side - d)
    for r in range(d):
        row = mixed[start + r]
        a_ref[d + r] = row
        b_ref[d + r] = row
        ends_ref[0, r] = mixed[r]
        ends_ref[1, r] = mixed[side - d + r]


def scatter(recv, weight, first, d):
    side, cols, ch = first.shape
    sources = recv.shape[0]
    out = VMEM((2 * d, cols, ch), BF16)
    return pl.pallas_call(
        functools.partial(scatter_kernel, d),
        out_shape=(VMEM((side, cols, ch), BF16), out, out, VMEM((2, d, cols, ch), BF16)),
        in_specs=[full_spec(), full_spec(), full_spec(pl.ANY)],
        out_specs=(full_spec(),) * 4,
        scratch_shapes=[
            VMEM(first.shape, F32),
            VMEM((side * cols, ch), F32),
            VMEM((side * cols, ch), F32),
            VMEM((sources * CAP, ch), F32),
            VMEM((sources // 8, 128), I32),
            pltpu.SMEM((sources // 8, 128), I32),
            pltpu.SemaphoreType.DMA((2,)),
        ],
        cost_estimate=pl.CostEstimate(
            flops=200_000_000, bytes_accessed=12_000_000, transcendentals=0
        ),
        compiler_params=room(28),
        name="scatter",
    )(keep(recv), weight, far(first))


def local(
    fields,
    first_kernel_taps,
    first_conv_bias,
    second_kernel_taps,
    second_conv_bias,
    obs_weight,
    obs_values,
    obs_owner,
    obs_cells,
    polar_neighbor_sector,
    polar_link_reversal,
):
    side = fields.shape[0]
    dests = lax.axis_size("face") * lax.axis_size("tile")
    d = FIRST_DILATION
    weights = pair_weights(first_kernel_taps)
    a, b, ends = edges(fields, d)
    sides = swap_faces((a, b))
    send = pack(obs_owner, obs_cells, obs_values, dests, side)
    recv = lax.all_to_all(send, ("face", "tile"), split_axis=0, concat_axis=0, tiled=True)
    wide = swap_tiles(widen(ends, sides, d))
    first = conv_rows(fields, sides, weights, first_conv_bias, d, None, F32)
    first = conv_ends(
        first, fields, sides, wide, polar_neighbor_sector, polar_link_reversal,
        weights, first_conv_bias, d, None,
    )
    d = SECOND_DILATION
    weights = pair_weights(second_kernel_taps)
    mixed, a, b, ends = scatter(recv, obs_weight, first, d)
    sides = swap_faces((a, b))
    out = conv_core(mixed, weights, second_conv_bias, d, fields)
    wide = swap_tiles(widen(ends, sides, d))
    out, own = conv_columns(out, mixed, sides, weights, second_conv_bias, d, fields)
    return conv_ends(
        out, mixed, sides, wide, polar_neighbor_sector, polar_link_reversal,
        weights, second_conv_bias, d, fields, own,
    )


def solution(mesh):
    in_specs = (
        P("tile", "face", None),
        P(),
        P(),
        P(),
        P(),
        P(),
        P(("face", "tile"), None),
        P(("face", "tile"), None),
        P(("face", "tile")),
        P(),
        P(),
    )
    out_specs = P("tile", "face", None)
    return jax.shard_map(local, mesh=mesh, in_specs=in_specs, out_specs=out_specs, check_vma=False)
```
